32 devices in a mesh: head: 4 (over x, core), blk: 8 (over z, y).
Axes of the slice: x: 2, y: 2, z: 4, core: 2. Of those that a mesh axis runs over, the one named last changes fastest.
Arguments:
- tokens: bfloat16 [4096, 2048], P(('blk', 'head')), may hold values from -6 to 6
- cotangent: bfloat16 [4096, 2048], P(('blk', 'head')), may hold values from -6 to 6
- segments: int32 [2, 2048], replicated, may hold values from 0 to 3, never falling along the last dimension, each value on 1 to 1024 neighbouring positions
- pair_order: int32 [8], replicated, may hold values from 0 to 7, each once
- norm_in: bfloat16 [2048], P(('head', 'blk')), may hold values from 0.25 to 1.75
- w_query: bfloat16 [2048, 2048], P(('head', 'blk')), may hold values from -0.1875 to 0.1875
- key_weight: bfloat16 [2048, 1024], P(('head', 'blk')), may hold values from -0.125 to 0.125
- value_weight: bfloat16 [2048, 1024], P(('head', 'blk')), may hold values from -0.125 to 0.125
- w_out: bfloat16 [2048, 2048], P(('head', 'blk')), may hold values from -0.75 to 0.75
- norm_mid: bfloat16 [2048], P(('head', 'blk')), may hold values from 0.25 to 1.75
- w_gate: bfloat16 [2048, 8192], P('blk', 'head'), may hold values from -0.125 to 0.125
- w_up: bfloat16 [2048, 8192], P('blk', 'head'), may hold values from -0.125 to 0.125
- w_down: bfloat16 [2048, 8192], P('blk', 'head'), may hold values from -0.125 to 0.125
Outputs:
- layer_out: bfloat16 [4096, 2048], P(('blk', 'head'))
- grad_tokens: float32 [4096, 2048], P(('blk', 'head'))
- grad_norm_in: float32 [2048], P(('head', 'blk'))
- grad_query: float32 [2048, 2048], P(('head', 'blk'))
- grad_key: float32 [2048, 1024], P(('head', 'blk'))
- grad_value: float32 [2048, 1024], P(('head', 'blk'))
- grad_out: float32 [2048, 2048], P(('head', 'blk'))
- grad_norm_mid: float32 [2048], P(('head', 'blk'))
- grad_gate: float32 [2048, 8192], P('blk', 'head')
- grad_up: float32 [2048, 8192], P('blk', 'head')
- grad_down: float32 [2048, 8192], P('blk', 'head')
The draws below stay inside these ranges and needn't reach their ends.
Inputs may be any that keep to these rules, and one draw needn't show every extreme that they name: `segments`: along each sequence the ids never fall; each id names one run of consecutive positions, and all four ids occur. `pair_order`: each pair number occurs once.
All inputs are finite; a program needn't handle non-finite values.
Results may differ from the reference program's by a relative error of at most 0.03.
Values may be sent and summed in bfloat16 or wider, within the bound.
No kernel may reach another device: no remote copies, remote signals or barrier semaphores. Data moves between devices by JAX's collectives and lax.ppermute only.
A program may use at most 448 MiB of HBM per device.

```python
import math
import jax
import jax.numpy as jnp
import numpy as np
from jax import lax

MODEL_WIDTH = 2048
QUERY_HEAD_COUNT = 8
KEY_VALUE_HEADS = 4
HEAD_WIDTH = 256
FF = 8192
TOK_DEV = 128
SEQS = 2
BLOCK = 256
TOKENS = 4096
SEQUENCE_LENGTH = 2048
N_HEAD = 4
N_BLK = 8


def strengthened(values, own_key, source, target, parts, factor):
    owner, partner = [(jnp.arange(values.shape[dim]) // (values.shape[dim] // parts)).reshape([-1 if axis == dim else 1 for axis in range(values.ndim)]) for dim in (source, target)]
    chosen = jax.random.permutation(own_key, parts)[partner]
    strong = (owner == chosen) | (owner == (partner + parts // 2) % parts)
    return jnp.where(strong, factor * values, values)


def block_levels(key, shape, split, smallest, high):
    loudness = 1.0
    for dim, shards_of in split:
        draws = jax.random.uniform(jax.random.fold_in(jax.random.fold_in(key, 6), dim), (shards_of,), jnp.float32, smallest / len(split), high / len(split))
        loudness = loudness * jnp.repeat(jnp.exp(draws), shape[dim] // shards_of).reshape((-1,) + (1,) * (len(shape) - 1 - dim))
    return loudness


def length_profile(count, total, reach, slope):
    portions = [(1 << 20) // math.isqrt(standing ** slope) + 1 for standing in range(2, count + 1)]
    rest, holding = total - reach - (count - 1), [1] * (count - 1)
    while rest > 0:
        movable = [i for i in range(count - 1) if holding[i] < reach]
        pool, left = sum([portions[i] for i in movable]), rest
        for i in movable:
            extra = min(reach - holding[i], max(1, left * portions[i] // pool), rest)
            holding[i] = holding[i] + extra
            rest = rest - extra
    return np.array([reach] + holding)


def uneven_parts(rng, count, total, limit, slope):
    if count == 2:
        one = jax.random.randint(rng, (), max(1, total - limit), min(limit, total - 1) + 1)
        return jnp.stack([one, total - one])
    lengths = jnp.asarray(length_profile(count, total, limit, slope), jnp.int32)
    twos = (count - 1) // 2
    giver, sink = lengths[1:1 + 2 * twos:2], lengths[2:2 + 2 * twos:2]
    margin = jnp.minimum(giver - 1, limit - sink)
    passed = jax.random.randint(jax.random.fold_in(rng, 1), (twos,), 0, 1 << 20) % (margin + 1)
    lengths = lengths.at[1:1 + 2 * twos:2].set(giver - passed).at[2:2 + 2 * twos:2].set(sink + passed)
    return lengths[jax.random.permutation(jax.random.fold_in(rng, 2), count)]


def normal_values(stream_key, extent, spread, reach, cuts=(), held_as=jnp.bfloat16):
    level = block_levels(stream_key, extent, cuts, -0.22, 0.18) if cuts else 1.0
    values = jax.random.normal(stream_key, extent, jnp.float32) * spread * level
    return jnp.minimum(jnp.maximum(values, -reach), reach).astype(held_as)


def heavy_noise(own_key, dims, deviation, bound, split, heavy, held_as=jnp.bfloat16):
    values = deviation * jax.random.normal(own_key, dims, jnp.float32)
    if split:
        values = values * block_levels(own_key, dims, split, -0.22, 0.18)
    return jnp.clip(strengthened(values, jax.random.fold_in(own_key, 3), *heavy), -bound, bound).astype(held_as)


def setup_inputs(seed: int = 0) -> dict:
    key_list = jax.random.split(jax.random.key(seed), 14)
    return {
        "tokens": normal_values(key_list[0], (TOKENS, MODEL_WIDTH), 1.0, 6.0, ((0, 32),)),
        "cotangent": heavy_noise(key_list[1], (TOKENS, MODEL_WIDTH), 1.0, 6.0, ((0, 32),), (0, 1, 32, 2.75)),
        "segments": jax.vmap(lambda own: jnp.searchsorted(jnp.cumsum(uneven_parts(own, 4, SEQUENCE_LENGTH, SEQUENCE_LENGTH // 2, 1)), jnp.arange(SEQUENCE_LENGTH), side="right"))(jax.random.split(key_list[2], SEQS)).reshape((SEQS, SEQUENCE_LENGTH)).astype(jnp.int32),
        "pair_order": jax.random.permutation(key_list[3], N_BLK).astype(jnp.int32),
        "norm_in": jnp.clip(1.0 + 0.15 * jax.random.normal(key_list[4], (MODEL_WIDTH,), jnp.float32), 0.25, 1.75).astype(jnp.bfloat16),
        "w_query": normal_values(key_list[5], (MODEL_WIDTH, QUERY_HEAD_COUNT * HEAD_WIDTH), (MODEL_WIDTH // 2) ** -0.5, 0.1875, ((0, 32),)),
        "key_weight": normal_values(key_list[6], (MODEL_WIDTH, KEY_VALUE_HEADS * HEAD_WIDTH), MODEL_WIDTH ** -0.5, 0.125, ((0, 32),)),
        "value_weight": normal_values(key_list[7], (MODEL_WIDTH, KEY_VALUE_HEADS * HEAD_WIDTH), MODEL_WIDTH ** -0.5, 0.125, ((0, 32),)),
        "w_out": normal_values(key_list[8], (MODEL_WIDTH, QUERY_HEAD_COUNT * HEAD_WIDTH), (max(1, QUERY_HEAD_COUNT * HEAD_WIDTH * 64 // SEQUENCE_LENGTH)) ** -0.5, 0.75, ((0, 32),)),
        "norm_mid": jnp.clip(1.0 + 0.15 * jax.random.normal(key_list[9], (MODEL_WIDTH,), jnp.float32), 0.25, 1.75).astype(jnp.bfloat16),
        "w_gate": normal_values(key_list[10], (MODEL_WIDTH, FF), MODEL_WIDTH ** -0.5, 0.125, ((0, 8), (1, 4))),
        "w_up": normal_values(key_list[11], (MODEL_WIDTH, FF), MODEL_WIDTH ** -0.5, 0.125, ((0, 8), (1, 4))),
        "w_down": normal_values(key_list[12], (MODEL_WIDTH, FF), (FF // 4) ** -0.5, 0.125, ((0, 8), (1, 4))),
    }


EPS = 1e-06
THETA = 1000042.0
NEGATIVE = -1e+30

@jax.custom_vjp
def reduced_precision(v):
    return lax.optimization_barrier(v.astype(jnp.bfloat16)).astype(jnp.float32)

@jax.custom_vjp
def reduced_backward(v):
    return v

def low_keep(v):
    return (reduced_precision(v), None)

def low_pass(kept, grad):
    return (grad,)

def back_keep(v):
    return (v, None)

def back_low(kept, grad):
    return (reduced_precision(grad),)
reduced_precision.defvjp(low_keep, low_pass)
reduced_backward.defvjp(back_keep, back_low)

def frequencies(head_size):
    return 1.0 / THETA ** (jnp.arange(0, head_size, 2, dtype=jnp.float32) / head_size)

def apply_rotary(values_in, cosine_table, sine_lookup):
    half_size = values_in.shape[-1] // 2
    first_half = values_in[..., :half_size]
    second_half = values_in[..., half_size:]
    return jnp.concatenate([first_half * cosine_table - second_half * sine_lookup, second_half * cosine_table + first_half * sine_lookup], axis=-1)

def key_layout(row_ids, pair_order, groups, group_rows):
    group_id = row_ids // group_rows
    chosen = group_id[:, None] == jnp.arange(groups, dtype=jnp.int32)[None, :]
    pair_id = lax.optimization_barrier(jnp.sum(jnp.where(chosen, pair_order[None, :], 0), axis=1)).astype(jnp.int32)
    per_seq = groups // SEQS
    seq_id = pair_id // per_seq
    first_span = pair_id % per_seq
    span_rows = group_rows // 2
    local_row = row_ids % group_rows
    span_id = jnp.where(local_row < span_rows, first_span, 2 * per_seq - 1 - first_span)
    return (seq_id, span_id * span_rows + local_row % span_rows)

def reference(tokens, cotangent, segments, pair_order, norm_in, w_query, key_weight, value_weight, w_out, norm_mid, w_gate, w_up, w_down):
    group_rows = TOK_DEV * N_HEAD
    row_ids = jnp.arange(TOKENS, dtype=jnp.int32)
    seq_id, position = key_layout(row_ids, pair_order, N_BLK, group_rows)
    seq_order = jnp.zeros((SEQS, SEQUENCE_LENGTH), jnp.int32).at[seq_id, position].set(row_ids)
    angles = jnp.arange(SEQUENCE_LENGTH, dtype=jnp.float32)[:, None] * frequencies(HEAD_WIDTH)[None, :]
    cosine_table = jnp.cos(angles)[:, None, :]
    sine_lookup = jnp.sin(angles)[:, None, :]
    blocks = jnp.arange(SEQUENCE_LENGTH, dtype=jnp.int32) // BLOCK
    query_row_values = min(512, SEQUENCE_LENGTH)
    score_scale = HEAD_WIDTH ** (-0.5)
    highest = lax.Precision.HIGHEST
    queries_per_key_value = QUERY_HEAD_COUNT // KEY_VALUE_HEADS

    def attend_block(block_index, query_matrix, keys_all, values_all, seg_ids):
        first_row_index = block_index * query_row_values
        query_block_slice = lax.dynamic_slice_in_dim(query_matrix, first_row_index, query_row_values, 0).reshape(query_row_values, KEY_VALUE_HEADS, queries_per_key_value, HEAD_WIDTH)
        scores = reduced_backward(jnp.einsum('qkgd,skd->kgqs', query_block_slice, keys_all, precision=highest) * score_scale)
        seg_query = lax.dynamic_slice_in_dim(seg_ids, first_row_index, query_row_values, 0)
        block_query = lax.dynamic_slice_in_dim(blocks, first_row_index, query_row_values, 0)
        visible = (seg_query[:, None] == seg_ids[None, :]) & (blocks[None, :] <= block_query[:, None])
        scores = jnp.where(visible, scores, NEGATIVE)
        row_max = lax.optimization_barrier(jnp.max(scores, axis=-1, keepdims=True))
        weights = jnp.exp(scores - row_max)
        probabilities = weights / lax.optimization_barrier(jnp.sum(weights, axis=-1, keepdims=True))
        output = jnp.einsum('kgqs,skd->qkgd', reduced_precision(probabilities), values_all, precision=highest)
        return output.reshape(query_row_values, QUERY_HEAD_COUNT * HEAD_WIDTH)
    checked_block = jax.checkpoint(attend_block)

    def sequence_layer(seq_rows, seg_ids, tokens_f, norm_a, query_w, key_w, value_w, out_w, norm_b, gate_w, up_w, down_w):
        rows_in = tokens_f[seq_rows]
        inv_in = lax.rsqrt(lax.optimization_barrier(jnp.mean(rows_in * rows_in, axis=-1, keepdims=True)) + EPS)
        input_low = reduced_precision(rows_in * inv_in * norm_a)
        query_lin = reduced_backward(jnp.dot(input_low, query_w, precision=highest))
        key_linear = reduced_backward(jnp.dot(input_low, key_w, precision=highest))
        value_linear = jnp.dot(input_low, value_w, precision=highest)
        query_matrix = reduced_precision(reduced_backward(apply_rotary(query_lin.reshape(SEQUENCE_LENGTH, QUERY_HEAD_COUNT, HEAD_WIDTH), cosine_table, sine_lookup)))
        rotated_keys = reduced_precision(reduced_backward(apply_rotary(key_linear.reshape(SEQUENCE_LENGTH, KEY_VALUE_HEADS, HEAD_WIDTH), cosine_table, sine_lookup)))
        reduced_values = reduced_precision(reduced_backward(value_linear)).reshape(SEQUENCE_LENGTH, KEY_VALUE_HEADS, HEAD_WIDTH)
        attention = lax.map(lambda block_index: checked_block(block_index, query_matrix, rotated_keys, reduced_values, seg_ids), jnp.arange(SEQUENCE_LENGTH // query_row_values, dtype=jnp.int32))
        attention = reduced_precision(reduced_backward(attention.reshape(SEQUENCE_LENGTH, QUERY_HEAD_COUNT * HEAD_WIDTH)))
        middle = rows_in + reduced_backward(jnp.dot(attention, out_w.T, precision=highest))
        inv_mid = lax.rsqrt(lax.optimization_barrier(jnp.mean(middle * middle, axis=-1, keepdims=True)) + EPS)
        mid_low = reduced_precision(middle * inv_mid * norm_b)
        gate_lin = reduced_backward(jnp.dot(mid_low, gate_w, precision=highest))
        up_proj = reduced_backward(jnp.dot(mid_low, up_w, precision=highest))
        hidden_act = reduced_precision(jax.nn.silu(gate_lin) * up_proj)
        return middle + reduced_backward(jnp.dot(hidden_act, down_w.T, precision=highest))
    checked_layer = jax.checkpoint(sequence_layer)

    def layer_fn(tokens_f, norm_a, query_w, key_w, value_w, out_w, norm_b, gate_w, up_w, down_w):

        def scan_step(unused, inputs_pair):
            return (unused, checked_layer(inputs_pair[0], inputs_pair[1], tokens_f, norm_a, query_w, key_w, value_w, out_w, norm_b, gate_w, up_w, down_w))
        ignored, outputs = lax.scan(scan_step, jnp.zeros((), jnp.float32), (seq_order, segments))
        return jnp.zeros((TOKENS, MODEL_WIDTH), jnp.float32).at[seq_order.reshape(-1)].set(outputs.reshape(-1, MODEL_WIDTH))
    primals = tuple((array_in.astype(jnp.float32) for array_in in (tokens, norm_in, w_query, key_weight, value_weight, w_out, norm_mid, w_gate, w_up, w_down)))
    result, pull_back = jax.vjp(layer_fn, *primals)
    gradients = pull_back(cotangent.astype(jnp.float32))
    return (result.astype(jnp.bfloat16), gradients[0], gradients[1], gradients[2], gradients[3], gradients[4], gradients[5], gradients[6], gradients[7], gradients[8], gradients[9])
```

```python
import functools

import jax
import jax.numpy as jnp
from jax import lax
from jax.experimental import pallas as pl
from jax.experimental.pallas import tpu as pltpu
from jax.sharding import PartitionSpec as P

QUERY_HEAD_COUNT = 8
KEY_VALUE_HEADS = 4
HEAD_WIDTH = 256
SEQS = 2
BLOCK = 256

EPS = 1e-06
THETA = 1000042.0
NEGATIVE = -1e30
ROWS = (((0,), (0,)), ((), ()))
COLS = (((1,), (1,)), ((), ()))
BF16 = jnp.bfloat16
F32 = jnp.float32

CORE, CROSS, TURN = 1, 2, 2


def frequencies(head_size):
    return 1.0 / THETA ** (jnp.arange(0, head_size, 2, dtype=F32) / head_size)


def rotate(values, cosine, sine):
    half = HEAD_WIDTH // 2
    parts = []
    for first in range(0, values.shape[-1], HEAD_WIDTH):
        a = values[:, first : first + half]
        b = values[:, first + half : first + HEAD_WIDTH]
        parts += [a * cosine - b * sine, b * cosine + a * sine]
    return jnp.concatenate(parts, axis=-1)


def swap(value, head_mask, blk_mask):
    groups = lax.axis_size("blk")
    count = lax.axis_size("head") * groups
    mask = head_mask * groups + blk_mask
    return lax.ppermute(value, ("head", "blk"), [(i, i ^ mask) for i in range(count)])


def masks_of(size):
    out, bit = [], size >> 1
    while bit:
        out.append(bit)
        bit >>= 1
    return out


def add(a, b, dtype):
    return (a.astype(F32) + b.astype(F32)).astype(dtype)


def spread(piece, masks):
    have = {0: piece}
    for mask in masks:
        for key, value in list(have.items()):
            have[key ^ mask] = swap(value, 0, mask)
    return have


def fold(pieces, masks):
    have = dict(pieces)
    for mask in masks:
        for key in sorted(k for k in have if k & mask):
            received = swap(have.pop(key), 0, mask)
            left = key ^ mask
            have[left] = add(have[left], received, F32 if mask == masks[-1] else BF16)
    return have[0]


def span_of(pair_ref, group, late, per_seq):
    pair = pair_ref[group]
    seq = pair // per_seq
    first = pair - seq * per_seq
    return seq, jnp.where(late == 0, first, 2 * per_seq - 1 - first)


def tile_visible(place_ref, pair_ref, seg_ref, step, part, per_seq, seq_len):
    group, cross = place_ref[0], place_ref[1]
    seq_k, span_k = span_of(pair_ref, group ^ (step // 2), cross ^ (step % 2), per_seq)
    seq_q, span_q = span_of(pair_ref, group, cross ^ part, per_seq)
    last_k = seg_ref[seq_k * seq_len + span_k * BLOCK + BLOCK - 1]
    first_q = seg_ref[seq_q * seq_len + span_q * BLOCK]
    visible = (seq_k == seq_q) & (span_k <= span_q) & (last_k >= first_q)
    spans = 2 * per_seq
    return visible, seq_k * spans + span_k, seq_q * spans + span_q


def tile_mask(seg_row_ref, seg_col_ref, place_k, place_q):
    lanes = lax.broadcasted_iota(jnp.int32, seg_col_ref.shape, 1)
    column = jnp.sum(jnp.where(lanes == place_k, seg_col_ref[...], 0), axis=1, keepdims=True)
    row = seg_row_ref[pl.ds(place_q, 1), :]
    row = jnp.concatenate([row, row], axis=1)
    return column == row


def stack_heads(ref, part):
    rows = pl.ds(part * BLOCK, BLOCK)
    return jnp.concatenate([ref[rows, :HEAD_WIDTH], ref[rows, HEAD_WIDTH:]], axis=0)


def forward_kernel(
    per_seq, place_ref, pair_ref, seg_ref, q_ref, kv_ref, row_ref, col_ref,
    low_ref, out_ref, lse_ref, max_ref, sum_ref, acc_ref,
):
    step = pl.program_id(0)
    seq_len = 2 * per_seq * BLOCK

    @pl.when(step == 0)
    def _():
        max_ref[...] = jnp.full(max_ref.shape, NEGATIVE, F32)
        sum_ref[...] = jnp.zeros(sum_ref.shape, F32)
        acc_ref[...] = jnp.zeros(acc_ref.shape, F32)

    for part in range(2):
        visible, place_k, place_q = tile_visible(
            place_ref, pair_ref, seg_ref, step, part, per_seq, seq_len
        )

        @pl.when(visible)
        def _():
            keys = kv_ref[:, :HEAD_WIDTH]
            values = kv_ref[:, HEAD_WIDTH:]
            queries = stack_heads(q_ref, part)
            scores = lax.dot_general(keys, queries, COLS, preferred_element_type=F32)
            mask = tile_mask(row_ref, col_ref, place_k, place_q)
            scores = jnp.where(mask, scores, NEGATIVE)
            old_max = max_ref[part]
            new_max = jnp.maximum(old_max, jnp.max(scores, axis=0, keepdims=True))
            weights = jnp.where(mask, jnp.exp(scores - new_max), 0.0)
            factor = jnp.exp(old_max - new_max)
            max_ref[part] = new_max
            sum_ref[part] = sum_ref[part] * factor + jnp.sum(weights, axis=0, keepdims=True)
            acc_ref[part] = acc_ref[part] * factor + lax.dot_general(
                values, weights.astype(BF16), ROWS, preferred_element_type=F32
            )

    @pl.when(step == pl.num_programs(0) - 1)
    def _():
        for part in range(2):
            total = sum_ref[part]
            attended = (acc_ref[part] / total).T
            rows = pl.ds(part * BLOCK, BLOCK)
            for head in range(2):
                one = attended[head * BLOCK : (head + 1) * BLOCK]
                cols = pl.ds(head * HEAD_WIDTH, HEAD_WIDTH)
                out_ref[rows, cols] = one
                low_ref[rows, cols] = one.astype(BF16)
            lse_ref[part] = max_ref[part] + jnp.log(total)


def backward_kernel(
    per_seq, place_ref, pair_ref, seg_ref, q_ref, kv_ref, row_ref, col_ref, lse_ref, out_ref, do_ref,
    dq_ref, dkv_ref, delta_ref, dq_acc, dk_acc, dv_acc,
):
    step = pl.program_id(0)
    seq_len = 2 * per_seq * BLOCK

    @pl.when(step == 0)
    def _():
        dq_acc[...] = jnp.zeros(dq_acc.shape, F32)
        for part in range(2):
            product = stack_heads(out_ref, part) * stack_heads(do_ref, part).astype(F32)
            delta_ref[part] = jnp.sum(product.T, axis=0, keepdims=True)

    dk_acc[...] = jnp.zeros(dk_acc.shape, F32)
    dv_acc[...] = jnp.zeros(dv_acc.shape, F32)
    for part in range(2):
        visible, place_k, place_q = tile_visible(
            place_ref, pair_ref, seg_ref, step, part, per_seq, seq_len
        )

        @pl.when(visible)
        def _():
            keys = kv_ref[:, :HEAD_WIDTH]
            values = kv_ref[:, HEAD_WIDTH:]
            queries = stack_heads(q_ref, part)
            grads = stack_heads(do_ref, part)
            scores = lax.dot_general(keys, queries, COLS, preferred_element_type=F32)
            mask = tile_mask(row_ref, col_ref, place_k, place_q)
            probs = jnp.where(mask, jnp.exp(scores - lse_ref[part]), 0.0)
            grad_probs = lax.dot_general(values, grads, COLS, preferred_element_type=F32)
            grad_scores = (probs * (grad_probs - delta_ref[part])).astype(BF16)
            dv_acc[...] += jnp.dot(probs.astype(BF16), grads, preferred_element_type=F32)
            dk_acc[...] += jnp.dot(grad_scores, queries, preferred_element_type=F32)
            dq_acc[part] += lax.dot_general(
                grad_scores, keys, ROWS, preferred_element_type=F32
            )

    dkv_ref[:, :HEAD_WIDTH] = dk_acc[...].astype(BF16)
    dkv_ref[:, HEAD_WIDTH:] = dv_acc[...].astype(BF16)

    @pl.when(step == pl.num_programs(0) - 1)
    def _():
        for part in range(2):
            rows = pl.ds(part * BLOCK, BLOCK)
            for head in range(2):
                one = dq_acc[part, head * BLOCK : (head + 1) * BLOCK]
                dq_ref[rows, pl.ds(head * HEAD_WIDTH, HEAD_WIDTH)] = (
                    one * HEAD_WIDTH ** (-0.5)
                ).astype(BF16)


def whole(shape):
    return pl.BlockSpec(shape, lambda step, *refs: (0,) * len(shape))


def attend(place, pair_order, seg_flat, queries, keys_values, seg_row, seg_col, per_seq):
    steps = keys_values.shape[0] // BLOCK
    rows, width = queries.shape
    return pl.pallas_call(
        functools.partial(forward_kernel, per_seq),
        grid_spec=pltpu.PrefetchScalarGridSpec(
            num_scalar_prefetch=3,
            grid=(steps,),
            in_specs=[
                whole(queries.shape),
                pl.BlockSpec((BLOCK, 2 * HEAD_WIDTH), lambda step, *refs: (step, 0)),
                whole(seg_row.shape),
                whole(seg_col.shape),
            ],
            out_specs=[whole((rows, width)), whole((rows, width)), whole((2, 1, rows))],
            scratch_shapes=[
                pltpu.VMEM((2, 1, rows), F32),
                pltpu.VMEM((2, 1, rows), F32),
                pltpu.VMEM((2, HEAD_WIDTH, rows), F32),
            ],
        ),
        out_shape=[
            jax.ShapeDtypeStruct((rows, width), BF16),
            jax.ShapeDtypeStruct((rows, width), F32),
            jax.ShapeDtypeStruct((2, 1, rows), F32),
        ],
        compiler_params=pltpu.CompilerParams(dimension_semantics=("arbitrary",)),
        cost_estimate=pl.CostEstimate(
            flops=6_000_000_000, bytes_accessed=6_000_000, transcendentals=2_000_000
        ),
        name="attend",
    )(place, pair_order, seg_flat, queries, keys_values, seg_row, seg_col)


def attend_back(
    place, pair_order, seg_flat, queries, keys_values, seg_row, seg_col, lse, out, grads, per_seq
):
    steps = keys_values.shape[0] // BLOCK
    rows, width = queries.shape
    return pl.pallas_call(
        functools.partial(backward_kernel, per_seq),
        grid_spec=pltpu.PrefetchScalarGridSpec(
            num_scalar_prefetch=3,
            grid=(steps,),
            in_specs=[
                whole(queries.shape),
                pl.BlockSpec((BLOCK, 2 * HEAD_WIDTH), lambda step, *refs: (step, 0)),
                whole(seg_row.shape),
                whole(seg_col.shape),
                whole(lse.shape),
                whole(out.shape),
                whole(grads.shape),
            ],
            out_specs=[
                whole((rows, width)),
                pl.BlockSpec((BLOCK, 2 * HEAD_WIDTH), lambda step, *refs: (step, 0)),
            ],
            scratch_shapes=[
                pltpu.VMEM((2, 1, rows), F32),
                pltpu.VMEM((2, rows, HEAD_WIDTH), F32),
                pltpu.VMEM((BLOCK, HEAD_WIDTH), F32),
                pltpu.VMEM((BLOCK, HEAD_WIDTH), F32),
            ],
        ),
        out_shape=[
            jax.ShapeDtypeStruct((rows, width), BF16),
            jax.ShapeDtypeStruct(keys_values.shape, BF16),
        ],
        compiler_params=pltpu.CompilerParams(dimension_semantics=("arbitrary",)),
        cost_estimate=pl.CostEstimate(
            flops=16_000_000_000, bytes_accessed=12_000_000, transcendentals=2_000_000
        ),
        name="attend_back",
    )(place, pair_order, seg_flat, queries, keys_values, seg_row, seg_col, lse, out, grads)


def gather_four(own):
    beside = swap(own, CORE, 0)
    across = swap(own, CROSS, 0)
    both = swap(across, CORE, 0)
    return jnp.concatenate([own, beside, across, both], axis=0)


def fold_four(partial_sum):
    rows = partial_sum.shape[0] // 4
    four = partial_sum.reshape(2, 2, rows, -1)
    across = add(four[1, 0], swap(four[1, 1], CORE, 0), BF16)
    own = add(four[0, 0], swap(four[0, 1], CORE, 0), F32)
    return own + swap(across, CROSS, 0).astype(F32)


def gather_eight(own):
    half = own.shape[1] // 2
    left, right = own[:, :half], own[:, half:]
    left_x = swap(left, CROSS, 0)
    right_t = swap(right, 0, TURN)
    left_t = swap(left, 0, TURN)
    right_x = swap(right, CROSS, 0)
    left_xt = swap(left_x, 0, TURN)
    right_xt = swap(right_t, CROSS, 0)
    four = jnp.concatenate(
        [
            jnp.concatenate([left, left_t, left_x, left_xt], axis=0),
            jnp.concatenate([right, right_t, right_x, right_xt], axis=0),
        ],
        axis=1,
    )
    return jnp.concatenate([four, swap(four, CORE, 0)], axis=0)


def fold_eight(partial_sum):
    rows, width = partial_sum.shape[0] // 8, partial_sum.shape[1]
    eight = partial_sum.reshape(2, 2, 2, rows, width)
    four = add(eight[0], swap(eight[1], CORE, 0), BF16)
    left, right = four[..., : width // 2], four[..., width // 2 :]
    left = add(left[:, 0], swap(left[:, 1], 0, TURN), BF16)
    right = add(right[0], swap(right[1], CROSS, 0), BF16)
    left = add(left[0], swap(left[1], CROSS, 0), F32)
    right = add(right[0], swap(right[1], 0, TURN), F32)
    return jnp.concatenate([left, right], axis=-1)


def rms_back(grad_norm, normed, inv_rms, gain):
    scaled = grad_norm * gain
    return inv_rms * (scaled - normed * jnp.mean(scaled * normed, axis=-1, keepdims=True))


def local(
    tokens,
    cotangent,
    segments,
    pair_order,
    norm_in,
    w_query,
    key_weight,
    value_weight,
    w_out,
    norm_mid,
    w_gate,
    w_up,
    w_down,
):
    heads = lax.axis_size("head")
    groups = lax.axis_size("blk")
    group = lax.axis_index("blk")
    head = lax.axis_index("head")
    cross, core = head // 2, head % 2
    turn = (group // TURN) % 2
    high, low = group // 4, group % 2
    token_rows, width = tokens.shape
    group_rows = token_rows * heads
    per_seq = groups // SEQS
    seq_len = segments.shape[1]
    shard = norm_in.shape[0]
    blk_masks = masks_of(groups)
    far_masks = [mask for mask in blk_masks if mask != TURN]
    key_local = HEAD_WIDTH
    query_local = w_query.shape[1] // heads

    rows = jnp.arange(group_rows, dtype=jnp.int32)
    local_row = (head ^ (rows // token_rows)) * token_rows + rows % token_rows
    pair = lax.dynamic_index_in_dim(pair_order, group, keepdims=False)
    first_span = pair % per_seq
    span = jnp.where(local_row < BLOCK, first_span, 2 * per_seq - 1 - first_span)
    positions = span * BLOCK + local_row % BLOCK
    angles = positions.astype(F32)[:, None] * frequencies(HEAD_WIDTH)[None, :]
    cosine, sine = jnp.cos(angles), jnp.sin(angles)
    seg_halves = segments.reshape(-1, 2, BLOCK // 2)
    seg_row = jnp.where(core == 0, seg_halves, seg_halves[:, ::-1]).reshape(-1, BLOCK)
    seg_col = seg_row.T
    seg_flat = segments.reshape(-1)
    place = jnp.stack([group, cross]).astype(jnp.int32)

    gains = jnp.zeros((2, heads * groups, shard), BF16)
    gains = lax.dynamic_update_slice(
        gains, jnp.stack([norm_in, norm_mid])[:, None], (0, head * groups + group, 0)
    )
    for mask in (CROSS, CORE):
        gains = gains + swap(gains, mask, 0)
    for mask in blk_masks:
        gains = gains + swap(gains, 0, mask)
    gains = gains.reshape(2, width).astype(F32)
    gain_in, gain_mid = gains[0], gains[1]

    def by_head(weight):
        return weight.reshape(shard, heads, -1).transpose(1, 0, 2)

    def gather_rows(local_cols):
        cols = local_cols.shape[-1]
        mine = lax.all_to_all(local_cols, "head", split_axis=0, concat_axis=0, tiled=True)
        full = jnp.zeros((heads, groups, shard, cols), BF16)
        for mask, piece in spread(mine, blk_masks).items():
            full = lax.dynamic_update_slice(full, piece[:, None], (0, group ^ mask, 0, 0))
        return full.reshape(width, cols)

    weight_in = gather_rows(
        jnp.concatenate([by_head(w_query), by_head(key_weight), by_head(value_weight)], axis=-1)
    )
    weight_out = gather_rows(by_head(w_out))

    token_group = gather_four(tokens).astype(F32)
    inv_group = lax.rsqrt(jnp.mean(token_group * token_group, axis=-1, keepdims=True) + EPS)
    input_low = (token_group * inv_group * gain_in).astype(BF16)
    lin = jnp.dot(input_low, weight_in, preferred_element_type=F32)
    keys_values = jnp.concatenate(
        [
            rotate(lin[:, query_local : query_local + key_local], cosine, sine).astype(BF16),
            lin[:, query_local + key_local :].astype(BF16),
        ],
        axis=-1,
    )
    queries = rotate(lin[:, :query_local], cosine, sine).astype(BF16)
    queries = queries * jnp.asarray(HEAD_WIDTH ** (-0.5), BF16)
    kv_pieces = spread(keys_values, blk_masks)
    kv_all = jnp.concatenate([kv_pieces[mask] for mask in range(groups)], axis=0)
    attention_low, attention_f, lse = attend(
        place, pair_order, seg_flat, queries, kv_all, seg_row, seg_col, per_seq
    )
    branch = fold_four(
        lax.dot_general(attention_low, weight_out, COLS, preferred_element_type=F32).astype(BF16)
    )
    tokens_f = tokens.astype(F32)
    middle = tokens_f + branch
    inv_mid = lax.rsqrt(jnp.mean(middle * middle, axis=-1, keepdims=True) + EPS)
    normed_mid = middle * inv_mid
    mid_low = (normed_mid * gain_mid).astype(BF16)

    ff_rows, ff_cols = w_gate.shape
    ff_own = ff_cols // 2

    def gather_ffn(weight):
        mine = lax.dynamic_slice_in_dim(weight, turn * ff_own, ff_own, 1)
        other = lax.dynamic_slice_in_dim(weight, (1 - turn) * ff_own, ff_own, 1)
        received = swap(other, 0, TURN)
        both = jnp.stack(
            [jnp.where(turn == 0, mine, received), jnp.where(turn == 0, received, mine)]
        )
        full = jnp.zeros((groups // 4, 2, 2, ff_rows, ff_own), BF16)
        for mask, piece in spread(both, far_masks).items():
            full = lax.dynamic_update_slice(
                full, piece[None, :, None], (high ^ (mask // 4), 0, low ^ (mask % 2), 0, 0)
            )
        return full.reshape(width, ff_own)

    down = gather_ffn(w_down)
    gate = gather_ffn(w_gate)
    up = gather_ffn(w_up)
    grad_group = gather_eight(cotangent)
    grad_hidden = jnp.dot(grad_group, down, preferred_element_type=F32)
    mid_group = gather_eight(mid_low)
    gate_lin = jnp.dot(mid_group, gate, preferred_element_type=F32)
    up_proj = jnp.dot(mid_group, up, preferred_element_type=F32)
    gate_sig = jax.nn.sigmoid(gate_lin)
    gate_silu = gate_lin * gate_sig
    hidden_act = (gate_silu * up_proj).astype(BF16)
    grad_gate_lin = (
        grad_hidden * up_proj * gate_sig * (1.0 + gate_lin * (1.0 - gate_sig))
    ).astype(BF16)
    grad_up_proj = (grad_hidden * gate_silu).astype(BF16)
    mid_partial = lax.dot_general(
        grad_gate_lin, gate, COLS, preferred_element_type=F32
    ) + lax.dot_general(grad_up_proj, up, COLS, preferred_element_type=F32)
    grad_mid = fold_eight(mid_partial.astype(BF16))
    ffn_partial = lax.dot_general(hidden_act, down, COLS, preferred_element_type=F32)
    ffn_out = fold_eight(ffn_partial.astype(BF16))
    layer_out = (middle + ffn_out).astype(BF16)

    def fold_ffn(lhs, rhs):
        partial_sum = lax.dot_general(lhs, rhs, ROWS, preferred_element_type=F32).astype(BF16)
        partial_sum = partial_sum.reshape(groups // 4, 2, 2, ff_rows, ff_own)
        pieces = {}
        for mask in range(groups):
            if mask & TURN:
                continue
            piece = lax.dynamic_slice(
                partial_sum,
                (high ^ (mask // 4), 0, low ^ (mask % 2), 0, 0),
                (1, 2, 1, ff_rows, ff_own),
            )
            pieces[mask] = piece.reshape(2, ff_rows, ff_own)
        total = fold(pieces, far_masks[::-1])
        mine = lax.dynamic_index_in_dim(total, turn, 0, keepdims=False)
        other = lax.dynamic_index_in_dim(total, 1 - turn, 0, keepdims=False).astype(BF16)
        received = swap(other, 0, TURN).astype(F32)
        return jnp.concatenate(
            [jnp.where(turn == 0, mine, received), jnp.where(turn == 0, received, mine)], axis=1
        )

    grad_down_w = fold_ffn(grad_group, hidden_act)
    grad_gate_w = fold_ffn(mid_group, grad_gate_lin)
    grad_up_w = fold_ffn(mid_group, grad_up_proj)

    def everywhere(vector):
        for mask in (CORE, CROSS):
            vector = vector + swap(vector, mask, 0)
        for mask in blk_masks:
            vector = vector + swap(vector, 0, mask)
        return lax.dynamic_slice_in_dim(vector, (head * groups + group) * shard, shard, 0)

    grad_norm_mid = everywhere(jnp.sum(grad_mid * normed_mid, axis=0))
    grad_y = cotangent.astype(F32)
    grad_middle = grad_y + rms_back(grad_mid, normed_mid, inv_mid, gain_mid)
    branch_group = gather_four(grad_middle.astype(BF16))

    def fold_rows(lhs, rhs):
        partial_sum = lax.dot_general(lhs, rhs, ROWS, preferred_element_type=F32).astype(BF16)
        cols = partial_sum.shape[1]
        partial_sum = partial_sum.reshape(heads, groups, shard, cols)
        pieces = {
            mask: lax.dynamic_index_in_dim(partial_sum, group ^ mask, 1, keepdims=False)
            for mask in range(groups)
        }
        total = fold(pieces, blk_masks[::-1]).astype(BF16)
        total = lax.all_to_all(total, "head", split_axis=0, concat_axis=0, tiled=True)
        return total.astype(F32)

    def full_cols(by_heads):
        return by_heads.transpose(1, 0, 2).reshape(shard, -1)

    grad_attention = jnp.dot(branch_group, weight_out, preferred_element_type=F32).astype(BF16)
    grad_out_w = full_cols(fold_rows(branch_group, attention_low))
    grad_queries, grad_kv = attend_back(
        place, pair_order, seg_flat, queries, kv_all, seg_row, seg_col,
        lse, attention_f, grad_attention, per_seq,
    )
    grad_kv = grad_kv.reshape(groups, group_rows, 2 * HEAD_WIDTH)
    kv_total = fold({mask: grad_kv[mask] for mask in range(groups)}, blk_masks[::-1])
    kv_low = kv_total.astype(BF16)
    grad_lin = jnp.concatenate(
        [
            rotate(grad_queries.astype(F32), cosine, -sine).astype(BF16),
            rotate(kv_low[:, :HEAD_WIDTH].astype(F32), cosine, -sine).astype(BF16),
            kv_low[:, HEAD_WIDTH:],
        ],
        axis=-1,
    )
    grad_in = fold_four(
        lax.dot_general(grad_lin, weight_in, COLS, preferred_element_type=F32).astype(BF16)
    )
    in_grads = fold_rows(input_low, grad_lin)
    inv_in = inv_group[:token_rows]
    normed_in = tokens_f * inv_in
    grad_norm_in = everywhere(jnp.sum(grad_in * normed_in, axis=0))
    grad_tokens = grad_middle + rms_back(grad_in, normed_in, inv_in, gain_in)
    first_value = query_local + key_local
    return (
        layer_out,
        grad_tokens,
        grad_norm_in,
        full_cols(in_grads[..., :query_local]),
        full_cols(in_grads[..., query_local:first_value]),
        full_cols(in_grads[..., first_value:]),
        grad_out_w,
        grad_norm_mid,
        grad_gate_w,
        grad_up_w,
        grad_down_w,
    )


def solution(mesh):
    rows = P(("blk", "head"), None)
    shards = P(("head", "blk"), None)
    vector = P(("head", "blk"))
    hidden = P("blk", "head")
    return jax.shard_map(
        local,
        mesh=mesh,
        in_specs=(
            rows, rows, P(), P(), vector, shards, shards, shards, shards, vector, hidden, hidden, hidden,
        ),
        out_specs=(
            rows, rows, vector, shards, shards, shards, shards, vector, hidden, hidden, hidden,
        ),
        check_vma=False,
    )
```

```python
import functools

import jax
import jax.numpy as jnp
from jax import lax
from jax.experimental import pallas as pl
from jax.experimental.layout import Layout, with_layout_constraint
from jax.experimental.pallas import tpu as pltpu
from jax.sharding import PartitionSpec as P

QUERY_HEAD_COUNT = 8
KEY_VALUE_HEADS = 4
HEAD_WIDTH = 256
SEQS = 2
BLOCK = 256

EPS = 1e-06
THETA = 1000042.0
NEGATIVE = -1e30
ROWS = (((0,), (0,)), ((), ()))
COLS = (((1,), (1,)), ((), ()))
BF16 = jnp.bfloat16
F32 = jnp.float32

CORE, CROSS, TURN = 1, 2, 2


def frequencies(head_size):
    return 1.0 / THETA ** (jnp.arange(0, head_size, 2, dtype=F32) / head_size)


def rotate(values, cosine, sine):
    half = HEAD_WIDTH // 2
    parts = []
    for first in range(0, values.shape[-1], HEAD_WIDTH):
        a = values[:, first : first + half]
        b = values[:, first + half : first + HEAD_WIDTH]
        parts += [a * cosine - b * sine, b * cosine + a * sine]
    return jnp.concatenate(parts, axis=-1)


def row_major(value):
    return with_layout_constraint(value, Layout(tuple(range(value.ndim))))


def swap(value, head_mask, blk_mask):
    groups = lax.axis_size("blk")
    count = lax.axis_size("head") * groups
    mask = head_mask * groups + blk_mask
    pairs = [(i, i ^ mask) for i in range(count)]
    return row_major(lax.ppermute(row_major(value), ("head", "blk"), pairs))


def masks_of(size):
    out, bit = [], size >> 1
    while bit:
        out.append(bit)
        bit >>= 1
    return out


def add(a, b, dtype):
    return (a.astype(F32) + b.astype(F32)).astype(dtype)


def pair(own, received, bit, axis):
    first = jnp.where(bit == 0, own, received)
    second = jnp.where(bit == 0, received, own)
    return jnp.stack([first, second], axis=axis)


def after(value, *others):
    return lax.optimization_barrier((value, *others))[0]


def assemble_kernel(places, *refs):
    parts, out, sems = refs[:-2], refs[-2], refs[-1]
    copies = [
        pltpu.make_async_copy(
            part,
            out.at[pl.ds(row, part.shape[0]), pl.ds(col, part.shape[1])],
            sems.at[i],
        )
        for i, (part, (row, col)) in enumerate(zip(parts, places))
    ]
    for copy in copies:
        copy.start()
    for copy in copies:
        copy.wait()


def assemble(parts, places):
    rows = max(row + part.shape[0] for part, (row, _) in zip(parts, places))
    cols = max(col + part.shape[1] for part, (_, col) in zip(parts, places))
    return pl.pallas_call(
        functools.partial(assemble_kernel, places),
        in_specs=[pl.BlockSpec(memory_space=pl.ANY)] * len(parts),
        out_specs=pl.BlockSpec(memory_space=pltpu.VMEM),
        out_shape=jax.ShapeDtypeStruct((rows, cols), parts[0].dtype),
        scratch_shapes=[pltpu.SemaphoreType.DMA((len(parts),))],
        cost_estimate=pl.CostEstimate(
            flops=0, bytes_accessed=4 * rows * cols, transcendentals=0
        ),
        name="assemble",
    )(*parts)


def stack_rows(parts):
    places, row = [], 0
    for part in parts:
        places.append((row, 0))
        row += part.shape[0]
    return assemble(parts, places)


class Sent:
    value = None


class Flow:
    def __init__(self):
        self.batch, self.before = [], []

    def send(self, value, head_mask, blk_mask):
        sent = Sent()
        self.batch.append((sent, value, head_mask, blk_mask))
        return sent

    def go(self):
        if not self.batch:
            return
        values = tuple(entry[1] for entry in self.batch)
        held = lax.optimization_barrier(values + tuple(sent.value for sent in self.before))
        arrived = [
            swap(value, head_mask, blk_mask)
            for (_, _, head_mask, blk_mask), value in zip(self.batch, held)
        ]
        for (sent, *_), value in zip(self.batch, lax.optimization_barrier(tuple(arrived))):
            sent.value = value
        self.before = [entry[0] for entry in self.batch]
        self.batch = []


    def join(self, value):
        return after(value, *(sent.value for sent in self.before))


class Spread:
    def __init__(self, own, masks):
        self.masks, self.have = masks, {0: own}
        self.sents = {}

    def wave(self, flow, count):
        self.settle()
        for key in sorted(self.have):
            if bin(key).count("1") == count:
                for mask in self.masks:
                    if key == 0 or mask < (key & -key):
                        self.sents[key ^ mask] = flow.send(
                            self.have[key], CROSS if mask == 1 else 0, mask & ~1
                        )

    def settle(self):
        for key, sent in list(self.sents.items()):
            self.have[key] = sent.value
            del self.sents[key]


class Chain:
    def __init__(self, own, masks):
        self.blocks, self.masks, self.sent = own[None], list(masks), None

    def advance(self, flow):
        self.settle()
        if self.masks:
            mask = self.masks.pop(0)
            self.sent = flow.send(self.blocks, CROSS if mask == 1 else 0, mask & ~1)

    def settle(self):
        if self.sent is not None:
            self.blocks = jnp.concatenate([self.blocks, self.sent.value], axis=0)
            self.sent = None


class Fold:
    def __init__(self, blocks, masks):
        self.blocks, self.masks, self.sent = blocks, list(masks), None

    def advance(self, flow):
        if self.sent is not None:
            self.blocks = add(self.keep, self.sent.value, BF16 if self.masks else F32)
            self.sent = None
        if not self.masks:
            return False
        mask = self.masks.pop(0)
        half = self.blocks.shape[0] // 2
        self.keep = self.blocks[:half]
        self.sent = flow.send(self.blocks[half:], CROSS if mask == 1 else 0, mask & ~1)
        return True


class Bulk:
    def __init__(self, masks, count):
        self.masks = masks
        self.pieces, self.sents, self.done = {}, [], {}
        keys = [0]
        self.order = {}
        for mask in masks:
            self.order[mask] = [(key, which) for key in keys for which in range(count)]
            keys = keys + [key ^ mask for key in keys]

    def settle(self):
        waiting = []
        for name, sent in self.sents:
            if sent.value is None:
                waiting.append((name, sent))
            else:
                self.pieces.setdefault(name, []).append(sent.value)
        self.sents = waiting

    def take(self, flow, mask, rows, limit):
        self.limit = limit
        self.settle()
        for name in self.order[mask]:
            piece, offset, total = self.done.get((mask, name), (0, 0, 0))
            have = self.pieces.get(name, [])
            if total == limit or piece >= len(have):
                continue
            value = have[piece][offset : offset + rows]
            offset += value.shape[0]
            total += value.shape[0]
            if offset == have[piece].shape[0]:
                piece, offset = piece + 1, 0
            self.done[mask, name] = (piece, offset, total)
            self.sents.append(((name[0] ^ mask, name[1]), flow.send(value, 0, mask)))
            return True
        return False

    def left(self, mask, which):
        return any(
            self.done.get((m, name), (0, 0, 0))[2] < self.limit
            for m in self.masks
            if mask in (None, m)
            for name in self.order[m]
            if name[1] == which
        )

    def parts(self, which):
        self.settle()
        return {key: parts for (key, place), parts in self.pieces.items() if place == which}


class FfnFold:
    def __init__(self, total, masks, turn):
        count = 1 << len(masks)
        blocks = total.reshape(count, -1, total.shape[1])
        self.blocks = [blocks[i] for i in range(count)]
        self.rows, self.turn = blocks.shape[1], turn
        self.missing, self.tasks, self.sent_rows = [len(masks)] + [0] * (count - 1), {}, {}
        for stage, mask in enumerate(masks):
            half = count >> (stage + 1)
            self.tasks[mask] = [(block, half) for block in range(2 * half - 1, half - 1, -1)]
            for block in range(half, 2 * half):
                self.missing[block] = stage
        self.got, self.sents, self.turning = {}, [], None

    def settle(self):
        waiting = []
        for block, half, sent in self.sents:
            if sent.value is None:
                waiting.append((block, half, sent))
                continue
            parts = self.got.setdefault(block, [])
            parts.append(sent.value)
            if sum(part.shape[0] for part in parts) == self.rows:
                into = block - half
                self.missing[into] -= 1
                received = jnp.concatenate(parts, axis=0)
                self.blocks[into] = add(self.blocks[into], received, BF16 if into else F32)
        self.sents = waiting

    def take(self, flow, mask, rows):
        self.settle()
        for block, half in self.tasks[mask]:
            if self.missing[block]:
                continue
            first = self.sent_rows.get(block, 0)
            piece = self.blocks[block][first : first + rows]
            self.sent_rows[block] = first + piece.shape[0]
            if self.sent_rows[block] == self.rows:
                self.tasks[mask].remove((block, half))
            self.sents.append((block, half, flow.send(piece, 0, mask)))
            return True
        return False

    def take_turn(self, flow):
        self.settle()
        if self.missing[0] or self.turning is not None:
            return False
        total = self.blocks[0].reshape(2, self.rows // 2, -1)
        self.mine = lax.dynamic_index_in_dim(total, self.turn, 0, keepdims=False)
        other = lax.dynamic_index_in_dim(total, 1 - self.turn, 0, keepdims=False)
        self.turning = flow.send(other.astype(BF16), 0, TURN)
        return True

    def result(self):
        rows, cols = self.mine.shape
        out = jnp.zeros((rows, 2 * cols), F32)
        out = lax.dynamic_update_slice(out, self.mine, (0, self.turn * cols))
        received = self.turning.value.astype(F32)
        return lax.dynamic_update_slice(out, received, (0, (1 - self.turn) * cols))


def span_of(pair_ref, group, late, per_seq):
    pair = pair_ref[group]
    seq = pair // per_seq
    first = pair - seq * per_seq
    return seq, jnp.where(late == 0, first, 2 * per_seq - 1 - first)


def tile_visible(place_ref, pair_ref, seg_ref, step, part, per_seq, seq_len):
    group, cross = place_ref[0], place_ref[1]
    piece, low = step // 2, step % 2
    key, count = 0, SEQS * per_seq
    bits = count.bit_length() - 1
    for bit in range(bits):
        key = key + ((piece >> bit) & 1) * (1 << (bits - 1 - bit))
    seq_k, span_k = span_of(
        pair_ref, group ^ (key - key % 2 + low), cross ^ (key % 2), per_seq
    )
    seq_q, span_q = span_of(pair_ref, group ^ part, cross, per_seq)
    last_k = seg_ref[seq_k * seq_len + span_k * BLOCK + BLOCK - 1]
    first_q = seg_ref[seq_q * seq_len + span_q * BLOCK]
    visible = (seq_k == seq_q) & (span_k <= span_q) & (last_k >= first_q)
    spans = 2 * per_seq
    return visible, seq_k * spans + span_k, seq_q * spans + span_q


def tile_mask(seg_row_ref, seg_col_ref, place_k, place_q):
    lanes = lax.broadcasted_iota(jnp.int32, seg_col_ref.shape, 1)
    column = jnp.sum(jnp.where(lanes == place_k, seg_col_ref[...], 0), axis=1, keepdims=True)
    row = seg_row_ref[pl.ds(place_q, 1), :]
    row = jnp.concatenate([row, row], axis=1)
    return column == row


def stack_heads(ref, part):
    rows = pl.ds(part * BLOCK, BLOCK)
    return jnp.concatenate([ref[rows, :HEAD_WIDTH], ref[rows, HEAD_WIDTH:]], axis=0)


def forward_kernel(
    per_seq, place_ref, pair_ref, seg_ref, q_ref, kv_ref, row_ref, col_ref,
    low_ref, out_ref, lse_ref, max_ref, sum_ref, acc_ref,
):
    step = pl.program_id(0)
    seq_len = 2 * per_seq * BLOCK

    @pl.when(step == 0)
    def _():
        max_ref[...] = jnp.full(max_ref.shape, NEGATIVE, F32)
        sum_ref[...] = jnp.zeros(sum_ref.shape, F32)
        acc_ref[...] = jnp.zeros(acc_ref.shape, F32)

    for part in range(2):
        visible, place_k, place_q = tile_visible(
            place_ref, pair_ref, seg_ref, step, part, per_seq, seq_len
        )

        @pl.when(visible)
        def _():
            keys = kv_ref[:, :HEAD_WIDTH]
            values = kv_ref[:, HEAD_WIDTH:]
            queries = stack_heads(q_ref, part)
            scores = lax.dot_general(keys, queries, COLS, preferred_element_type=F32)
            mask = tile_mask(row_ref, col_ref, place_k, place_q)
            scores = jnp.where(mask, scores, NEGATIVE)
            old_max = max_ref[part]
            new_max = jnp.maximum(old_max, jnp.max(scores, axis=0, keepdims=True))
            weights = jnp.where(mask, jnp.exp(scores - new_max), 0.0)
            factor = jnp.exp(old_max - new_max)
            max_ref[part] = new_max
            sum_ref[part] = sum_ref[part] * factor + jnp.sum(weights, axis=0, keepdims=True)
            acc_ref[part] = acc_ref[part] * factor + lax.dot_general(
                values, weights.astype(BF16), ROWS, preferred_element_type=F32
            )

    @pl.when(step == pl.num_programs(0) - 1)
    def _():
        for part in range(2):
            total = sum_ref[part]
            attended = (acc_ref[part] / total).T
            rows = pl.ds(part * BLOCK, BLOCK)
            for head in range(2):
                one = attended[head * BLOCK : (head + 1) * BLOCK]
                cols = pl.ds(head * HEAD_WIDTH, HEAD_WIDTH)
                out_ref[rows, cols] = one
                low_ref[rows, cols] = one.astype(BF16)
            lse_ref[part] = max_ref[part] + jnp.log(total)


def backward_kernel(
    per_seq, place_ref, pair_ref, seg_ref, q_ref, kv_ref, row_ref, col_ref, lse_ref, out_ref, do_ref,
    dq_ref, dk_ref, dv_ref, delta_ref, dq_acc, dk_acc, dv_acc,
):
    step = pl.program_id(0)
    seq_len = 2 * per_seq * BLOCK

    @pl.when(step == 0)
    def _():
        dq_acc[...] = jnp.zeros(dq_acc.shape, F32)
        for part in range(2):
            product = stack_heads(out_ref, part) * stack_heads(do_ref, part).astype(F32)
            delta_ref[part] = jnp.sum(product.T, axis=0, keepdims=True)

    dk_acc[...] = jnp.zeros(dk_acc.shape, F32)
    dv_acc[...] = jnp.zeros(dv_acc.shape, F32)
    for part in range(2):
        visible, place_k, place_q = tile_visible(
            place_ref, pair_ref, seg_ref, step, part, per_seq, seq_len
        )

        @pl.when(visible)
        def _():
            keys = kv_ref[:, :HEAD_WIDTH]
            values = kv_ref[:, HEAD_WIDTH:]
            queries = stack_heads(q_ref, part)
            grads = stack_heads(do_ref, part)
            scores = lax.dot_general(keys, queries, COLS, preferred_element_type=F32)
            mask = tile_mask(row_ref, col_ref, place_k, place_q)
            probs = jnp.where(mask, jnp.exp(scores - lse_ref[part]), 0.0)
            grad_probs = lax.dot_general(values, grads, COLS, preferred_element_type=F32)
            grad_scores = (probs * (grad_probs - delta_ref[part])).astype(BF16)
            dv_acc[...] += jnp.dot(probs.astype(BF16), grads, preferred_element_type=F32)
            dk_acc[...] += jnp.dot(grad_scores, queries, preferred_element_type=F32)
            dq_acc[part] += lax.dot_general(
                grad_scores, keys, ROWS, preferred_element_type=F32
            )

    dk_ref[...] = dk_acc[...].astype(BF16)
    dv_ref[...] = dv_acc[...].astype(BF16)

    @pl.when(step == pl.num_programs(0) - 1)
    def _():
        for part in range(2):
            rows = pl.ds(part * BLOCK, BLOCK)
            for head in range(2):
                one = dq_acc[part, head * BLOCK : (head + 1) * BLOCK]
                dq_ref[rows, pl.ds(head * HEAD_WIDTH, HEAD_WIDTH)] = (
                    one * HEAD_WIDTH ** (-0.5)
                ).astype(BF16)


def whole(shape):
    return pl.BlockSpec(shape, lambda step, *refs: (0,) * len(shape))


def attend(place, pair_order, seg_flat, queries, keys_values, seg_row, seg_col, per_seq):
    steps = keys_values.shape[0] // BLOCK
    rows, width = queries.shape
    return pl.pallas_call(
        functools.partial(forward_kernel, per_seq),
        grid_spec=pltpu.PrefetchScalarGridSpec(
            num_scalar_prefetch=3,
            grid=(steps,),
            in_specs=[
                whole(queries.shape),
                pl.BlockSpec((BLOCK, 2 * HEAD_WIDTH), lambda step, *refs: (step, 0)),
                whole(seg_row.shape),
                whole(seg_col.shape),
            ],
            out_specs=[whole((rows, width)), whole((rows, width)), whole((2, 1, rows))],
            scratch_shapes=[
                pltpu.VMEM((2, 1, rows), F32),
                pltpu.VMEM((2, 1, rows), F32),
                pltpu.VMEM((2, HEAD_WIDTH, rows), F32),
            ],
        ),
        out_shape=[
            jax.ShapeDtypeStruct((rows, width), BF16),
            jax.ShapeDtypeStruct((rows, width), F32),
            jax.ShapeDtypeStruct((2, 1, rows), F32),
        ],
        compiler_params=pltpu.CompilerParams(dimension_semantics=("arbitrary",)),
        cost_estimate=pl.CostEstimate(
            flops=6_000_000_000, bytes_accessed=6_000_000, transcendentals=2_000_000
        ),
        name="attend",
    )(place, pair_order, seg_flat, queries, keys_values, seg_row, seg_col)


def attend_back(
    place, pair_order, seg_flat, queries, keys_values, seg_row, seg_col, lse, out, grads, per_seq
):
    steps = keys_values.shape[0] // BLOCK
    rows, width = queries.shape
    return pl.pallas_call(
        functools.partial(backward_kernel, per_seq),
        grid_spec=pltpu.PrefetchScalarGridSpec(
            num_scalar_prefetch=3,
            grid=(steps,),
            in_specs=[
                whole(queries.shape),
                pl.BlockSpec((BLOCK, 2 * HEAD_WIDTH), lambda step, *refs: (step, 0)),
                whole(seg_row.shape),
                whole(seg_col.shape),
                whole(lse.shape),
                whole(out.shape),
                whole(grads.shape),
            ],
            out_specs=[
                whole((rows, width)),
                pl.BlockSpec((BLOCK, HEAD_WIDTH), lambda step, *refs: (step, 0)),
                pl.BlockSpec((BLOCK, HEAD_WIDTH), lambda step, *refs: (step, 0)),
            ],
            scratch_shapes=[
                pltpu.VMEM((2, 1, rows), F32),
                pltpu.VMEM((2, rows, HEAD_WIDTH), F32),
                pltpu.VMEM((BLOCK, HEAD_WIDTH), F32),
                pltpu.VMEM((BLOCK, HEAD_WIDTH), F32),
            ],
        ),
        out_shape=[
            jax.ShapeDtypeStruct((rows, width), BF16),
            jax.ShapeDtypeStruct((keys_values.shape[0], HEAD_WIDTH), BF16),
            jax.ShapeDtypeStruct((keys_values.shape[0], HEAD_WIDTH), BF16),
        ],
        compiler_params=pltpu.CompilerParams(dimension_semantics=("arbitrary",)),
        cost_estimate=pl.CostEstimate(
            flops=16_000_000_000, bytes_accessed=12_000_000, transcendentals=2_000_000
        ),
        name="attend_back",
    )(place, pair_order, seg_flat, queries, keys_values, seg_row, seg_col, lse, out, grads)


def rms_back(scaled, normed, inv_rms):
    return inv_rms * (scaled - normed * jnp.mean(scaled * normed, axis=-1, keepdims=True))


def bits_of(number, count):
    return [(number >> (count - 1 - i)) & 1 for i in range(count)]


def flip(value, bits, axes):
    for bit, axis in zip(bits, axes):
        value = jnp.where(bit == 0, value, jnp.flip(value, axis))
    return value


def local(
    tokens,
    cotangent,
    segments,
    pair_order,
    norm_in,
    w_query,
    key_weight,
    value_weight,
    w_out,
    norm_mid,
    w_gate,
    w_up,
    w_down,
):
    heads = lax.axis_size("head")
    groups = lax.axis_size("blk")
    group = lax.axis_index("blk")
    head = lax.axis_index("head")
    cross, core = head // 2, head % 2
    turn = (group // TURN) % 2
    low = group % 2
    depth = groups.bit_length() - 1
    token_rows, width = tokens.shape
    group_rows = token_rows * heads
    per_seq = groups // SEQS
    shard = norm_in.shape[0]
    blk_masks = masks_of(groups)
    wide_masks = blk_masks[:-1] + [1]
    far_masks = [mask for mask in blk_masks if mask != TURN]
    key_local = HEAD_WIDTH
    query_local = w_query.shape[1] // heads
    in_cols = query_local + 2 * key_local
    ff_rows, ff_cols = w_gate.shape
    ff_own = ff_cols // 2
    group_bits = bits_of(group, depth)

    wide_axes = [-depth - 2] + [-depth + i for i in range(depth - 1)]
    wide_bits = [cross] + group_bits[:-1]

    def to_wide(value):
        lead = value.shape[:-1]
        value = value.reshape(lead + (2, 2) + (2,) * (depth - 1) + (2 * shard,))
        value = flip(value, wide_bits, wide_axes)
        base = len(lead)
        order = [base] + [base + 2 + i for i in range(depth - 2, -1, -1)]
        order += [base + 1, base + depth + 1]
        return value.transpose(*range(base), *order).reshape(lead + (width,))

    def from_wide(value):
        lead = value.shape[:-1]
        value = value.reshape(lead + (2,) + (2,) * (depth - 1) + (2, 2 * shard))
        base = len(lead)
        order = [base, base + depth] + [base + 1 + i for i in range(depth - 2, -1, -1)]
        order += [base + depth + 1]
        value = value.transpose(*range(base), *order)
        return flip(value, wide_bits, wide_axes).reshape(lead + (width,))

    far_axes = [-depth - 1 + i for i in range(depth - 2)] + [-2]
    far_bits = group_bits[: depth - 2] + [low]

    def to_far(value):
        lead = value.shape[:-1]
        value = value.reshape(lead + (2,) * depth + (ff_rows,))
        value = flip(value, far_bits, far_axes)
        base = len(lead)
        order = [base + depth - 1] + [base + i for i in range(depth - 3, -1, -1)]
        order += [base + depth - 2, base + depth]
        return value.transpose(*range(base), *order).reshape(lead + (width,))

    def from_far(value):
        lead = value.shape[:-1]
        value = value.reshape(lead + (2,) * depth + (ff_rows,))
        base = len(lead)
        order = [base + 1 + i for i in range(depth - 3, -1, -1)]
        order += [base + depth - 1, base, base + depth]
        value = value.transpose(*range(base), *order)
        return flip(value, far_bits, far_axes).reshape(lead + (width,))

    def reversed_key(place, masks):
        bits = [(place >> (len(masks) - 1 - i)) & 1 for i in range(len(masks))]
        return sum(mask for bit, mask in zip(bits, masks[::-1]) if bit)

    def in_fold_order(have, masks):
        return [have[reversed_key(place, masks)] for place in range(1 << len(masks))]

    rows = jnp.arange(group_rows, dtype=jnp.int32)
    part_rows = 2 * token_rows
    local_row = cross * part_rows + (core ^ (rows % part_rows // token_rows)) * token_rows
    local_row = local_row + rows % token_rows
    pairs = [lax.dynamic_index_in_dim(pair_order, group ^ part, keepdims=False) for part in (0, 1)]
    first_span = jnp.where(rows < part_rows, pairs[0], pairs[1]) % per_seq
    span = jnp.where(local_row < BLOCK, first_span, 2 * per_seq - 1 - first_span)
    positions = span * BLOCK + local_row % BLOCK
    angles = positions.astype(F32)[:, None] * frequencies(HEAD_WIDTH)[None, :]
    cosine, sine = jnp.cos(angles), jnp.sin(angles)
    seg_halves = segments.reshape(-1, 2, BLOCK // 2)
    seg_row = jnp.where(core == 0, seg_halves, seg_halves[:, ::-1]).reshape(-1, BLOCK)
    seg_col = seg_row.T
    seg_flat = segments.reshape(-1)
    place = jnp.stack([group, cross]).astype(jnp.int32)

    flow = Flow()

    gains = jnp.zeros((2, heads * groups, shard), BF16)
    gains = lax.dynamic_update_slice(
        gains, jnp.stack([norm_in, norm_mid])[:, None], (0, head * groups + group, 0)
    )
    hops = [blk_masks[:1], blk_masks[-1:], blk_masks[1:-1], [None]]

    def hop():
        nonlocal gains, gain_sent
        if gain_sent is not None:
            gains = gains + gain_sent.value
            gain_sent = None
        if hops:
            *direct, last = hops.pop(0)
            for mask in direct:
                gains = gains + swap(gains, 0, mask)
            gain_sent = flow.send(gains, *((CROSS, 0) if last is None else (0, last)))

    gain_sent = None

    def column_half(weights, bit):
        return jnp.concatenate(
            [
                lax.dynamic_slice_in_dim(weight, bit * (weight.shape[1] // 2), weight.shape[1] // 2, 1)
                for weight in weights
            ],
            axis=1,
        )

    def core_half(value, bit):
        parts, first = [], 0
        for count in (2 * query_local, 2 * key_local, 2 * key_local, 2 * query_local):
            parts.append(
                lax.dynamic_slice_in_dim(value, first + bit * (count // 2), count // 2, 2)
            )
            first += count
        return jnp.concatenate(parts, axis=2)

    attention_weights = (w_query, key_weight, value_weight, w_out)

    def index(value, place):
        return lax.dynamic_index_in_dim(value, place, 0, keepdims=False)

    def halves(weight, bit):
        return lax.dynamic_slice_in_dim(weight, bit * ff_own, ff_own, 1)

    ffn_weights = (w_down, w_gate, w_up)
    bulk, block_rows = Bulk(far_masks, 3), 2 * ff_rows

    def send_turn(which):
        return flow.send(halves(ffn_weights[which], 1 - turn), 0, TURN)

    def end_turn(which, sent):
        own = pair(halves(ffn_weights[which], turn), sent.value, turn, 0)
        bulk.pieces[0, which] = [own.reshape(block_rows, -1)]

    def near(rows):
        return bulk.take(flow, 1, rows, block_rows)

    def high(rows):
        return any([bulk.take(flow, mask, rows, block_rows) for mask in far_masks[:-1]])

    weights_low = flow.send(column_half(attention_weights, 1 - low), 0, 1)
    turned = send_turn(0)
    cot_far = to_far(cotangent)
    cot_x = flow.send(cot_far, CROSS, 0)
    hop()
    flow.go()
    end_turn(0, turned)
    both = pair(column_half(attention_weights, low), weights_low.value, low, 0)
    weights_core = flow.send(core_half(both, 1 - core), CORE, 0)
    hop()
    flow.go()
    own_cols = pair(core_half(both, core), weights_core.value, core, 0).reshape(4 * shard, -1)
    spread_in = Spread(own_cols[:, :in_cols], wide_masks)
    chain_out = Chain(own_cols[:, in_cols:], wide_masks)
    spread_in.wave(flow, 0)
    token_x = to_wide(tokens)
    token_low = flow.send(token_x, 0, 1)
    hop()
    flow.go()
    token_group = jnp.concatenate(
        [token_x, swap(token_x, CORE, 0), token_low.value, swap(token_low.value, CORE, 0)], axis=0
    ).astype(F32)
    spread_in.wave(flow, 1)
    near(block_rows)
    high(ff_rows)
    flow.go()
    for count in range(2, depth):
        if count > 2:
            flow.go()
        spread_in.wave(flow, count)
    chain_out.advance(flow)
    turned = send_turn(1)
    hop()
    flow.go()
    end_turn(1, turned)
    hop()
    spread_in.settle()
    weight_in = jnp.concatenate(in_fold_order(spread_in.have, wide_masks), axis=0)
    gains = gains + swap(gains, CORE, 0)
    gains = gains.reshape(2, width).astype(F32)
    gain_in, gain_mid = to_wide(gains[:1]), gains[1:]
    turned = send_turn(2)
    near(ff_rows)
    high(ff_rows)
    flow.go()
    end_turn(2, turned)

    inv_group = lax.rsqrt(jnp.mean(token_group * token_group, axis=-1, keepdims=True) + EPS)
    input_low = (token_group * inv_group * gain_in).astype(BF16)
    lin = flow.join(jnp.dot(input_low, weight_in, preferred_element_type=F32))
    keys_values = jnp.concatenate(
        [
            rotate(lin[:, query_local : query_local + key_local], cosine, sine).astype(BF16),
            lin[:, query_local + key_local :].astype(BF16),
        ],
        axis=-1,
    )
    queries = rotate(lin[:, :query_local], cosine, sine).astype(BF16)
    queries = queries * jnp.asarray(HEAD_WIDTH ** (-0.5), BF16)

    spread_kv = Spread(keys_values, wide_masks)
    spread_kv.wave(flow, 0)
    near(ff_rows)
    near(ff_rows)
    flow.go()
    spread_kv.wave(flow, 1)
    near(ff_rows)
    high(ff_rows)
    flow.go()
    for count in range(2, depth):
        if count > 2:
            flow.go()
        spread_kv.wave(flow, count)
    chain_out.advance(flow)
    high(ff_rows)
    near(ff_rows)
    flow.go()
    spread_kv.settle()
    kv_all = jnp.concatenate(in_fold_order(spread_kv.have, wide_masks), axis=0)
    while chain_out.masks:
        chain_out.advance(flow)
        if not chain_out.masks:
            high(ff_rows)
            near(ff_rows)
            cot_t = flow.send(cot_far, 0, TURN)
        flow.go()
    attention_low, attention_f, lse = attend(
        place, pair_order, seg_flat, queries, kv_all, seg_row, seg_col, per_seq
    )
    attention_low = flow.join(attention_low)
    chain_out.settle()
    weight_out = chain_out.blocks.reshape(width, -1)
    branch = lax.dot_general(attention_low, weight_out, COLS, preferred_element_type=F32)
    branch = row_major(branch.astype(BF16)).reshape(2, 2, token_rows, width)
    branch_across = add(branch[1, 0], swap(branch[1, 1], CORE, 0), BF16)
    branch_own = add(branch[0, 0], swap(branch[0, 1], CORE, 0), F32)
    branch_sent = flow.send(branch_across, 0, 1)
    cot_xt = flow.send(cot_t.value, CROSS, 0)
    high(ff_rows // 2)
    flow.go()
    branch = branch_own + branch_sent.value.astype(F32)

    tokens_f = tokens.astype(F32)
    middle = tokens_f + from_wide(branch)
    inv_mid = lax.rsqrt(jnp.mean(middle * middle, axis=-1, keepdims=True) + EPS)
    normed_mid = middle * inv_mid
    mid_low = to_far((normed_mid * gain_mid).astype(BF16))

    half = width // 2
    left, right = mid_low[:, :half], mid_low[:, half:]
    left_x = flow.send(left, CROSS, 0)
    right_t = flow.send(right, 0, TURN)
    near(ff_rows)
    high(ff_rows // 2)
    flow.go()
    left_t = flow.send(left, 0, TURN)
    right_x = flow.send(right, CROSS, 0)
    left_xt = flow.send(left_x.value, 0, TURN)
    right_xt = flow.send(right_t.value, CROSS, 0)
    high(ff_rows)
    flow.go()
    def four_rows(parts, first_col):
        return [(part, (i * token_rows, first_col)) for i, part in enumerate(parts)]

    placed = four_rows([left, left_t.value, left_x.value, left_xt.value], 0)
    placed += four_rows([right, right_t.value, right_x.value, right_xt.value], half)
    mid_four = assemble([part for part, _ in placed], [where for _, where in placed])
    early = [near(block_rows) for _ in range(2)] + [high(block_rows)]
    flow.go()

    def eight(four):
        return stack_rows([four, swap(four, CORE, 0)])

    mid_group = eight(mid_four)
    cot_four = jnp.concatenate([cot_far, cot_t.value, cot_x.value, cot_xt.value], axis=0)
    grad_group = jnp.concatenate([cot_four, swap(cot_four, CORE, 0)], axis=0)

    def weight_of(which):
        have = bulk.parts(which)
        return jnp.concatenate(
            [part for parts in in_fold_order(have, far_masks) for part in parts], axis=0
        )

    while bulk.left(None, 0):
        near(block_rows), high(block_rows)
        flow.go()
    down = weight_of(0)
    grad_hidden = flow.join(jnp.dot(grad_group, down, preferred_element_type=F32))
    while bulk.left(1, 1):
        near(block_rows), high(block_rows)
        flow.go()
    while True:
        more = [near(block_rows) for _ in range(4)] + [high(block_rows)]
        flow.go()
        if not bulk.left(None, 2):
            break
    gate = weight_of(1)
    gate_lin = flow.join(jnp.dot(mid_group, gate, preferred_element_type=F32))
    up = weight_of(2)
    up_proj = jnp.dot(mid_group, up, preferred_element_type=F32)
    gate_sig = jax.nn.sigmoid(gate_lin)
    gate_silu = gate_lin * gate_sig
    hidden_act = (gate_silu * up_proj).astype(BF16)
    grad_gate_lin = (
        grad_hidden * up_proj * gate_sig * (1.0 + gate_lin * (1.0 - gate_sig))
    ).astype(BF16)
    grad_up_proj = (grad_hidden * gate_silu).astype(BF16)

    def ffn_fold(lhs, rhs):
        total = lax.dot_general(lhs, rhs, ROWS, preferred_element_type=F32)
        total = row_major(total.astype(BF16))
        return FfnFold(total, far_masks[::-1], turn)

    down_fold = ffn_fold(grad_group, hidden_act)
    ffn_folds = [down_fold]

    def near(rows):
        found = [
            (-block, i)
            for i, fold in enumerate(ffn_folds)
            for block, _ in fold.tasks[1][:1]
            if not fold.missing[block]
        ]
        return bool(found) and ffn_folds[min(found)[1]].take(flow, 1, rows)

    def high(rows):
        found = False
        for mask in far_masks[:-1][::-1]:
            found = any(fold.take(flow, mask, rows) for fold in ffn_folds) or found
        return found

    near(ff_rows)
    flow.go()
    mid_partial = lax.dot_general(
        grad_gate_lin, gate, COLS, preferred_element_type=F32
    ) + lax.dot_general(grad_up_proj, up, COLS, preferred_element_type=F32)
    mid_partial = flow.join(row_major(mid_partial.astype(BF16))).reshape(2, 2, 2, token_rows, width)
    four = add(mid_partial[0], swap(mid_partial[1], CORE, 0), BF16)
    left, right = four[..., :half], four[..., half:]
    left_sent = flow.send(left[:, 1], 0, TURN)
    right_sent = flow.send(right[1], CROSS, 0)
    near(ff_rows)
    flow.go()
    gate_fold = ffn_fold(mid_group, grad_gate_lin)
    ffn_partial = lax.dot_general(hidden_act, down, COLS, preferred_element_type=F32)
    ffn_partial = row_major(ffn_partial.astype(BF16)).reshape(2, 2, 2, token_rows, width)
    out_four = add(ffn_partial[0], swap(ffn_partial[1], CORE, 0), BF16)
    left = add(left[:, 0], left_sent.value, BF16)
    right = add(right[0], right_sent.value, BF16)
    left_sent = flow.send(left[1], CROSS, 0)
    right_sent = flow.send(right[1], 0, TURN)
    high(ff_rows // 2)
    flow.go()
    ffn_folds.append(gate_fold)
    grad_mid = jnp.concatenate(
        [add(left[0], left_sent.value, F32), add(right[0], right_sent.value, F32)], axis=-1
    )
    grad_mid = from_far(grad_mid)
    norm_mid_sum = jnp.sum(grad_mid * normed_mid, axis=0)
    grad_y = cotangent.astype(F32)
    grad_middle = grad_y + rms_back(grad_mid * gain_mid, normed_mid, inv_mid)
    grad_branch = to_wide(grad_middle.astype(BF16))
    branch_low = flow.send(grad_branch, 0, 1)
    high(ff_rows // 2)
    out_parts = [flow.send(out_four[1, 0], CROSS, 0)]
    flow.go()
    up_fold = ffn_fold(mid_group, grad_up_proj)
    ffn_folds.append(up_fold)
    branch_group = jnp.concatenate(
        [grad_branch, swap(grad_branch, CORE, 0), branch_low.value, swap(branch_low.value, CORE, 0)],
        axis=0,
    )
    grad_attention = jnp.dot(branch_group, weight_out, preferred_element_type=F32).astype(BF16)

    def weight_fold(lhs, rhs, extra=None):
        total = lax.dot_general(lhs, rhs, ROWS, preferred_element_type=F32)
        if extra is not None:
            column = jnp.broadcast_to(to_wide(extra[None])[0][:, None], (width, 128))
            total = jnp.concatenate([total, column], axis=1)
        total = row_major(total.astype(BF16))
        return Fold(total.reshape(groups, 4 * shard, -1), wide_masks[::-1])

    out_fold = weight_fold(branch_group, attention_low, norm_mid_sum)
    out_fold.advance(flow)
    near(block_rows)
    high(ff_rows)
    flow.go()
    grad_queries, grad_keys, grad_values = attend_back(
        place, pair_order, seg_flat, queries, kv_all, seg_row, seg_col,
        lse, attention_f, grad_attention, per_seq,
    )
    grad_queries = flow.join(grad_queries)
    grad_keys = flow.join(grad_keys)
    key_fold = Fold(grad_keys.reshape(groups, group_rows, -1), wide_masks[::-1])
    value_fold = Fold(grad_values.reshape(groups, group_rows, -1), wide_masks[::-1])
    key_fold.advance(flow)
    near(block_rows)
    high(ff_rows)
    flow.go()
    key_fold.advance(flow)
    value_fold.advance(flow)
    near(block_rows)
    high(ff_rows)
    flow.go()
    query_lin = rotate(grad_queries.astype(F32), cosine, -sine).astype(BF16)
    query_fold = weight_fold(input_low, query_lin)
    turns = [down_fold, gate_fold, up_fold]

    def take_turn():
        for fold in turns:
            if fold.take_turn(flow):
                turns.remove(fold)
                return

    while True:
        running = [fold.advance(flow) for fold in (key_fold, value_fold)]
        if not any(running):
            break
        query_fold.advance(flow)
        if all(running):
            high(ff_rows // 2)
            near(block_rows)
        else:
            near(ff_rows)
            if len(out_parts) == 1:
                out_parts.append(flow.send(out_four[1, 1], CROSS, 0))
        flow.go()
    high(ff_rows // 2)
    take_turn()
    flow.go()
    keys_low, values_low = key_fold.blocks[0].astype(BF16), value_fold.blocks[0].astype(BF16)
    kv_lin = jnp.concatenate(
        [rotate(keys_low.astype(F32), cosine, -sine).astype(BF16), values_low], axis=-1
    )
    grad_lin = jnp.concatenate([query_lin, kv_lin], axis=-1)
    grad_in = lax.dot_general(grad_lin, weight_in, COLS, preferred_element_type=F32)
    grad_in = row_major(grad_in.astype(BF16)).reshape(2, 2, token_rows, width)
    in_across = add(grad_in[1, 0], swap(grad_in[1, 1], CORE, 0), BF16)
    in_own = add(grad_in[0, 0], swap(grad_in[0, 1], CORE, 0), F32)
    in_sent = flow.send(in_across, 0, 1)
    kv_fold = weight_fold(input_low, kv_lin)
    kv_fold.advance(flow)
    query_fold.advance(flow)
    out_fold.advance(flow)
    high(ff_rows // 2)
    near(ff_rows)
    flow.go()
    kv_fold.advance(flow)
    query_fold.advance(flow)
    high(ff_rows // 2)
    near(ff_rows)
    flow.go()
    kv_fold.advance(flow)
    out_fold.advance(flow)
    high(ff_rows)
    near(block_rows)
    take_turn()
    flow.go()
    out_two = [add(out_four[0, i], sent.value, BF16) for i, sent in enumerate(out_parts)]
    while True:
        running = [fold.advance(flow) for fold in (kv_fold, query_fold, out_fold)]
        if not any(running):
            break
        near(block_rows), high(block_rows)
        flow.go()

    total = jnp.concatenate(
        [fold.blocks[0] for fold in (query_fold, kv_fold, out_fold)], axis=-1
    ).reshape(2, 2, shard, -1)
    total_core = flow.send(index(total, 1 - core).astype(BF16), CORE, 0)
    out_sent = flow.send(out_two[1], 0, TURN)
    flow.go()
    total = pair(index(total, core), total_core.value.astype(F32), core, 1)
    total_low = flow.send(index(total, 1 - low).astype(BF16), 0, 1)
    while True:
        near(block_rows), high(block_rows)
        for fold in list(turns):
            if fold.take_turn(flow):
                turns.remove(fold)
        if not flow.batch:
            break
        flow.go()
    total = pair(index(total, low), total_low.value.astype(F32), low, 0).reshape(4, shard, -1)
    layer_out = (middle + from_far(add(out_two[0], out_sent.value, F32))).astype(BF16)
    scaled = in_own + in_sent.value.astype(F32)
    tokens_f = tokens.astype(F32)
    inv_in = inv_group[:token_rows]
    normed_in = tokens_f * inv_in
    grad_tokens = grad_middle + rms_back(from_wide(scaled * gain_in), normed_in, inv_in)

    def columns(first, count):
        return total[..., first : first + count].transpose(1, 0, 2).reshape(shard, -1)

    in_grads = [
        columns(0, query_local),
        columns(query_local, key_local),
        columns(query_local + key_local, key_local),
    ]
    grad_norm_in = sum(
        jnp.sum(grad * weight.astype(F32), axis=1)
        for grad, weight in zip(in_grads, attention_weights)
    ) / norm_in.astype(F32)
    grad_norm_mid = jnp.sum(total[..., in_cols + query_local], axis=0)
    return (
        layer_out,
        grad_tokens,
        grad_norm_in,
        *in_grads,
        columns(in_cols, query_local),
        grad_norm_mid,
        gate_fold.result(),
        up_fold.result(),
        down_fold.result(),
    )


def solution(mesh):
    rows = P(("blk", "head"), None)
    shards = P(("head", "blk"), None)
    vector = P(("head", "blk"))
    hidden = P("blk", "head")
    return jax.shard_map(
        local,
        mesh=mesh,
        in_specs=(
            rows, rows, P(), P(), vector, shards, shards, shards, shards, vector, hidden, hidden, hidden,
        ),
        out_specs=(
            rows, rows, vector, shards, shards, shards, shards, vector, hidden, hidden, hidden,
        ),
        check_vma=False,
    )
```

```python
import functools

import jax
import jax.numpy as jnp
from jax import lax
from jax.experimental import pallas as pl
from jax.experimental.layout import Layout, with_layout_constraint
from jax.experimental.pallas import tpu as pltpu
from jax.sharding import PartitionSpec as P

QUERY_HEAD_COUNT = 8
KEY_VALUE_HEADS = 4
HEAD_WIDTH = 256
SEQS = 2
BLOCK = 256

EPS = 1e-06
THETA = 1000042.0
NEGATIVE = -1e30
ROWS = (((0,), (0,)), ((), ()))
COLS = (((1,), (1,)), ((), ()))
BF16 = jnp.bfloat16
F32 = jnp.float32

CORE, CROSS, TURN = 1, 2, 2


def frequencies(head_size):
    return 1.0 / THETA ** (jnp.arange(0, head_size, 2, dtype=F32) / head_size)


def rotate(values, cosine, sine):
    half = HEAD_WIDTH // 2
    parts = []
    for first in range(0, values.shape[-1], HEAD_WIDTH):
        a = values[:, first : first + half]
        b = values[:, first + half : first + HEAD_WIDTH]
        parts += [a * cosine - b * sine, b * cosine + a * sine]
    return jnp.concatenate(parts, axis=-1)


def row_major(value):
    return with_layout_constraint(value, Layout(tuple(range(value.ndim))))


def swap(value, head_mask, blk_mask):
    groups = lax.axis_size("blk")
    count = lax.axis_size("head") * groups
    mask = head_mask * groups + blk_mask
    pairs = [(i, i ^ mask) for i in range(count)]
    return row_major(lax.ppermute(row_major(value), ("head", "blk"), pairs))


def masks_of(size):
    out, bit = [], size >> 1
    while bit:
        out.append(bit)
        bit >>= 1
    return out


def add(a, b, dtype):
    return (a.astype(F32) + b.astype(F32)).astype(dtype)


def pair(own, received, bit, axis):
    first = jnp.where(bit == 0, own, received)
    second = jnp.where(bit == 0, received, own)
    return jnp.stack([first, second], axis=axis)


def after(value, *others):
    return lax.optimization_barrier((value, *others))[0]


def assemble_kernel(places, *refs):
    parts, out, sems = refs[:-2], refs[-2], refs[-1]
    copies = [
        pltpu.make_async_copy(
            part,
            out.at[pl.ds(row, part.shape[0]), pl.ds(col, part.shape[1])],
            sems.at[i],
        )
        for i, (part, (row, col)) in enumerate(zip(parts, places))
    ]
    for copy in copies:
        copy.start()
    for copy in copies:
        copy.wait()


def assemble(parts, places):
    rows = max(row + part.shape[0] for part, (row, _) in zip(parts, places))
    cols = max(col + part.shape[1] for part, (_, col) in zip(parts, places))
    return pl.pallas_call(
        functools.partial(assemble_kernel, places),
        in_specs=[pl.BlockSpec(memory_space=pl.ANY)] * len(parts),
        out_specs=pl.BlockSpec(memory_space=pltpu.VMEM),
        out_shape=jax.ShapeDtypeStruct((rows, cols), parts[0].dtype),
        scratch_shapes=[pltpu.SemaphoreType.DMA((len(parts),))],
        cost_estimate=pl.CostEstimate(
            flops=0, bytes_accessed=4 * rows * cols, transcendentals=0
        ),
        name="assemble",
    )(*parts)


def stack_rows(parts):
    places, row = [], 0
    for part in parts:
        places.append((row, 0))
        row += part.shape[0]
    return assemble(parts, places)


class Sent:
    value = None


class Flow:
    def __init__(self):
        self.batch, self.before = [], []

    def send(self, value, head_mask, blk_mask):
        sent = Sent()
        self.batch.append((sent, value, head_mask, blk_mask))
        return sent

    def go(self):
        if not self.batch:
            return
        values = tuple(entry[1] for entry in self.batch)
        held = lax.optimization_barrier(values + tuple(sent.value for sent in self.before))
        arrived = [
            swap(value, head_mask, blk_mask)
            for (_, _, head_mask, blk_mask), value in zip(self.batch, held)
        ]
        for (sent, *_), value in zip(self.batch, lax.optimization_barrier(tuple(arrived))):
            sent.value = value
        self.before = [entry[0] for entry in self.batch]
        self.batch = []


    def join(self, value):
        return after(value, *(sent.value for sent in self.before))


class Spread:
    def __init__(self, own, masks):
        self.masks, self.have = masks, {0: own}
        self.sents = {}

    def wave(self, flow, count):
        self.settle()
        for key in sorted(self.have):
            if bin(key).count("1") == count:
                for mask in self.masks:
                    if key == 0 or mask < (key & -key):
                        self.sents[key ^ mask] = flow.send(
                            self.have[key], CROSS if mask == 1 else 0, mask & ~1
                        )

    def settle(self):
        for key, sent in list(self.sents.items()):
            self.have[key] = sent.value
            del self.sents[key]


class Chain:
    def __init__(self, own, masks):
        self.blocks, self.masks, self.sent = own[None], list(masks), None

    def advance(self, flow):
        self.settle()
        if self.masks:
            mask = self.masks.pop(0)
            self.sent = flow.send(self.blocks, CROSS if mask == 1 else 0, mask & ~1)

    def settle(self):
        if self.sent is not None:
            self.blocks = jnp.concatenate([self.blocks, self.sent.value], axis=0)
            self.sent = None


class Fold:
    def __init__(self, blocks, masks):
        self.blocks, self.masks, self.sent = blocks, list(masks), None

    def advance(self, flow):
        if self.sent is not None:
            self.blocks = add(self.keep, self.sent.value, BF16 if self.masks else F32)
            self.sent = None
        if not self.masks:
            return False
        mask = self.masks.pop(0)
        half = self.blocks.shape[0] // 2
        self.keep = self.blocks[:half]
        self.sent = flow.send(self.blocks[half:], CROSS if mask == 1 else 0, mask & ~1)
        return True


class Bulk:
    def __init__(self, masks, count):
        self.masks = masks
        self.pieces, self.sents, self.done = {}, [], {}
        keys = [0]
        self.order = {}
        for mask in masks:
            self.order[mask] = [(key, which) for key in keys for which in range(count)]
            keys = keys + [key ^ mask for key in keys]

    def settle(self):
        waiting = []
        for name, sent in self.sents:
            if sent.value is None:
                waiting.append((name, sent))
            else:
                self.pieces.setdefault(name, []).append(sent.value)
        self.sents = waiting

    def take(self, flow, mask, rows, limit):
        self.limit = limit
        self.settle()
        for name in self.order[mask]:
            piece, offset, total = self.done.get((mask, name), (0, 0, 0))
            have = self.pieces.get(name, [])
            if total == limit or piece >= len(have):
                continue
            value = have[piece][offset : offset + rows]
            offset += value.shape[0]
            total += value.shape[0]
            if offset == have[piece].shape[0]:
                piece, offset = piece + 1, 0
            self.done[mask, name] = (piece, offset, total)
            self.sents.append(((name[0] ^ mask, name[1]), flow.send(value, 0, mask)))
            return True
        return False

    def left(self, mask, which):
        return any(
            self.done.get((m, name), (0, 0, 0))[2] < self.limit
            for m in self.masks
            if mask in (None, m)
            for name in self.order[m]
            if name[1] == which
        )

    def parts(self, which):
        self.settle()
        return {key: parts for (key, place), parts in self.pieces.items() if place == which}


class FfnFold:
    def __init__(self, total, masks, turn):
        count = 1 << len(masks)
        blocks = total.reshape(count, -1, total.shape[1])
        self.blocks = [blocks[i] for i in range(count)]
        self.rows, self.turn = blocks.shape[1], turn
        self.missing, self.tasks, self.sent_rows = [len(masks)] + [0] * (count - 1), {}, {}
        for stage, mask in enumerate(masks):
            half = count >> (stage + 1)
            self.tasks[mask] = [(block, half) for block in range(2 * half - 1, half - 1, -1)]
            for block in range(half, 2 * half):
                self.missing[block] = stage
        self.got, self.sents, self.turning = {}, [], None

    def settle(self):
        waiting = []
        for block, half, sent in self.sents:
            if sent.value is None:
                waiting.append((block, half, sent))
                continue
            parts = self.got.setdefault(block, [])
            parts.append(sent.value)
            if sum(part.shape[0] for part in parts) == self.rows:
                into = block - half
                self.missing[into] -= 1
                received = jnp.concatenate(parts, axis=0)
                self.blocks[into] = add(self.blocks[into], received, BF16 if into else F32)
        self.sents = waiting

    def take(self, flow, mask, rows):
        self.settle()
        for block, half in self.tasks[mask]:
            if self.missing[block]:
                continue
            first = self.sent_rows.get(block, 0)
            piece = self.blocks[block][first : first + rows]
            self.sent_rows[block] = first + piece.shape[0]
            if self.sent_rows[block] == self.rows:
                self.tasks[mask].remove((block, half))
            self.sents.append((block, half, flow.send(piece, 0, mask)))
            return True
        return False

    def take_turn(self, flow):
        self.settle()
        if self.missing[0] or self.turning is not None:
            return False
        total = self.blocks[0].reshape(2, self.rows // 2, -1)
        self.mine = lax.dynamic_index_in_dim(total, self.turn, 0, keepdims=False)
        other = lax.dynamic_index_in_dim(total, 1 - self.turn, 0, keepdims=False)
        self.turning = flow.send(other.astype(BF16), 0, TURN)
        return True

    def result(self):
        rows, cols = self.mine.shape
        out = jnp.zeros((rows, 2 * cols), F32)
        out = lax.dynamic_update_slice(out, self.mine, (0, self.turn * cols))
        received = self.turning.value.astype(F32)
        return lax.dynamic_update_slice(out, received, (0, (1 - self.turn) * cols))


def span_of(pair_ref, group, late, per_seq):
    pair = pair_ref[group]
    seq = pair // per_seq
    first = pair - seq * per_seq
    return seq, jnp.where(late == 0, first, 2 * per_seq - 1 - first)


def tile_visible(place_ref, pair_ref, seg_ref, step, part, per_seq, seq_len):
    group, cross = place_ref[0], place_ref[1]
    piece, low = step // 2, step % 2
    key, count = 0, SEQS * per_seq
    bits = count.bit_length() - 1
    for bit in range(bits):
        key = key + ((piece >> bit) & 1) * (1 << (bits - 1 - bit))
    seq_k, span_k = span_of(
        pair_ref, group ^ (key - key % 2 + low), cross ^ (key % 2), per_seq
    )
    seq_q, span_q = span_of(pair_ref, group ^ part, cross, per_seq)
    last_k = seg_ref[seq_k * seq_len + span_k * BLOCK + BLOCK - 1]
    first_q = seg_ref[seq_q * seq_len + span_q * BLOCK]
    visible = (seq_k == seq_q) & (span_k <= span_q) & (last_k >= first_q)
    spans = 2 * per_seq
    return visible, seq_k * spans + span_k, seq_q * spans + span_q


def tile_mask(seg_row_ref, seg_col_ref, place_k, place_q):
    lanes = lax.broadcasted_iota(jnp.int32, seg_col_ref.shape, 1)
    column = jnp.sum(jnp.where(lanes == place_k, seg_col_ref[...], 0), axis=1, keepdims=True)
    row = seg_row_ref[pl.ds(place_q, 1), :]
    row = jnp.concatenate([row, row], axis=1)
    return column == row


def stack_heads(ref, part):
    rows = pl.ds(part * BLOCK, BLOCK)
    return jnp.concatenate([ref[rows, :HEAD_WIDTH], ref[rows, HEAD_WIDTH:]], axis=0)


def forward_kernel(
    per_seq, place_ref, pair_ref, seg_ref, q_ref, kv_ref, row_ref, col_ref,
    low_ref, out_ref, lse_ref, max_ref, sum_ref, acc_ref,
):
    step = pl.program_id(0)
    seq_len = 2 * per_seq * BLOCK

    @pl.when(step == 0)
    def _():
        max_ref[...] = jnp.full(max_ref.shape, NEGATIVE, F32)
        sum_ref[...] = jnp.zeros(sum_ref.shape, F32)
        acc_ref[...] = jnp.zeros(acc_ref.shape, F32)

    for part in range(2):
        visible, place_k, place_q = tile_visible(
            place_ref, pair_ref, seg_ref, step, part, per_seq, seq_len
        )

        @pl.when(visible)
        def _():
            keys = kv_ref[:, :HEAD_WIDTH]
            values = kv_ref[:, HEAD_WIDTH:]
            queries = stack_heads(q_ref, part)
            scores = lax.dot_general(keys, queries, COLS, preferred_element_type=F32)
            mask = tile_mask(row_ref, col_ref, place_k, place_q)
            scores = jnp.where(mask, scores, NEGATIVE)
            old_max = max_ref[part]
            new_max = jnp.maximum(old_max, jnp.max(scores, axis=0, keepdims=True))
            weights = jnp.where(mask, jnp.exp(scores - new_max), 0.0)
            factor = jnp.exp(old_max - new_max)
            max_ref[part] = new_max
            sum_ref[part] = sum_ref[part] * factor + jnp.sum(weights, axis=0, keepdims=True)
            acc_ref[part] = acc_ref[part] * factor + lax.dot_general(
                values, weights.astype(BF16), ROWS, preferred_element_type=F32
            )

    @pl.when(step == pl.num_programs(0) - 1)
    def _():
        for part in range(2):
            total = sum_ref[part]
            attended = (acc_ref[part] / total).T
            rows = pl.ds(part * BLOCK, BLOCK)
            for head in range(2):
                one = attended[head * BLOCK : (head + 1) * BLOCK]
                cols = pl.ds(head * HEAD_WIDTH, HEAD_WIDTH)
                out_ref[rows, cols] = one
                low_ref[rows, cols] = one.astype(BF16)
            lse_ref[part] = max_ref[part] + jnp.log(total)


def backward_kernel(
    per_seq, place_ref, pair_ref, seg_ref, q_ref, kv_ref, row_ref, col_ref, lse_ref, out_ref, do_ref,
    dq_ref, dk_ref, dv_ref, delta_ref, dq_acc, dk_acc, dv_acc,
):
    step = pl.program_id(0)
    seq_len = 2 * per_seq * BLOCK

    @pl.when(step == 0)
    def _():
        dq_acc[...] = jnp.zeros(dq_acc.shape, F32)
        for part in range(2):
            product = stack_heads(out_ref, part) * stack_heads(do_ref, part).astype(F32)
            delta_ref[part] = jnp.sum(product.T, axis=0, keepdims=True)

    dk_acc[...] = jnp.zeros(dk_acc.shape, F32)
    dv_acc[...] = jnp.zeros(dv_acc.shape, F32)
    for part in range(2):
        visible, place_k, place_q = tile_visible(
            place_ref, pair_ref, seg_ref, step, part, per_seq, seq_len
        )

        @pl.when(visible)
        def _():
            keys = kv_ref[:, :HEAD_WIDTH]
            values = kv_ref[:, HEAD_WIDTH:]
            queries = stack_heads(q_ref, part)
            grads = stack_heads(do_ref, part)
            scores = lax.dot_general(keys, queries, COLS, preferred_element_type=F32)
            mask = tile_mask(row_ref, col_ref, place_k, place_q)
            probs = jnp.where(mask, jnp.exp(scores - lse_ref[part]), 0.0)
            grad_probs = lax.dot_general(values, grads, COLS, preferred_element_type=F32)
            grad_scores = (probs * (grad_probs - delta_ref[part])).astype(BF16)
            dv_acc[...] += jnp.dot(probs.astype(BF16), grads, preferred_element_type=F32)
            dk_acc[...] += jnp.dot(grad_scores, queries, preferred_element_type=F32)
            dq_acc[part] += lax.dot_general(
                grad_scores, keys, ROWS, preferred_element_type=F32
            )

    dk_ref[...] = dk_acc[...].astype(BF16)
    dv_ref[...] = dv_acc[...].astype(BF16)

    @pl.when(step == pl.num_programs(0) - 1)
    def _():
        for part in range(2):
            rows = pl.ds(part * BLOCK, BLOCK)
            for head in range(2):
                one = dq_acc[part, head * BLOCK : (head + 1) * BLOCK]
                dq_ref[rows, pl.ds(head * HEAD_WIDTH, HEAD_WIDTH)] = (
                    one * HEAD_WIDTH ** (-0.5)
                ).astype(BF16)


def whole(shape):
    return pl.BlockSpec(shape, lambda step, *refs: (0,) * len(shape))


def attend(place, pair_order, seg_flat, queries, keys_values, seg_row, seg_col, per_seq):
    steps = keys_values.shape[0] // BLOCK
    rows, width = queries.shape
    return pl.pallas_call(
        functools.partial(forward_kernel, per_seq),
        grid_spec=pltpu.PrefetchScalarGridSpec(
            num_scalar_prefetch=3,
            grid=(steps,),
            in_specs=[
                whole(queries.shape),
                pl.BlockSpec((BLOCK, 2 * HEAD_WIDTH), lambda step, *refs: (step, 0)),
                whole(seg_row.shape),
                whole(seg_col.shape),
            ],
            out_specs=[whole((rows, width)), whole((rows, width)), whole((2, 1, rows))],
            scratch_shapes=[
                pltpu.VMEM((2, 1, rows), F32),
                pltpu.VMEM((2, 1, rows), F32),
                pltpu.VMEM((2, HEAD_WIDTH, rows), F32),
            ],
        ),
        out_shape=[
            jax.ShapeDtypeStruct((rows, width), BF16),
            jax.ShapeDtypeStruct((rows, width), F32),
            jax.ShapeDtypeStruct((2, 1, rows), F32),
        ],
        compiler_params=pltpu.CompilerParams(dimension_semantics=("arbitrary",)),
        cost_estimate=pl.CostEstimate(
            flops=6_000_000_000, bytes_accessed=6_000_000, transcendentals=2_000_000
        ),
        name="attend",
    )(place, pair_order, seg_flat, queries, keys_values, seg_row, seg_col)


def attend_back(
    place, pair_order, seg_flat, queries, keys_values, seg_row, seg_col, lse, out, grads, per_seq
):
    steps = keys_values.shape[0] // BLOCK
    rows, width = queries.shape
    return pl.pallas_call(
        functools.partial(backward_kernel, per_seq),
        grid_spec=pltpu.PrefetchScalarGridSpec(
            num_scalar_prefetch=3,
            grid=(steps,),
            in_specs=[
                whole(queries.shape),
                pl.BlockSpec((BLOCK, 2 * HEAD_WIDTH), lambda step, *refs: (step, 0)),
                whole(seg_row.shape),
                whole(seg_col.shape),
                whole(lse.shape),
                whole(out.shape),
                whole(grads.shape),
            ],
            out_specs=[
                whole((rows, width)),
                pl.BlockSpec((BLOCK, HEAD_WIDTH), lambda step, *refs: (step, 0)),
                pl.BlockSpec((BLOCK, HEAD_WIDTH), lambda step, *refs: (step, 0)),
            ],
            scratch_shapes=[
                pltpu.VMEM((2, 1, rows), F32),
                pltpu.VMEM((2, rows, HEAD_WIDTH), F32),
                pltpu.VMEM((BLOCK, HEAD_WIDTH), F32),
                pltpu.VMEM((BLOCK, HEAD_WIDTH), F32),
            ],
        ),
        out_shape=[
            jax.ShapeDtypeStruct((rows, width), BF16),
            jax.ShapeDtypeStruct((keys_values.shape[0], HEAD_WIDTH), BF16),
            jax.ShapeDtypeStruct((keys_values.shape[0], HEAD_WIDTH), BF16),
        ],
        compiler_params=pltpu.CompilerParams(dimension_semantics=("arbitrary",)),
        cost_estimate=pl.CostEstimate(
            flops=16_000_000_000, bytes_accessed=12_000_000, transcendentals=2_000_000
        ),
        name="attend_back",
    )(place, pair_order, seg_flat, queries, keys_values, seg_row, seg_col, lse, out, grads)


def rms_back(scaled, normed, inv_rms):
    return inv_rms * (scaled - normed * jnp.mean(scaled * normed, axis=-1, keepdims=True))


def bits_of(number, count):
    return [(number >> (count - 1 - i)) & 1 for i in range(count)]


def flip(value, bits, axes):
    for bit, axis in zip(bits, axes):
        value = jnp.where(bit == 0, value, jnp.flip(value, axis))
    return value


def local(
    tokens,
    cotangent,
    segments,
    pair_order,
    norm_in,
    w_query,
    key_weight,
    value_weight,
    w_out,
    norm_mid,
    w_gate,
    w_up,
    w_down,
):
    heads = lax.axis_size("head")
    groups = lax.axis_size("blk")
    group = lax.axis_index("blk")
    head = lax.axis_index("head")
    cross, core = head // 2, head % 2
    turn = (group // TURN) % 2
    low = group % 2
    depth = groups.bit_length() - 1
    token_rows, width = tokens.shape
    group_rows = token_rows * heads
    per_seq = groups // SEQS
    shard = norm_in.shape[0]
    blk_masks = masks_of(groups)
    wide_masks = blk_masks[:-1] + [1]
    far_masks = [mask for mask in blk_masks if mask != TURN]
    key_local = HEAD_WIDTH
    query_local = w_query.shape[1] // heads
    in_cols = query_local + 2 * key_local
    ff_rows, ff_cols = w_gate.shape
    ff_own = ff_cols // 2
    group_bits = bits_of(group, depth)

    wide_axes = [-depth - 2] + [-depth + i for i in range(depth - 1)]
    wide_bits = [cross] + group_bits[:-1]

    def to_wide(value):
        lead = value.shape[:-1]
        value = value.reshape(lead + (2, 2) + (2,) * (depth - 1) + (2 * shard,))
        value = flip(value, wide_bits, wide_axes)
        base = len(lead)
        order = [base] + [base + 2 + i for i in range(depth - 2, -1, -1)]
        order += [base + 1, base + depth + 1]
        return value.transpose(*range(base), *order).reshape(lead + (width,))

    def from_wide(value):
        lead = value.shape[:-1]
        value = value.reshape(lead + (2,) + (2,) * (depth - 1) + (2, 2 * shard))
        base = len(lead)
        order = [base, base + depth] + [base + 1 + i for i in range(depth - 2, -1, -1)]
        order += [base + depth + 1]
        value = value.transpose(*range(base), *order)
        return flip(value, wide_bits, wide_axes).reshape(lead + (width,))

    far_axes = [-depth - 1 + i for i in range(depth - 2)] + [-2]
    far_bits = group_bits[: depth - 2] + [low]

    def to_far(value):
        lead = value.shape[:-1]
        value = value.reshape(lead + (2,) * depth + (ff_rows,))
        value = flip(value, far_bits, far_axes)
        base = len(lead)
        order = [base + depth - 1] + [base + i for i in range(depth - 3, -1, -1)]
        order += [base + depth - 2, base + depth]
        return value.transpose(*range(base), *order).reshape(lead + (width,))

    def from_far(value):
        lead = value.shape[:-1]
        value = value.reshape(lead + (2,) * depth + (ff_rows,))
        base = len(lead)
        order = [base + 1 + i for i in range(depth - 3, -1, -1)]
        order += [base + depth - 1, base, base + depth]
        value = value.transpose(*range(base), *order)
        return flip(value, far_bits, far_axes).reshape(lead + (width,))

    def reversed_key(place, masks):
        bits = [(place >> (len(masks) - 1 - i)) & 1 for i in range(len(masks))]
        return sum(mask for bit, mask in zip(bits, masks[::-1]) if bit)

    def in_fold_order(have, masks):
        return [have[reversed_key(place, masks)] for place in range(1 << len(masks))]

    rows = jnp.arange(group_rows, dtype=jnp.int32)
    part_rows = 2 * token_rows
    local_row = cross * part_rows + (core ^ (rows % part_rows // token_rows)) * token_rows
    local_row = local_row + rows % token_rows
    pairs = [lax.dynamic_index_in_dim(pair_order, group ^ part, keepdims=False) for part in (0, 1)]
    first_span = jnp.where(rows < part_rows, pairs[0], pairs[1]) % per_seq
    span = jnp.where(local_row < BLOCK, first_span, 2 * per_seq - 1 - first_span)
    positions = span * BLOCK + local_row % BLOCK
    angles = positions.astype(F32)[:, None] * frequencies(HEAD_WIDTH)[None, :]
    cosine, sine = jnp.cos(angles), jnp.sin(angles)
    seg_halves = segments.reshape(-1, 2, BLOCK // 2)
    seg_row = jnp.where(core == 0, seg_halves, seg_halves[:, ::-1]).reshape(-1, BLOCK)
    seg_col = seg_row.T
    seg_flat = segments.reshape(-1)
    place = jnp.stack([group, cross]).astype(jnp.int32)

    flow = Flow()

    gains = jnp.zeros((2, heads * groups, shard), BF16)
    gains = lax.dynamic_update_slice(
        gains, jnp.stack([norm_in, norm_mid])[:, None], (0, head * groups + group, 0)
    )
    hops = [blk_masks[:1], blk_masks[1:-1], blk_masks[-1:], [None]]

    def hop():
        nonlocal gains, gain_sent
        if gain_sent is not None:
            gains = gains + gain_sent.value
            gain_sent = None
        if hops:
            *direct, last = hops.pop(0)
            for mask in direct:
                gains = gains + swap(gains, 0, mask)
            gain_sent = flow.send(gains, *((CROSS, 0) if last is None else (0, last)))

    gain_sent = None

    def column_half(weights, bit):
        return jnp.concatenate(
            [
                lax.dynamic_slice_in_dim(weight, bit * (weight.shape[1] // 2), weight.shape[1] // 2, 1)
                for weight in weights
            ],
            axis=1,
        )

    def core_half(value, bit):
        parts, first = [], 0
        for count in (2 * query_local, 2 * key_local, 2 * key_local, 2 * query_local):
            parts.append(
                lax.dynamic_slice_in_dim(value, first + bit * (count // 2), count // 2, 1)
            )
            first += count
        return jnp.concatenate(parts, axis=1)

    attention_weights = (w_query, key_weight, value_weight, w_out)

    def index(value, place):
        return lax.dynamic_index_in_dim(value, place, 0, keepdims=False)

    def halves(weight, bit):
        return lax.dynamic_slice_in_dim(weight, bit * ff_own, ff_own, 1)

    ffn_weights = (w_down, w_gate, w_up)
    bulk, block_rows = Bulk(far_masks, 3), 2 * ff_rows

    def send_turn(which):
        return flow.send(halves(ffn_weights[which], 1 - turn), 0, TURN)

    def end_turn(which, sent):
        own = pair(halves(ffn_weights[which], turn), sent.value, turn, 0)
        bulk.pieces[0, which] = [own.reshape(block_rows, -1)]

    def near(rows):
        return bulk.take(flow, 1, rows, block_rows)

    def high(rows):
        return any([bulk.take(flow, mask, rows, block_rows) for mask in far_masks[:-1]])

    own_half, other_half = (column_half(attention_weights, bit) for bit in (low, 1 - low))
    cols_core = flow.send(core_half(own_half, 1 - core), CORE, 0)
    cols_low = flow.send(core_half(other_half, core), 0, 1)
    cols_both = flow.send(core_half(other_half, 1 - core), CORE, 1)
    turned = send_turn(0)
    hop()
    flow.go()
    end_turn(0, turned)
    own_cols = pair(
        pair(core_half(own_half, core), cols_low.value, low, 0),
        pair(cols_core.value, cols_both.value, low, 0),
        core, 0,
    ).reshape(4 * shard, -1)
    spread_in = Spread(own_cols[:, :in_cols], wide_masks)
    chain_out = Chain(own_cols[:, in_cols:], wide_masks)
    spread_in.wave(flow, 0)
    token_x = to_wide(tokens)
    token_low = flow.send(token_x, 0, 1)
    hop()
    flow.go()
    spread_in.wave(flow, 1)
    high(ff_rows)
    hop()
    flow.go()
    for count in range(2, depth):
        if count > 2:
            flow.go()
        spread_in.wave(flow, count)
    token_core = flow.send(token_x, CORE, 0)
    token_both = flow.send(token_low.value, CORE, 0)
    turned = send_turn(1)
    hop()
    flow.go()
    token_group = jnp.concatenate(
        [token_x, token_core.value, token_low.value, token_both.value], axis=0
    ).astype(F32)
    end_turn(1, turned)
    hop()
    spread_in.settle()
    weight_in = jnp.concatenate(in_fold_order(spread_in.have, wide_masks), axis=0)
    gains = gains + swap(gains, CORE, 0)
    gains = gains.reshape(2, width).astype(F32)
    gain_in, gain_mid = to_wide(gains[:1]), gains[1:]
    turned = send_turn(2)
    near(ff_rows)
    chain_out.advance(flow)
    cot_far = to_far(cotangent)
    cot_x = flow.send(cot_far, CROSS, 0)
    flow.go()
    end_turn(2, turned)

    inv_group = lax.rsqrt(jnp.mean(token_group * token_group, axis=-1, keepdims=True) + EPS)
    input_low = (token_group * inv_group * gain_in).astype(BF16)
    lin = flow.join(jnp.dot(input_low, weight_in, preferred_element_type=F32))
    keys_values = jnp.concatenate(
        [
            rotate(lin[:, query_local : query_local + key_local], cosine, sine).astype(BF16),
            lin[:, query_local + key_local :].astype(BF16),
        ],
        axis=-1,
    )
    queries = rotate(lin[:, :query_local], cosine, sine).astype(BF16)
    queries = queries * jnp.asarray(HEAD_WIDTH ** (-0.5), BF16)

    spread_kv = Spread(keys_values, wide_masks)
    spread_kv.wave(flow, 0)
    near(ff_rows)
    near(ff_rows)
    flow.go()
    spread_kv.wave(flow, 1)
    near(block_rows)
    high(ff_rows)
    flow.go()
    for count in range(2, depth):
        if count > 2:
            flow.go()
        spread_kv.wave(flow, count)
    chain_out.advance(flow)
    high(ff_rows)
    near(ff_rows)
    near(ff_rows)
    flow.go()
    spread_kv.settle()
    kv_all = jnp.concatenate(in_fold_order(spread_kv.have, wide_masks), axis=0)
    while chain_out.masks:
        chain_out.advance(flow)
        if not chain_out.masks:
            high(ff_rows)
            near(ff_rows)
            near(ff_rows)
            cot_t = flow.send(cot_far, 0, TURN)
        flow.go()
    attention_low, attention_f, lse = attend(
        place, pair_order, seg_flat, queries, kv_all, seg_row, seg_col, per_seq
    )
    attention_low = flow.join(attention_low)
    chain_out.settle()
    weight_out = chain_out.blocks.reshape(width, -1)
    branch = lax.dot_general(attention_low, weight_out, COLS, preferred_element_type=F32)
    branch = row_major(branch.astype(BF16)).reshape(2, 2, token_rows, width)
    branch_across = add(branch[1, 0], swap(branch[1, 1], CORE, 0), BF16)
    branch_own = add(branch[0, 0], swap(branch[0, 1], CORE, 0), F32)
    branch_sent = flow.send(branch_across, 0, 1)
    cot_xt = flow.send(cot_t.value, CROSS, 0)
    high(ff_rows // 2)
    flow.go()
    branch = branch_own + branch_sent.value.astype(F32)

    tokens_f = tokens.astype(F32)
    middle = tokens_f + from_wide(branch)
    inv_mid = lax.rsqrt(jnp.mean(middle * middle, axis=-1, keepdims=True) + EPS)
    normed_mid = middle * inv_mid
    mid_low = to_far((normed_mid * gain_mid).astype(BF16))

    half = width // 2
    left, right = mid_low[:, :half], mid_low[:, half:]
    left_x = flow.send(left, CROSS, 0)
    right_t = flow.send(right, 0, TURN)
    near(ff_rows)
    high(ff_rows // 2)
    flow.go()
    left_t = flow.send(left, 0, TURN)
    right_x = flow.send(right, CROSS, 0)
    left_xt = flow.send(left_x.value, 0, TURN)
    right_xt = flow.send(right_t.value, CROSS, 0)
    high(ff_rows // 2)
    flow.go()
    def four_rows(parts, first_col):
        return [(part, (i * token_rows, first_col)) for i, part in enumerate(parts)]

    placed = four_rows([left, left_t.value, left_x.value, left_xt.value], 0)
    placed += four_rows([right, right_t.value, right_x.value, right_xt.value], half)
    mid_four = assemble([part for part, _ in placed], [where for _, where in placed])
    early = [near(block_rows) for _ in range(2)] + [high(block_rows)]
    flow.go()

    def eight(four):
        return stack_rows([four, swap(four, CORE, 0)])

    mid_group = eight(mid_four)
    cot_four = jnp.concatenate([cot_far, cot_t.value, cot_x.value, cot_xt.value], axis=0)
    grad_group = jnp.concatenate([cot_four, swap(cot_four, CORE, 0)], axis=0)

    def weight_of(which):
        have = bulk.parts(which)
        return jnp.concatenate(
            [part for parts in in_fold_order(have, far_masks) for part in parts], axis=0
        )

    while bulk.left(None, 0):
        near(block_rows), high(block_rows)
        flow.go()
    down = weight_of(0)
    grad_hidden = flow.join(jnp.dot(grad_group, down, preferred_element_type=F32))
    while bulk.left(1, 1):
        near(block_rows), high(block_rows)
        flow.go()
    while True:
        more = [near(block_rows) for _ in range(4)] + [high(block_rows)]
        flow.go()
        if not bulk.left(None, 2):
            break
    gate = weight_of(1)
    gate_lin = flow.join(jnp.dot(mid_group, gate, preferred_element_type=F32))
    up = weight_of(2)
    up_proj = jnp.dot(mid_group, up, preferred_element_type=F32)
    gate_sig = jax.nn.sigmoid(gate_lin)
    gate_silu = gate_lin * gate_sig
    hidden_act = (gate_silu * up_proj).astype(BF16)
    grad_gate_lin = (
        grad_hidden * up_proj * gate_sig * (1.0 + gate_lin * (1.0 - gate_sig))
    ).astype(BF16)
    grad_up_proj = (grad_hidden * gate_silu).astype(BF16)

    def ffn_fold(lhs, rhs):
        total = lax.dot_general(lhs, rhs, ROWS, preferred_element_type=F32)
        total = row_major(total.astype(BF16))
        return FfnFold(total, far_masks[::-1], turn)

    down_fold = ffn_fold(grad_group, hidden_act)
    ffn_folds = [down_fold]

    def near(rows):
        found = [
            (-block, i)
            for i, fold in enumerate(ffn_folds)
            for block, _ in fold.tasks[1][:1]
            if not fold.missing[block]
        ]
        return bool(found) and ffn_folds[min(found)[1]].take(flow, 1, rows)

    def high(rows):
        found = False
        for mask in far_masks[:-1][::-1]:
            found = any(fold.take(flow, mask, rows) for fold in ffn_folds) or found
        return found

    near(ff_rows)
    flow.go()
    mid_partial = lax.dot_general(
        grad_gate_lin, gate, COLS, preferred_element_type=F32
    ) + lax.dot_general(grad_up_proj, up, COLS, preferred_element_type=F32)
    mid_partial = flow.join(row_major(mid_partial.astype(BF16))).reshape(2, 2, 2, token_rows, width)
    four = add(mid_partial[0], swap(mid_partial[1], CORE, 0), BF16)
    left, right = four[..., :half], four[..., half:]
    left_sent = flow.send(left[:, 1], 0, TURN)
    right_sent = flow.send(right[1], CROSS, 0)
    near(ff_rows)
    flow.go()
    gate_fold = ffn_fold(mid_group, grad_gate_lin)
    ffn_partial = lax.dot_general(hidden_act, down, COLS, preferred_element_type=F32)
    ffn_partial = row_major(ffn_partial.astype(BF16)).reshape(2, 2, 2, token_rows, width)
    out_four = add(ffn_partial[0], swap(ffn_partial[1], CORE, 0), BF16)
    left = add(left[:, 0], left_sent.value, BF16)
    right = add(right[0], right_sent.value, BF16)
    left_sent = flow.send(left[1], CROSS, 0)
    right_sent = flow.send(right[1], 0, TURN)
    high(ff_rows // 2)
    flow.go()
    ffn_folds.append(gate_fold)
    grad_mid = jnp.concatenate(
        [add(left[0], left_sent.value, F32), add(right[0], right_sent.value, F32)], axis=-1
    )
    grad_mid = from_far(grad_mid)
    norm_mid_sum = jnp.sum(grad_mid * normed_mid, axis=0)
    grad_y = cotangent.astype(F32)
    grad_middle = grad_y + rms_back(grad_mid * gain_mid, normed_mid, inv_mid)
    grad_branch = to_wide(grad_middle.astype(BF16))
    branch_low = flow.send(grad_branch, 0, 1)
    high(ff_rows // 2)
    out_parts = [flow.send(out_four[1, 0], CROSS, 0)]
    flow.go()
    up_fold = ffn_fold(mid_group, grad_up_proj)
    ffn_folds.append(up_fold)
    branch_group = jnp.concatenate(
        [grad_branch, swap(grad_branch, CORE, 0), branch_low.value, swap(branch_low.value, CORE, 0)],
        axis=0,
    )
    grad_attention = jnp.dot(branch_group, weight_out, preferred_element_type=F32).astype(BF16)

    def weight_fold(lhs, rhs, extra=None):
        total = lax.dot_general(lhs, rhs, ROWS, preferred_element_type=F32)
        if extra is not None:
            column = jnp.broadcast_to(to_wide(extra[None])[0][:, None], (width, 128))
            total = jnp.concatenate([total, column], axis=1)
        total = row_major(total.astype(BF16))
        return Fold(total.reshape(groups, 4 * shard, -1), wide_masks[::-1])

    out_fold = weight_fold(branch_group, attention_low, norm_mid_sum)
    out_fold.advance(flow)
    near(block_rows)
    high(ff_rows)
    flow.go()
    grad_queries, grad_keys, grad_values = attend_back(
        place, pair_order, seg_flat, queries, kv_all, seg_row, seg_col,
        lse, attention_f, grad_attention, per_seq,
    )
    grad_queries = flow.join(grad_queries)
    grad_keys = flow.join(grad_keys)
    key_fold = Fold(grad_keys.reshape(groups, group_rows, -1), wide_masks[::-1])
    value_fold = Fold(grad_values.reshape(groups, group_rows, -1), wide_masks[::-1])
    key_fold.advance(flow)
    near(block_rows)
    high(ff_rows)
    flow.go()
    key_fold.advance(flow)
    value_fold.advance(flow)
    near(block_rows)
    high(ff_rows)
    flow.go()
    query_lin = rotate(grad_queries.astype(F32), cosine, -sine).astype(BF16)
    query_fold = weight_fold(input_low, query_lin)
    turns = [down_fold, gate_fold, up_fold]

    def take_turn():
        for fold in turns:
            if fold.take_turn(flow):
                turns.remove(fold)
                return

    while True:
        running = [fold.advance(flow) for fold in (key_fold, value_fold)]
        if not any(running):
            break
        query_fold.advance(flow)
        if all(running):
            high(ff_rows // 2)
            near(block_rows)
        else:
            near(ff_rows)
            high(ff_rows // 2)
            if len(out_parts) == 1:
                out_parts.append(flow.send(out_four[1, 1], CROSS, 0))
        flow.go()
    out_two = [add(out_four[0, i], sent.value, BF16) for i, sent in enumerate(out_parts)]
    out_sent = flow.send(out_two[1], 0, TURN)
    high(ff_rows // 2)
    flow.go()
    layer_out = (middle + from_far(add(out_two[0], out_sent.value, F32))).astype(BF16)
    keys_low, values_low = key_fold.blocks[0].astype(BF16), value_fold.blocks[0].astype(BF16)
    kv_lin = jnp.concatenate(
        [rotate(keys_low.astype(F32), cosine, -sine).astype(BF16), values_low], axis=-1
    )
    grad_lin = jnp.concatenate([query_lin, kv_lin], axis=-1)
    grad_in = lax.dot_general(grad_lin, weight_in, COLS, preferred_element_type=F32)
    grad_in = row_major(grad_in.astype(BF16)).reshape(2, 2, token_rows, width)
    in_across = add(grad_in[1, 0], swap(grad_in[1, 1], CORE, 0), BF16)
    in_own = add(grad_in[0, 0], swap(grad_in[0, 1], CORE, 0), F32)
    in_sent = flow.send(in_across, 0, 1)
    kv_fold = weight_fold(input_low, kv_lin)
    kv_fold.advance(flow)
    query_fold.advance(flow)
    out_fold.advance(flow)
    flow.go()
    kv_fold.advance(flow)
    query_fold.advance(flow)
    out_fold.advance(flow)
    near(ff_rows)
    flow.go()
    kv_fold.advance(flow)
    high(ff_rows)
    near(block_rows)
    take_turn()
    flow.go()
    while True:
        running = [fold.advance(flow) for fold in (kv_fold, query_fold, out_fold)]
        if not any(running):
            break
        near(block_rows), high(block_rows)
        flow.go()

    total = jnp.concatenate(
        [fold.blocks[0] for fold in (query_fold, kv_fold, out_fold)], axis=-1
    ).reshape(2, 2, shard, -1)

    def block_of(core_bit, low_bit):
        return index(index(total, core_bit), low_bit)

    sent_core = flow.send(block_of(1 - core, low).astype(BF16), CORE, 0)
    sent_low = flow.send(block_of(core, 1 - low).astype(BF16), 0, 1)
    sent_both = flow.send(block_of(1 - core, 1 - low).astype(BF16), CORE, 1)
    for fold in list(turns):
        if fold.take_turn(flow):
            turns.remove(fold)
    flow.go()
    while True:
        near(block_rows), high(block_rows)
        for fold in list(turns):
            if fold.take_turn(flow):
                turns.remove(fold)
        if not flow.batch:
            break
        flow.go()
    total = pair(
        pair(block_of(core, low), sent_core.value.astype(F32), core, 0),
        pair(sent_low.value.astype(F32), sent_both.value.astype(F32), core, 0),
        low, 0,
    ).reshape(4, shard, -1)
    scaled = in_own + in_sent.value.astype(F32)
    inv_in = inv_group[:token_rows]
    normed_in = tokens_f * inv_in
    grad_tokens = grad_middle + rms_back(from_wide(scaled * gain_in), normed_in, inv_in)

    def columns(first, count):
        return total[..., first : first + count].transpose(1, 0, 2).reshape(shard, -1)

    in_grads = [
        columns(0, query_local),
        columns(query_local, key_local),
        columns(query_local + key_local, key_local),
    ]
    grad_norm_in = sum(
        jnp.sum(grad * weight.astype(F32), axis=1)
        for grad, weight in zip(in_grads, attention_weights)
    ) / norm_in.astype(F32)
    grad_norm_mid = jnp.sum(total[..., in_cols + query_local], axis=0)
    return (
        layer_out,
        grad_tokens,
        grad_norm_in,
        *in_grads,
        columns(in_cols, query_local),
        grad_norm_mid,
        gate_fold.result(),
        up_fold.result(),
        down_fold.result(),
    )


def solution(mesh):
    rows = P(("blk", "head"), None)
    shards = P(("head", "blk"), None)
    vector = P(("head", "blk"))
    hidden = P("blk", "head")
    return jax.shard_map(
        local,
        mesh=mesh,
        in_specs=(
            rows, rows, P(), P(), vector, shards, shards, shards, shards, vector, hidden, hidden, hidden,
        ),
        out_specs=(
            rows, rows, vector, shards, shards, shards, shards, vector, hidden, hidden, hidden,
        ),
        check_vma=False,
    )
```

```python
import functools

import jax
import jax.numpy as jnp
from jax import lax
from jax.experimental import pallas as pl
from jax.experimental.layout import Layout, with_layout_constraint
from jax.experimental.pallas import tpu as pltpu
from jax.sharding import PartitionSpec as P

QUERY_HEAD_COUNT = 8
KEY_VALUE_HEADS = 4
HEAD_WIDTH = 256
SEQS = 2
BLOCK = 256

EPS = 1e-06
THETA = 1000042.0
NEGATIVE = -1e30
ROWS = (((0,), (0,)), ((), ()))
COLS = (((1,), (1,)), ((), ()))
BF16 = jnp.bfloat16
F32 = jnp.float32

CORE, CROSS, TURN = 1, 2, 2


def frequencies(head_size):
    return 1.0 / THETA ** (jnp.arange(0, head_size, 2, dtype=F32) / head_size)


def rotate(values, cosine, sine):
    half = HEAD_WIDTH // 2
    parts = []
    for first in range(0, values.shape[-1], HEAD_WIDTH):
        a = values[:, first : first + half]
        b = values[:, first + half : first + HEAD_WIDTH]
        parts += [a * cosine - b * sine, b * cosine + a * sine]
    return jnp.concatenate(parts, axis=-1)


def row_major(value):
    return with_layout_constraint(value, Layout(tuple(range(value.ndim))))


def swap(value, head_mask, blk_mask):
    groups = lax.axis_size("blk")
    count = lax.axis_size("head") * groups
    mask = head_mask * groups + blk_mask
    pairs = [(i, i ^ mask) for i in range(count)]
    return row_major(lax.ppermute(row_major(value), ("head", "blk"), pairs))


def masks_of(size):
    out, bit = [], size >> 1
    while bit:
        out.append(bit)
        bit >>= 1
    return out


def add(a, b, dtype):
    return (a.astype(F32) + b.astype(F32)).astype(dtype)


def pair(own, received, bit, axis):
    first = jnp.where(bit == 0, own, received)
    second = jnp.where(bit == 0, received, own)
    return jnp.stack([first, second], axis=axis)


def after(value, *others):
    return lax.optimization_barrier((value, *others))[0]


def assemble_kernel(places, *refs):
    parts, out, sems = refs[:-2], refs[-2], refs[-1]
    copies = [
        pltpu.make_async_copy(
            part,
            out.at[pl.ds(row, part.shape[0]), pl.ds(col, part.shape[1])],
            sems.at[i],
        )
        for i, (part, (row, col)) in enumerate(zip(parts, places))
    ]
    for copy in copies:
        copy.start()
    for copy in copies:
        copy.wait()


def assemble(parts, places):
    rows = max(row + part.shape[0] for part, (row, _) in zip(parts, places))
    cols = max(col + part.shape[1] for part, (_, col) in zip(parts, places))
    return pl.pallas_call(
        functools.partial(assemble_kernel, places),
        in_specs=[pl.BlockSpec(memory_space=pl.ANY)] * len(parts),
        out_specs=pl.BlockSpec(memory_space=pltpu.VMEM),
        out_shape=jax.ShapeDtypeStruct((rows, cols), parts[0].dtype),
        scratch_shapes=[pltpu.SemaphoreType.DMA((len(parts),))],
        cost_estimate=pl.CostEstimate(
            flops=0, bytes_accessed=4 * rows * cols, transcendentals=0
        ),
        name="assemble",
    )(*parts)


def stack_rows(parts):
    places, row = [], 0
    for part in parts:
        places.append((row, 0))
        row += part.shape[0]
    return assemble(parts, places)


class Sent:
    value = None


class Flow:
    def __init__(self):
        self.batch, self.before = [], []

    def send(self, value, head_mask, blk_mask):
        sent = Sent()
        self.batch.append((sent, value, head_mask, blk_mask))
        return sent

    def go(self):
        if not self.batch:
            return
        values = tuple(entry[1] for entry in self.batch)
        held = lax.optimization_barrier(values + tuple(sent.value for sent in self.before))
        arrived = [
            swap(value, head_mask, blk_mask)
            for (_, _, head_mask, blk_mask), value in zip(self.batch, held)
        ]
        for (sent, *_), value in zip(self.batch, lax.optimization_barrier(tuple(arrived))):
            sent.value = value
        self.before = [entry[0] for entry in self.batch]
        self.batch = []


    def join(self, value):
        value, *arrived = lax.optimization_barrier((value, *(sent.value for sent in self.before)))
        for sent, one in zip(self.before, arrived):
            sent.value = one
        return value


class Spread:
    def __init__(self, own, masks):
        self.masks, self.have = masks, {0: own}
        self.sents = {}

    def wave(self, flow, count):
        self.settle()
        for key in sorted(self.have):
            if bin(key).count("1") == count:
                for mask in self.masks:
                    if key == 0 or mask < (key & -key):
                        self.sents[key ^ mask] = flow.send(
                            self.have[key], CROSS if mask == 1 else 0, mask & ~1
                        )

    def settle(self):
        for key, sent in list(self.sents.items()):
            self.have[key] = sent.value
            del self.sents[key]


class Chain:
    def __init__(self, own, masks):
        self.blocks, self.masks, self.sent = own[None], list(masks), None

    def advance(self, flow):
        self.settle()
        if self.masks:
            mask = self.masks.pop(0)
            self.sent = flow.send(self.blocks, CROSS if mask == 1 else 0, mask & ~1)

    def settle(self):
        if self.sent is not None:
            self.blocks = jnp.concatenate([self.blocks, self.sent.value], axis=0)
            self.sent = None


class Fold:
    def __init__(self, blocks, masks):
        self.blocks, self.masks, self.sent = blocks, list(masks), None

    def advance(self, flow):
        if self.sent is not None:
            self.blocks = add(self.keep, self.sent.value, BF16 if self.masks else F32)
            self.sent = None
        if not self.masks:
            return False
        mask = self.masks.pop(0)
        half = self.blocks.shape[0] // 2
        self.keep = self.blocks[:half]
        self.sent = flow.send(self.blocks[half:], CROSS if mask == 1 else 0, mask & ~1)
        return True


class Bulk:
    def __init__(self, masks, count):
        self.masks = masks
        self.pieces, self.sents, self.done = {}, [], {}
        keys = [0]
        self.order = {}
        for mask in masks:
            self.order[mask] = [(key, which) for key in keys for which in range(count)]
            keys = keys + [key ^ mask for key in keys]

    def settle(self):
        waiting = []
        for name, sent in self.sents:
            if sent.value is None:
                waiting.append((name, sent))
            else:
                self.pieces.setdefault(name, []).append(sent.value)
        self.sents = waiting

    def take(self, flow, mask, rows, limit):
        self.limit = limit
        self.settle()
        for name in self.order[mask]:
            piece, offset, total = self.done.get((mask, name), (0, 0, 0))
            have = self.pieces.get(name, [])
            if total == limit or piece >= len(have):
                continue
            value = have[piece][offset : offset + rows]
            offset += value.shape[0]
            total += value.shape[0]
            if offset == have[piece].shape[0]:
                piece, offset = piece + 1, 0
            self.done[mask, name] = (piece, offset, total)
            self.sents.append(((name[0] ^ mask, name[1]), flow.send(value, 0, mask)))
            return True
        return False

    def left(self, mask, which):
        return any(
            self.done.get((m, name), (0, 0, 0))[2] < self.limit
            for m in self.masks
            if mask in (None, m)
            for name in self.order[m]
            if name[1] == which
        )

    def parts(self, which):
        self.settle()
        return {key: parts for (key, place), parts in self.pieces.items() if place == which}


class FfnFold:
    def __init__(self, total, masks, turn):
        count = 1 << len(masks)
        blocks = total.reshape(count, -1, total.shape[1])
        self.rows, self.half = blocks.shape[1], blocks.shape[1] // 2
        self.raw, self.halves = [blocks[i] for i in range(count)], {}
        self.turn, self.turning = turn, None
        self.missing = [[len(masks)] * 2] + [[0, 0] for _ in range(count - 1)]
        self.tasks, self.sent_rows = {}, {}
        for stage, mask in enumerate(masks):
            half = count >> (stage + 1)
            self.tasks[mask] = [(block, half) for block in range(2 * half - 1, half - 1, -1)]
            for block in range(half, 2 * half):
                self.missing[block] = [stage, stage]
        self.got, self.sents = {}, []

    def half_of(self, block, part):
        if (block, part) not in self.halves:
            first = part * self.half
            self.halves[block, part] = self.raw[block][first : first + self.half]
        return self.halves[block, part]

    def settle(self):
        waiting = []
        for block, half, first, sent in self.sents:
            if sent.value is None:
                waiting.append((block, half, first, sent))
                continue
            value = sent.value
            while value.shape[0]:
                part = first // self.half
                rows = min(value.shape[0], (part + 1) * self.half - first)
                parts = self.got.setdefault((block, part), [])
                parts.append(value[:rows])
                value, first = value[rows:], first + rows
                if sum(one.shape[0] for one in parts) == self.half:
                    into = block - half
                    self.missing[into][part] -= 1
                    received = jnp.concatenate(parts, axis=0) if len(parts) > 1 else parts[0]
                    self.halves[into, part] = add(
                        self.half_of(into, part), received, BF16 if into else F32
                    )
        self.sents = waiting

    def ready(self, block):
        if self.missing[block][0]:
            return 0
        return self.half if self.missing[block][1] else self.rows

    def next(self, mask):
        self.settle()
        for block, half in self.tasks[mask]:
            if self.ready(block) > self.sent_rows.get(block, 0):
                return block, half
        return None

    def take(self, flow, mask, rows):
        found = self.next(mask)
        if found is None:
            return False
        block, half = found
        first = self.sent_rows.get(block, 0)
        if (block, 0) in self.halves or (block, 1) in self.halves:
            part = first // self.half
            start = first - part * self.half
            piece = self.half_of(block, part)[start : start + rows]
        else:
            piece = self.raw[block][first : min(first + rows, self.ready(block))]
        self.sent_rows[block] = first + piece.shape[0]
        if self.sent_rows[block] == self.rows:
            self.tasks[mask].remove(found)
        self.sents.append((block, half, first, flow.send(piece, 0, mask)))
        return True

    def take_turn(self, flow):
        self.settle()
        if any(self.missing[0]) or self.turning is not None:
            return False
        parts = [self.half_of(0, part) for part in (0, 1)]
        self.mine = jnp.where(self.turn == 0, parts[0], parts[1])
        other = jnp.where(self.turn == 0, parts[1], parts[0])
        self.turning = flow.send(other.astype(BF16), 0, TURN)
        return True

    def result(self):
        rows, cols = self.mine.shape
        out = jnp.zeros((rows, 2 * cols), F32)
        out = lax.dynamic_update_slice(out, self.mine, (0, self.turn * cols))
        received = self.turning.value.astype(F32)
        return lax.dynamic_update_slice(out, received, (0, (1 - self.turn) * cols))


def span_of(pair_ref, group, late, per_seq):
    pair = pair_ref[group]
    seq = pair // per_seq
    first = pair - seq * per_seq
    return seq, jnp.where(late == 0, first, 2 * per_seq - 1 - first)


def tile_visible(place_ref, pair_ref, seg_ref, step, part, per_seq, seq_len):
    group, cross = place_ref[0], place_ref[1]
    piece, low = step // 2, step % 2
    key, count = 0, SEQS * per_seq
    bits = count.bit_length() - 1
    for bit in range(bits):
        key = key + ((piece >> bit) & 1) * (1 << (bits - 1 - bit))
    seq_k, span_k = span_of(
        pair_ref, group ^ (key - key % 2 + low), cross ^ (key % 2), per_seq
    )
    seq_q, span_q = span_of(pair_ref, group ^ part, cross, per_seq)
    last_k = seg_ref[seq_k * seq_len + span_k * BLOCK + BLOCK - 1]
    first_q = seg_ref[seq_q * seq_len + span_q * BLOCK]
    visible = (seq_k == seq_q) & (span_k <= span_q) & (last_k >= first_q)
    spans = 2 * per_seq
    return visible, seq_k * spans + span_k, seq_q * spans + span_q


def tile_mask(seg_row_ref, seg_col_ref, place_k, place_q):
    lanes = lax.broadcasted_iota(jnp.int32, seg_col_ref.shape, 1)
    column = jnp.sum(jnp.where(lanes == place_k, seg_col_ref[...], 0), axis=1, keepdims=True)
    row = seg_row_ref[pl.ds(place_q, 1), :]
    row = jnp.concatenate([row, row], axis=1)
    return column == row


def stack_heads(ref, part):
    rows = pl.ds(part * BLOCK, BLOCK)
    return jnp.concatenate([ref[rows, :HEAD_WIDTH], ref[rows, HEAD_WIDTH:]], axis=0)


def forward_kernel(
    per_seq, place_ref, pair_ref, seg_ref, q_ref, kv_ref, row_ref, col_ref,
    low_ref, out_ref, lse_ref, max_ref, sum_ref, acc_ref,
):
    step = pl.program_id(0)
    seq_len = 2 * per_seq * BLOCK

    @pl.when(step == 0)
    def _():
        max_ref[...] = jnp.full(max_ref.shape, NEGATIVE, F32)
        sum_ref[...] = jnp.zeros(sum_ref.shape, F32)
        acc_ref[...] = jnp.zeros(acc_ref.shape, F32)

    for part in range(2):
        visible, place_k, place_q = tile_visible(
            place_ref, pair_ref, seg_ref, step, part, per_seq, seq_len
        )

        @pl.when(visible)
        def _():
            keys = kv_ref[:, :HEAD_WIDTH]
            values = kv_ref[:, HEAD_WIDTH:]
            queries = stack_heads(q_ref, part)
            scores = lax.dot_general(keys, queries, COLS, preferred_element_type=F32)
            mask = tile_mask(row_ref, col_ref, place_k, place_q)
            scores = jnp.where(mask, scores, NEGATIVE)
            old_max = max_ref[part]
            new_max = jnp.maximum(old_max, jnp.max(scores, axis=0, keepdims=True))
            weights = jnp.where(mask, jnp.exp(scores - new_max), 0.0)
            factor = jnp.exp(old_max - new_max)
            max_ref[part] = new_max
            sum_ref[part] = sum_ref[part] * factor + jnp.sum(weights, axis=0, keepdims=True)
            acc_ref[part] = acc_ref[part] * factor + lax.dot_general(
                values, weights.astype(BF16), ROWS, preferred_element_type=F32
            )

    @pl.when(step == pl.num_programs(0) - 1)
    def _():
        for part in range(2):
            total = sum_ref[part]
            attended = (acc_ref[part] / total).T
            rows = pl.ds(part * BLOCK, BLOCK)
            for head in range(2):
                one = attended[head * BLOCK : (head + 1) * BLOCK]
                cols = pl.ds(head * HEAD_WIDTH, HEAD_WIDTH)
                out_ref[rows, cols] = one
                low_ref[rows, cols] = one.astype(BF16)
            lse_ref[part] = max_ref[part] + jnp.log(total)


def backward_kernel(
    per_seq, place_ref, pair_ref, seg_ref, q_ref, kv_ref, row_ref, col_ref, lse_ref, out_ref, do_ref,
    dq_ref, dk_ref, dv_ref, delta_ref, dq_acc, dk_acc, dv_acc,
):
    step = pl.program_id(0)
    seq_len = 2 * per_seq * BLOCK

    @pl.when(step == 0)
    def _():
        dq_acc[...] = jnp.zeros(dq_acc.shape, F32)
        for part in range(2):
            product = stack_heads(out_ref, part) * stack_heads(do_ref, part).astype(F32)
            delta_ref[part] = jnp.sum(product.T, axis=0, keepdims=True)

    dk_acc[...] = jnp.zeros(dk_acc.shape, F32)
    dv_acc[...] = jnp.zeros(dv_acc.shape, F32)
    for part in range(2):
        visible, place_k, place_q = tile_visible(
            place_ref, pair_ref, seg_ref, step, part, per_seq, seq_len
        )

        @pl.when(visible)
        def _():
            keys = kv_ref[:, :HEAD_WIDTH]
            values = kv_ref[:, HEAD_WIDTH:]
            queries = stack_heads(q_ref, part)
            grads = stack_heads(do_ref, part)
            scores = lax.dot_general(keys, queries, COLS, preferred_element_type=F32)
            mask = tile_mask(row_ref, col_ref, place_k, place_q)
            probs = jnp.where(mask, jnp.exp(scores - lse_ref[part]), 0.0)
            grad_probs = lax.dot_general(values, grads, COLS, preferred_element_type=F32)
            grad_scores = (probs * (grad_probs - delta_ref[part])).astype(BF16)
            dv_acc[...] += jnp.dot(probs.astype(BF16), grads, preferred_element_type=F32)
            dk_acc[...] += jnp.dot(grad_scores, queries, preferred_element_type=F32)
            dq_acc[part] += lax.dot_general(
                grad_scores, keys, ROWS, preferred_element_type=F32
            )

    dk_ref[...] = dk_acc[...].astype(BF16)
    dv_ref[...] = dv_acc[...].astype(BF16)

    @pl.when(step == pl.num_programs(0) - 1)
    def _():
        for part in range(2):
            rows = pl.ds(part * BLOCK, BLOCK)
            for head in range(2):
                one = dq_acc[part, head * BLOCK : (head + 1) * BLOCK]
                dq_ref[rows, pl.ds(head * HEAD_WIDTH, HEAD_WIDTH)] = (
                    one * HEAD_WIDTH ** (-0.5)
                ).astype(BF16)


def whole(shape):
    return pl.BlockSpec(shape, lambda step, *refs: (0,) * len(shape))


def attend(place, pair_order, seg_flat, queries, keys_values, seg_row, seg_col, per_seq):
    steps = keys_values.shape[0] // BLOCK
    rows, width = queries.shape
    return pl.pallas_call(
        functools.partial(forward_kernel, per_seq),
        grid_spec=pltpu.PrefetchScalarGridSpec(
            num_scalar_prefetch=3,
            grid=(steps,),
            in_specs=[
                whole(queries.shape),
                pl.BlockSpec((BLOCK, 2 * HEAD_WIDTH), lambda step, *refs: (step, 0)),
                whole(seg_row.shape),
                whole(seg_col.shape),
            ],
            out_specs=[whole((rows, width)), whole((rows, width)), whole((2, 1, rows))],
            scratch_shapes=[
                pltpu.VMEM((2, 1, rows), F32),
                pltpu.VMEM((2, 1, rows), F32),
                pltpu.VMEM((2, HEAD_WIDTH, rows), F32),
            ],
        ),
        out_shape=[
            jax.ShapeDtypeStruct((rows, width), BF16),
            jax.ShapeDtypeStruct((rows, width), F32),
            jax.ShapeDtypeStruct((2, 1, rows), F32),
        ],
        compiler_params=pltpu.CompilerParams(dimension_semantics=("arbitrary",)),
        cost_estimate=pl.CostEstimate(
            flops=6_000_000_000, bytes_accessed=6_000_000, transcendentals=2_000_000
        ),
        name="attend",
    )(place, pair_order, seg_flat, queries, keys_values, seg_row, seg_col)


def attend_back(
    place, pair_order, seg_flat, queries, keys_values, seg_row, seg_col, lse, out, grads, per_seq
):
    steps = keys_values.shape[0] // BLOCK
    rows, width = queries.shape
    return pl.pallas_call(
        functools.partial(backward_kernel, per_seq),
        grid_spec=pltpu.PrefetchScalarGridSpec(
            num_scalar_prefetch=3,
            grid=(steps,),
            in_specs=[
                whole(queries.shape),
                pl.BlockSpec((BLOCK, 2 * HEAD_WIDTH), lambda step, *refs: (step, 0)),
                whole(seg_row.shape),
                whole(seg_col.shape),
                whole(lse.shape),
                whole(out.shape),
                whole(grads.shape),
            ],
            out_specs=[
                whole((rows, width)),
                pl.BlockSpec((BLOCK, HEAD_WIDTH), lambda step, *refs: (step, 0)),
                pl.BlockSpec((BLOCK, HEAD_WIDTH), lambda step, *refs: (step, 0)),
            ],
            scratch_shapes=[
                pltpu.VMEM((2, 1, rows), F32),
                pltpu.VMEM((2, rows, HEAD_WIDTH), F32),
                pltpu.VMEM((BLOCK, HEAD_WIDTH), F32),
                pltpu.VMEM((BLOCK, HEAD_WIDTH), F32),
            ],
        ),
        out_shape=[
            jax.ShapeDtypeStruct((rows, width), BF16),
            jax.ShapeDtypeStruct((keys_values.shape[0], HEAD_WIDTH), BF16),
            jax.ShapeDtypeStruct((keys_values.shape[0], HEAD_WIDTH), BF16),
        ],
        compiler_params=pltpu.CompilerParams(dimension_semantics=("arbitrary",)),
        cost_estimate=pl.CostEstimate(
            flops=16_000_000_000, bytes_accessed=12_000_000, transcendentals=2_000_000
        ),
        name="attend_back",
    )(place, pair_order, seg_flat, queries, keys_values, seg_row, seg_col, lse, out, grads)


def rms_back(scaled, normed, inv_rms):
    return inv_rms * (scaled - normed * jnp.mean(scaled * normed, axis=-1, keepdims=True))


def bits_of(number, count):
    return [(number >> (count - 1 - i)) & 1 for i in range(count)]


def flip(value, bits, axes):
    for bit, axis in zip(bits, axes):
        value = jnp.where(bit == 0, value, jnp.flip(value, axis))
    return value


def local(
    tokens,
    cotangent,
    segments,
    pair_order,
    norm_in,
    w_query,
    key_weight,
    value_weight,
    w_out,
    norm_mid,
    w_gate,
    w_up,
    w_down,
):
    heads = lax.axis_size("head")
    groups = lax.axis_size("blk")
    group = lax.axis_index("blk")
    head = lax.axis_index("head")
    cross, core = head // 2, head % 2
    turn = (group // TURN) % 2
    low = group % 2
    depth = groups.bit_length() - 1
    token_rows, width = tokens.shape
    group_rows = token_rows * heads
    per_seq = groups // SEQS
    shard = norm_in.shape[0]
    blk_masks = masks_of(groups)
    wide_masks = blk_masks[:-1] + [1]
    far_masks = [mask for mask in blk_masks if mask != TURN]
    key_local = HEAD_WIDTH
    query_local = w_query.shape[1] // heads
    in_cols = query_local + 2 * key_local
    ff_rows, ff_cols = w_gate.shape
    ff_own = ff_cols // 2
    group_bits = bits_of(group, depth)

    wide_axes = [-depth - 2] + [-depth + i for i in range(depth - 1)]
    wide_bits = [cross] + group_bits[:-1]

    def to_wide(value):
        lead = value.shape[:-1]
        value = value.reshape(lead + (2, 2) + (2,) * (depth - 1) + (2 * shard,))
        value = flip(value, wide_bits, wide_axes)
        base = len(lead)
        order = [base] + [base + 2 + i for i in range(depth - 2, -1, -1)]
        order += [base + 1, base + depth + 1]
        return value.transpose(*range(base), *order).reshape(lead + (width,))

    def from_wide(value):
        lead = value.shape[:-1]
        value = value.reshape(lead + (2,) + (2,) * (depth - 1) + (2, 2 * shard))
        base = len(lead)
        order = [base, base + depth] + [base + 1 + i for i in range(depth - 2, -1, -1)]
        order += [base + depth + 1]
        value = value.transpose(*range(base), *order)
        return flip(value, wide_bits, wide_axes).reshape(lead + (width,))

    far_axes = [-depth - 1 + i for i in range(depth - 2)] + [-2]
    far_bits = group_bits[: depth - 2] + [low]

    def to_far(value):
        lead = value.shape[:-1]
        value = value.reshape(lead + (2,) * depth + (ff_rows,))
        value = flip(value, far_bits, far_axes)
        base = len(lead)
        order = [base + depth - 1] + [base + i for i in range(depth - 3, -1, -1)]
        order += [base + depth - 2, base + depth]
        return value.transpose(*range(base), *order).reshape(lead + (width,))

    def from_far(value):
        lead = value.shape[:-1]
        value = value.reshape(lead + (2,) * depth + (ff_rows,))
        base = len(lead)
        order = [base + 1 + i for i in range(depth - 3, -1, -1)]
        order += [base + depth - 1, base, base + depth]
        value = value.transpose(*range(base), *order)
        return flip(value, far_bits, far_axes).reshape(lead + (width,))

    def reversed_key(place, masks):
        bits = [(place >> (len(masks) - 1 - i)) & 1 for i in range(len(masks))]
        return sum(mask for bit, mask in zip(bits, masks[::-1]) if bit)

    def in_fold_order(have, masks):
        return [have[reversed_key(place, masks)] for place in range(1 << len(masks))]

    rows = jnp.arange(group_rows, dtype=jnp.int32)
    part_rows = 2 * token_rows
    local_row = cross * part_rows + (core ^ (rows % part_rows // token_rows)) * token_rows
    local_row = local_row + rows % token_rows
    pairs = [lax.dynamic_index_in_dim(pair_order, group ^ part, keepdims=False) for part in (0, 1)]
    first_span = jnp.where(rows < part_rows, pairs[0], pairs[1]) % per_seq
    span = jnp.where(local_row < BLOCK, first_span, 2 * per_seq - 1 - first_span)
    positions = span * BLOCK + local_row % BLOCK
    angles = positions.astype(F32)[:, None] * frequencies(HEAD_WIDTH)[None, :]
    cosine, sine = jnp.cos(angles), jnp.sin(angles)
    seg_halves = segments.reshape(-1, 2, BLOCK // 2)
    seg_row = jnp.where(core == 0, seg_halves, seg_halves[:, ::-1]).reshape(-1, BLOCK)
    seg_col = seg_row.T
    seg_flat = segments.reshape(-1)
    place = jnp.stack([group, cross]).astype(jnp.int32)

    flow = Flow()

    gains = jnp.zeros((2, heads * groups, shard), BF16)
    gains = lax.dynamic_update_slice(
        gains, jnp.stack([norm_in, norm_mid])[:, None], (0, head * groups + group, 0)
    )
    hops = [blk_masks[:1], blk_masks[1:-1], blk_masks[-1:], [None]]

    def hop():
        nonlocal gains, gain_sent
        if gain_sent is not None:
            gains = gains + gain_sent.value
            gain_sent = None
        if hops:
            *direct, last = hops.pop(0)
            for mask in direct:
                gains = gains + swap(gains, 0, mask)
            gain_sent = flow.send(gains, *((CROSS, 0) if last is None else (0, last)))

    gain_sent = None

    def column_half(weights, bit):
        return jnp.concatenate(
            [
                lax.dynamic_slice_in_dim(weight, bit * (weight.shape[1] // 2), weight.shape[1] // 2, 1)
                for weight in weights
            ],
            axis=1,
        )

    def core_half(value, bit):
        parts, first = [], 0
        for count in (2 * query_local, 2 * key_local, 2 * key_local, 2 * query_local):
            parts.append(
                lax.dynamic_slice_in_dim(value, first + bit * (count // 2), count // 2, 1)
            )
            first += count
        return jnp.concatenate(parts, axis=1)

    attention_weights = (w_query, key_weight, value_weight, w_out)

    def index(value, place):
        return lax.dynamic_index_in_dim(value, place, 0, keepdims=False)

    def halves(weight, bit):
        return lax.dynamic_slice_in_dim(weight, bit * ff_own, ff_own, 1)

    ffn_weights = (w_down, w_gate, w_up)
    bulk, block_rows = Bulk(far_masks, 3), 2 * ff_rows

    def send_turn(which):
        return flow.send(halves(ffn_weights[which], 1 - turn), 0, TURN)

    def end_turn(which, sent):
        own = pair(halves(ffn_weights[which], turn), sent.value, turn, 0)
        bulk.pieces[0, which] = [own.reshape(block_rows, -1)]

    def near(rows):
        return bulk.take(flow, 1, rows, block_rows)

    def high(rows):
        return any([bulk.take(flow, mask, rows, block_rows) for mask in far_masks[:-1]])

    own_half, other_half = (column_half(attention_weights, bit) for bit in (low, 1 - low))
    cols_core = flow.send(core_half(own_half, 1 - core), CORE, 0)
    cols_low = flow.send(core_half(other_half, core), 0, 1)
    cols_both = flow.send(core_half(other_half, 1 - core), CORE, 1)
    turned = send_turn(0)
    hop()
    flow.go()
    end_turn(0, turned)
    own_cols = pair(
        pair(core_half(own_half, core), cols_low.value, low, 0),
        pair(cols_core.value, cols_both.value, low, 0),
        core, 0,
    ).reshape(4 * shard, -1)
    spread_in = Spread(own_cols[:, :in_cols], wide_masks)
    chain_out = Chain(own_cols[:, in_cols:], wide_masks)
    spread_in.wave(flow, 0)
    token_x = to_wide(tokens)
    token_low = flow.send(token_x, 0, 1)
    hop()
    flow.go()
    spread_in.wave(flow, 1)
    high(ff_rows)
    hop()
    flow.go()
    for count in range(2, depth):
        if count > 2:
            flow.go()
        spread_in.wave(flow, count)
    token_core = flow.send(token_x, CORE, 0)
    token_both = flow.send(token_low.value, CORE, 0)
    turned = send_turn(1)
    hop()
    flow.go()
    token_group = jnp.concatenate(
        [token_x, token_core.value, token_low.value, token_both.value], axis=0
    ).astype(F32)
    end_turn(1, turned)
    hop()
    spread_in.settle()
    weight_in = jnp.concatenate(in_fold_order(spread_in.have, wide_masks), axis=0)
    gains = gains + swap(gains, CORE, 0)
    gains = gains.reshape(2, width).astype(F32)
    gain_in, gain_mid = to_wide(gains[:1]), gains[1:]
    turned = send_turn(2)
    near(ff_rows)
    chain_out.advance(flow)
    cot_far = to_far(cotangent)
    cot_x = flow.send(cot_far, CROSS, 0)
    flow.go()
    end_turn(2, turned)

    inv_group = lax.rsqrt(jnp.mean(token_group * token_group, axis=-1, keepdims=True) + EPS)
    input_low = (token_group * inv_group * gain_in).astype(BF16)
    lin = flow.join(jnp.dot(input_low, weight_in, preferred_element_type=F32))
    keys_values = jnp.concatenate(
        [
            rotate(lin[:, query_local : query_local + key_local], cosine, sine).astype(BF16),
            lin[:, query_local + key_local :].astype(BF16),
        ],
        axis=-1,
    )
    queries = rotate(lin[:, :query_local], cosine, sine).astype(BF16)
    queries = queries * jnp.asarray(HEAD_WIDTH ** (-0.5), BF16)

    spread_kv = Spread(keys_values, wide_masks)
    spread_kv.wave(flow, 0)
    near(ff_rows)
    near(ff_rows)
    flow.go()
    spread_kv.wave(flow, 1)
    near(block_rows)
    high(ff_rows)
    flow.go()
    for count in range(2, depth):
        if count > 2:
            flow.go()
        spread_kv.wave(flow, count)
    chain_out.advance(flow)
    high(ff_rows)
    near(ff_rows)
    near(ff_rows)
    flow.go()
    spread_kv.settle()
    kv_all = jnp.concatenate(in_fold_order(spread_kv.have, wide_masks), axis=0)
    while chain_out.masks:
        chain_out.advance(flow)
        if not chain_out.masks:
            high(ff_rows)
            near(ff_rows)
            near(ff_rows)
            cot_t = flow.send(cot_far, 0, TURN)
        flow.go()
    attention_low, attention_f, lse = attend(
        place, pair_order, seg_flat, queries, kv_all, seg_row, seg_col, per_seq
    )
    attention_low = flow.join(attention_low)
    chain_out.settle()
    weight_out = chain_out.blocks.reshape(width, -1)
    branch = lax.dot_general(attention_low, weight_out, COLS, preferred_element_type=F32)
    branch = row_major(branch.astype(BF16)).reshape(2, 2, token_rows, width)
    branch_across = add(branch[1, 0], swap(branch[1, 1], CORE, 0), BF16)
    branch_own = add(branch[0, 0], swap(branch[0, 1], CORE, 0), F32)
    branch_sent = flow.send(branch_across, 0, 1)
    cot_xt = flow.send(cot_t.value, CROSS, 0)
    high(ff_rows // 2)
    flow.go()
    branch = branch_own + branch_sent.value.astype(F32)

    tokens_f = tokens.astype(F32)
    middle = tokens_f + from_wide(branch)
    inv_mid = lax.rsqrt(jnp.mean(middle * middle, axis=-1, keepdims=True) + EPS)
    normed_mid = middle * inv_mid
    mid_low = to_far((normed_mid * gain_mid).astype(BF16))

    half = width // 2
    left, right = mid_low[:, :half], mid_low[:, half:]
    left_x = flow.send(left, CROSS, 0)
    right_t = flow.send(right, 0, TURN)
    near(ff_rows)
    high(ff_rows // 2)
    flow.go()
    left_t = flow.send(left, 0, TURN)
    right_x = flow.send(right, CROSS, 0)
    left_xt = flow.send(left_x.value, 0, TURN)
    right_xt = flow.send(right_t.value, CROSS, 0)
    high(ff_rows // 2)
    flow.go()
    def four_rows(parts, first_col):
        return [(part, (i * token_rows, first_col)) for i, part in enumerate(parts)]

    placed = four_rows([left, left_t.value, left_x.value, left_xt.value], 0)
    placed += four_rows([right, right_t.value, right_x.value, right_xt.value], half)
    mid_four = assemble([part for part, _ in placed], [where for _, where in placed])
    def eight(four):
        return stack_rows([four, swap(four, CORE, 0)])

    def weight_of(which):
        have = bulk.parts(which)
        return jnp.concatenate(
            [part for parts in in_fold_order(have, far_masks) for part in parts], axis=0
        )

    cot_four = jnp.concatenate([cot_far, cot_t.value, cot_x.value, cot_xt.value], axis=0)
    grad_group = jnp.concatenate([cot_four, swap(cot_four, CORE, 0)], axis=0)
    while bulk.left(None, 0):
        near(block_rows), high(block_rows)
        flow.go()
    down = weight_of(0)
    near(block_rows), near(block_rows), high(block_rows)
    flow.go()
    mid_group = eight(mid_four)
    grad_hidden = flow.join(jnp.dot(grad_group, down, preferred_element_type=F32))
    while bulk.left(None, 1):
        near(block_rows), near(block_rows), high(block_rows)
        flow.go()
    gate = weight_of(1)
    while bulk.left(None, 2):
        for _ in range(4):
            near(block_rows)
        high(block_rows)
        flow.go()
    gate_lin = flow.join(jnp.dot(mid_group, gate, preferred_element_type=F32))
    up = weight_of(2)
    up_proj = jnp.dot(mid_group, up, preferred_element_type=F32)
    gate_sig = jax.nn.sigmoid(gate_lin)
    gate_silu = gate_lin * gate_sig
    hidden_act = (gate_silu * up_proj).astype(BF16)
    grad_gate_lin = (
        grad_hidden * up_proj * gate_sig * (1.0 + gate_lin * (1.0 - gate_sig))
    ).astype(BF16)
    grad_up_proj = (grad_hidden * gate_silu).astype(BF16)

    def ffn_fold(lhs, rhs):
        total = lax.dot_general(lhs, rhs, ROWS, preferred_element_type=F32)
        total = row_major(total.astype(BF16))
        return FfnFold(total, far_masks[::-1], turn)

    ffn_folds = []

    def near(rows):
        found = [(fold.next(1), i) for i, fold in enumerate(ffn_folds)]
        found = [(-block[0], i) for block, i in found if block is not None]
        return bool(found) and ffn_folds[min(found)[1]].take(flow, 1, rows)

    def high(rows):
        found = False
        for mask in far_masks[:-1][::-1]:
            found = any(fold.take(flow, mask, rows) for fold in ffn_folds) or found
        return found

    mid_partial = lax.dot_general(
        grad_gate_lin, gate, COLS, preferred_element_type=F32
    ) + lax.dot_general(grad_up_proj, up, COLS, preferred_element_type=F32)
    mid_partial = row_major(mid_partial.astype(BF16))
    down_fold = ffn_fold(grad_group, after(hidden_act, mid_partial))
    ffn_folds.append(down_fold)
    mid_partial = mid_partial.reshape(2, 2, 2, token_rows, width)
    four = add(mid_partial[0], swap(mid_partial[1], CORE, 0), BF16)
    left, right = four[..., :half], four[..., half:]
    left_sent = flow.send(left[:, 1], 0, TURN)
    right_sent = flow.send(right[1], CROSS, 0)
    near(ff_rows)
    flow.go()
    gate_fold = ffn_fold(mid_group, after(grad_gate_lin, four))
    first_step = left_sent.value
    ffn_partial = lax.dot_general(
        after(hidden_act, four), down, COLS, preferred_element_type=F32
    )
    ffn_partial = row_major(ffn_partial.astype(BF16)).reshape(2, 2, 2, token_rows, width)
    out_four = add(ffn_partial[0], swap(ffn_partial[1], CORE, 0), BF16)
    left = add(left[:, 0], left_sent.value, BF16)
    right = add(right[0], right_sent.value, BF16)
    left_sent = flow.send(left[1], CROSS, 0)
    right_sent = flow.send(right[1], 0, TURN)
    near(ff_rows)
    high(ff_rows // 2)
    flow.go()
    ffn_folds.append(gate_fold)
    grad_mid = jnp.concatenate(
        [add(left[0], left_sent.value, F32), add(right[0], right_sent.value, F32)], axis=-1
    )
    grad_mid = from_far(grad_mid)
    norm_mid_sum = jnp.sum(grad_mid * normed_mid, axis=0)
    grad_y = cotangent.astype(F32)
    grad_middle = grad_y + rms_back(grad_mid * gain_mid, normed_mid, inv_mid)
    grad_branch = to_wide(grad_middle.astype(BF16))
    branch_low = flow.send(grad_branch, 0, 1)
    high(ff_rows // 2)
    out_parts = [flow.send(out_four[1, 0], CROSS, 0)]
    flow.go()
    up_fold = ffn_fold(mid_group, after(grad_up_proj, first_step))
    ffn_folds.append(up_fold)
    branch_group = jnp.concatenate(
        [grad_branch, swap(grad_branch, CORE, 0), branch_low.value, swap(branch_low.value, CORE, 0)],
        axis=0,
    )
    grad_attention = jnp.dot(branch_group, weight_out, preferred_element_type=F32).astype(BF16)

    def weight_fold(lhs, rhs, extra=None):
        total = lax.dot_general(lhs, rhs, ROWS, preferred_element_type=F32)
        if extra is not None:
            column = jnp.broadcast_to(to_wide(extra[None])[0][:, None], (width, 128))
            total = jnp.concatenate([total, column], axis=1)
        total = row_major(total.astype(BF16))
        return Fold(total.reshape(groups, 4 * shard, -1), wide_masks[::-1])

    out_fold = weight_fold(branch_group, attention_low, norm_mid_sum)
    out_fold.advance(flow)
    near(block_rows)
    high(ff_rows)
    flow.go()
    grad_queries, grad_keys, grad_values = attend_back(
        place, pair_order, seg_flat, queries, kv_all, seg_row, seg_col,
        lse, attention_f, grad_attention, per_seq,
    )
    grad_queries = flow.join(grad_queries)
    grad_keys = flow.join(grad_keys)
    key_fold = Fold(grad_keys.reshape(groups, group_rows, -1), wide_masks[::-1])
    value_fold = Fold(grad_values.reshape(groups, group_rows, -1), wide_masks[::-1])
    key_fold.advance(flow)
    near(block_rows)
    high(ff_rows)
    flow.go()
    key_fold.advance(flow)
    value_fold.advance(flow)
    near(block_rows)
    high(ff_rows)
    flow.go()
    query_lin = rotate(grad_queries.astype(F32), cosine, -sine).astype(BF16)
    query_fold = weight_fold(input_low, query_lin)
    turns = [down_fold, gate_fold, up_fold]

    def take_turn():
        for fold in turns:
            if fold.take_turn(flow):
                turns.remove(fold)
                return

    while True:
        running = [fold.advance(flow) for fold in (key_fold, value_fold)]
        if not any(running):
            break
        query_fold.advance(flow)
        if all(running):
            high(ff_rows // 2)
            near(block_rows)
        else:
            near(ff_rows)
            high(ff_rows // 2)
            if len(out_parts) == 1:
                out_parts.append(flow.send(out_four[1, 1], CROSS, 0))
        flow.go()
    out_two = [add(out_four[0, i], sent.value, BF16) for i, sent in enumerate(out_parts)]
    out_sent = flow.send(out_two[1], 0, TURN)
    high(ff_rows // 2)
    flow.go()
    layer_out = (middle + from_far(add(out_two[0], out_sent.value, F32))).astype(BF16)
    keys_low, values_low = key_fold.blocks[0].astype(BF16), value_fold.blocks[0].astype(BF16)
    kv_lin = jnp.concatenate(
        [rotate(keys_low.astype(F32), cosine, -sine).astype(BF16), values_low], axis=-1
    )
    grad_lin = jnp.concatenate([query_lin, kv_lin], axis=-1)
    grad_in = lax.dot_general(grad_lin, weight_in, COLS, preferred_element_type=F32)
    grad_in = row_major(grad_in.astype(BF16)).reshape(2, 2, token_rows, width)
    in_across = add(grad_in[1, 0], swap(grad_in[1, 1], CORE, 0), BF16)
    in_own = add(grad_in[0, 0], swap(grad_in[0, 1], CORE, 0), F32)
    in_sent = flow.send(in_across, 0, 1)
    kv_fold = weight_fold(input_low, kv_lin)
    kv_fold.advance(flow)
    query_fold.advance(flow)
    out_fold.advance(flow)
    flow.go()
    kv_fold.advance(flow)
    query_fold.advance(flow)
    out_fold.advance(flow)
    near(ff_rows)
    flow.go()
    kv_fold.advance(flow)
    high(ff_rows)
    near(block_rows)
    take_turn()
    flow.go()
    while True:
        running = [fold.advance(flow) for fold in (kv_fold, query_fold, out_fold)]
        if not any(running):
            break
        near(block_rows), high(block_rows)
        flow.go()

    total = jnp.concatenate(
        [fold.blocks[0] for fold in (query_fold, kv_fold, out_fold)], axis=-1
    ).reshape(2, 2, shard, -1)

    def block_of(core_bit, low_bit):
        return index(index(total, core_bit), low_bit)

    sent_core = flow.send(block_of(1 - core, low).astype(BF16), CORE, 0)
    sent_low = flow.send(block_of(core, 1 - low).astype(BF16), 0, 1)
    sent_both = flow.send(block_of(1 - core, 1 - low).astype(BF16), CORE, 1)
    for fold in list(turns):
        if fold.take_turn(flow):
            turns.remove(fold)
    flow.go()
    while True:
        near(block_rows), high(block_rows)
        for fold in list(turns):
            if fold.take_turn(flow):
                turns.remove(fold)
        if not flow.batch:
            break
        flow.go()
    total = pair(
        pair(block_of(core, low), sent_core.value.astype(F32), core, 0),
        pair(sent_low.value.astype(F32), sent_both.value.astype(F32), core, 0),
        low, 0,
    ).reshape(4, shard, -1)
    scaled = in_own + in_sent.value.astype(F32)
    inv_in = inv_group[:token_rows]
    normed_in = tokens_f * inv_in
    grad_tokens = grad_middle + rms_back(from_wide(scaled * gain_in), normed_in, inv_in)

    def columns(first, count):
        return total[..., first : first + count].transpose(1, 0, 2).reshape(shard, -1)

    in_grads = [
        columns(0, query_local),
        columns(query_local, key_local),
        columns(query_local + key_local, key_local),
    ]
    grad_norm_in = sum(
        jnp.sum(grad * weight.astype(F32), axis=1)
        for grad, weight in zip(in_grads, attention_weights)
    ) / norm_in.astype(F32)
    grad_norm_mid = jnp.sum(total[..., in_cols + query_local], axis=0)
    return (
        layer_out,
        grad_tokens,
        grad_norm_in,
        *in_grads,
        columns(in_cols, query_local),
        grad_norm_mid,
        gate_fold.result(),
        up_fold.result(),
        down_fold.result(),
    )


def solution(mesh):
    rows = P(("blk", "head"), None)
    shards = P(("head", "blk"), None)
    vector = P(("head", "blk"))
    hidden = P("blk", "head")
    return jax.shard_map(
        local,
        mesh=mesh,
        in_specs=(
            rows, rows, P(), P(), vector, shards, shards, shards, shards, vector, hidden, hidden, hidden,
        ),
        out_specs=(
            rows, rows, vector, shards, shards, shards, shards, vector, hidden, hidden, hidden,
        ),
        check_vma=False,
    )
```

```python
import functools

import jax
import jax.numpy as jnp
from jax import lax
from jax.experimental import pallas as pl
from jax.experimental.layout import Layout, with_layout_constraint
from jax.experimental.pallas import tpu as pltpu
from jax.sharding import PartitionSpec as P

QUERY_HEAD_COUNT = 8
KEY_VALUE_HEADS = 4
HEAD_WIDTH = 256
SEQS = 2
BLOCK = 256

EPS = 1e-06
THETA = 1000042.0
NEGATIVE = -1e30
ROWS = (((0,), (0,)), ((), ()))
COLS = (((1,), (1,)), ((), ()))
BF16 = jnp.bfloat16
F32 = jnp.float32

CORE, CROSS, TURN = 1, 2, 2


def frequencies(head_size):
    return 1.0 / THETA ** (jnp.arange(0, head_size, 2, dtype=F32) / head_size)


def rotate(values, cosine, sine):
    half = HEAD_WIDTH // 2
    parts = []
    for first in range(0, values.shape[-1], HEAD_WIDTH):
        a = values[:, first : first + half]
        b = values[:, first + half : first + HEAD_WIDTH]
        parts += [a * cosine - b * sine, b * cosine + a * sine]
    return jnp.concatenate(parts, axis=-1)


def row_major(value):
    return with_layout_constraint(value, Layout(tuple(range(value.ndim))))


def swap(value, head_mask, blk_mask):
    groups = lax.axis_size("blk")
    count = lax.axis_size("head") * groups
    mask = head_mask * groups + blk_mask
    pairs = [(i, i ^ mask) for i in range(count)]
    return row_major(lax.ppermute(row_major(value), ("head", "blk"), pairs))


def masks_of(size):
    out, bit = [], size >> 1
    while bit:
        out.append(bit)
        bit >>= 1
    return out


def add(a, b, dtype):
    return (a.astype(F32) + b.astype(F32)).astype(dtype)


def pair(own, received, bit, axis):
    first = jnp.where(bit == 0, own, received)
    second = jnp.where(bit == 0, received, own)
    return jnp.stack([first, second], axis=axis)


def after(value, *others):
    return lax.optimization_barrier((value, *others))[0]


def assemble_kernel(places, *refs):
    parts, out, sems = refs[:-2], refs[-2], refs[-1]
    copies = [
        pltpu.make_async_copy(
            part,
            out.at[pl.ds(row, part.shape[0]), pl.ds(col, part.shape[1])],
            sems.at[i],
        )
        for i, (part, (row, col)) in enumerate(zip(parts, places))
    ]
    for copy in copies:
        copy.start()
    for copy in copies:
        copy.wait()


def assemble(parts, places):
    rows = max(row + part.shape[0] for part, (row, _) in zip(parts, places))
    cols = max(col + part.shape[1] for part, (_, col) in zip(parts, places))
    return pl.pallas_call(
        functools.partial(assemble_kernel, places),
        in_specs=[pl.BlockSpec(memory_space=pl.ANY)] * len(parts),
        out_specs=pl.BlockSpec(memory_space=pltpu.VMEM),
        out_shape=jax.ShapeDtypeStruct((rows, cols), parts[0].dtype),
        scratch_shapes=[pltpu.SemaphoreType.DMA((len(parts),))],
        cost_estimate=pl.CostEstimate(
            flops=0, bytes_accessed=4 * rows * cols, transcendentals=0
        ),
        name="assemble",
    )(*parts)


def stack_rows(parts):
    places, row = [], 0
    for part in parts:
        places.append((row, 0))
        row += part.shape[0]
    return assemble(parts, places)


class Sent:
    value = None


class Flow:
    def __init__(self):
        self.batch, self.before = [], []

    def send(self, value, head_mask, blk_mask):
        sent = Sent()
        self.batch.append((sent, value, head_mask, blk_mask))
        return sent

    def go(self):
        if not self.batch:
            return
        values = tuple(entry[1] for entry in self.batch)
        held = lax.optimization_barrier(values + tuple(sent.value for sent in self.before))
        arrived = [
            swap(value, head_mask, blk_mask)
            for (_, _, head_mask, blk_mask), value in zip(self.batch, held)
        ]
        for (sent, *_), value in zip(self.batch, lax.optimization_barrier(tuple(arrived))):
            sent.value = value
        self.before = [entry[0] for entry in self.batch]
        self.batch = []


    def join(self, value):
        value, *arrived = lax.optimization_barrier((value, *(sent.value for sent in self.before)))
        for sent, one in zip(self.before, arrived):
            sent.value = one
        return value


class Spread:
    def __init__(self, own, masks):
        self.masks, self.have = masks, {0: own}
        self.sents = {}

    def wave(self, flow, count):
        self.settle()
        for key in sorted(self.have):
            if bin(key).count("1") == count:
                for mask in self.masks:
                    if key == 0 or mask < (key & -key):
                        self.sents[key ^ mask] = flow.send(
                            self.have[key], CROSS if mask == 1 else 0, mask & ~1
                        )

    def settle(self):
        for key, sent in list(self.sents.items()):
            self.have[key] = sent.value
            del self.sents[key]


class Chain:
    def __init__(self, own, masks):
        self.blocks, self.masks, self.sent = own[None], list(masks), None

    def advance(self, flow):
        self.settle()
        if self.masks:
            mask = self.masks.pop(0)
            self.sent = flow.send(self.blocks, CROSS if mask == 1 else 0, mask & ~1)

    def settle(self):
        if self.sent is not None:
            self.blocks = jnp.concatenate([self.blocks, self.sent.value], axis=0)
            self.sent = None


class Fold:
    def __init__(self, blocks, masks):
        self.blocks, self.masks, self.sent = blocks, list(masks), None

    def advance(self, flow):
        if self.sent is not None:
            self.blocks = add(self.keep, self.sent.value, BF16 if self.masks else F32)
            self.sent = None
        if not self.masks:
            return False
        mask = self.masks.pop(0)
        half = self.blocks.shape[0] // 2
        self.keep = self.blocks[:half]
        self.sent = flow.send(self.blocks[half:], CROSS if mask == 1 else 0, mask & ~1)
        return True


class Bulk:
    def __init__(self, masks, count):
        self.masks = masks
        self.pieces, self.sents, self.done = {}, [], {}
        keys = [0]
        self.order = {}
        for mask in masks:
            self.order[mask] = [(key, which) for key in keys for which in range(count)]
            keys = keys + [key ^ mask for key in keys]

    def settle(self):
        waiting = []
        for name, sent in self.sents:
            if sent.value is None:
                waiting.append((name, sent))
            else:
                self.pieces.setdefault(name, []).append(sent.value)
        self.sents = waiting

    def take(self, flow, mask, rows, limit):
        self.limit = limit
        self.settle()
        for name in self.order[mask]:
            piece, offset, total = self.done.get((mask, name), (0, 0, 0))
            have = self.pieces.get(name, [])
            if total == limit or piece >= len(have):
                continue
            value = have[piece][offset : offset + rows]
            offset += value.shape[0]
            total += value.shape[0]
            if offset == have[piece].shape[0]:
                piece, offset = piece + 1, 0
            self.done[mask, name] = (piece, offset, total)
            self.sents.append(((name[0] ^ mask, name[1]), flow.send(value, 0, mask)))
            return True
        return False

    def left(self, mask, which):
        return any(
            self.done.get((m, name), (0, 0, 0))[2] < self.limit
            for m in self.masks
            if mask in (None, m)
            for name in self.order[m]
            if name[1] == which
        )

    def parts(self, which):
        self.settle()
        return {key: parts for (key, place), parts in self.pieces.items() if place == which}


class FfnFold:
    def __init__(self, total, masks, turn):
        count = 1 << len(masks)
        blocks = total.reshape(count, -1, total.shape[1])
        self.rows, self.half = blocks.shape[1], blocks.shape[1] // 2
        self.raw, self.halves = [blocks[i] for i in range(count)], {}
        self.turn, self.turning = turn, None
        self.missing = [[len(masks)] * 2] + [[0, 0] for _ in range(count - 1)]
        self.tasks, self.sent_rows = {}, {}
        for stage, mask in enumerate(masks):
            half = count >> (stage + 1)
            self.tasks[mask] = [(block, half) for block in range(2 * half - 1, half - 1, -1)]
            for block in range(half, 2 * half):
                self.missing[block] = [stage, stage]
        self.got, self.sents = {}, []

    def half_of(self, block, part):
        if (block, part) not in self.halves:
            first = part * self.half
            self.halves[block, part] = self.raw[block][first : first + self.half]
        return self.halves[block, part]

    def settle(self):
        waiting = []
        for block, half, first, sent in self.sents:
            if sent.value is None:
                waiting.append((block, half, first, sent))
                continue
            value = sent.value
            while value.shape[0]:
                part = first // self.half
                rows = min(value.shape[0], (part + 1) * self.half - first)
                parts = self.got.setdefault((block, part), [])
                parts.append(value[:rows])
                value, first = value[rows:], first + rows
                if sum(one.shape[0] for one in parts) == self.half:
                    into = block - half
                    self.missing[into][part] -= 1
                    received = jnp.concatenate(parts, axis=0) if len(parts) > 1 else parts[0]
                    self.halves[into, part] = add(
                        self.half_of(into, part), received, BF16 if into else F32
                    )
        self.sents = waiting

    def ready(self, block):
        if self.missing[block][0]:
            return 0
        return self.half if self.missing[block][1] else self.rows

    def next(self, mask):
        self.settle()
        for block, half in self.tasks[mask]:
            if self.ready(block) > self.sent_rows.get(block, 0):
                return block, half
        return None

    def take(self, flow, mask, rows):
        found = self.next(mask)
        if found is None:
            return False
        block, half = found
        first = self.sent_rows.get(block, 0)
        if (block, 0) in self.halves or (block, 1) in self.halves:
            part = first // self.half
            start = first - part * self.half
            piece = self.half_of(block, part)[start : start + rows]
        else:
            piece = self.raw[block][first : min(first + rows, self.ready(block))]
        self.sent_rows[block] = first + piece.shape[0]
        if self.sent_rows[block] == self.rows:
            self.tasks[mask].remove(found)
        self.sents.append((block, half, first, flow.send(piece, 0, mask)))
        return True

    def take_turn(self, flow):
        self.settle()
        if any(self.missing[0]) or self.turning is not None:
            return False
        parts = [self.half_of(0, part) for part in (0, 1)]
        self.mine = jnp.where(self.turn == 0, parts[0], parts[1])
        other = jnp.where(self.turn == 0, parts[1], parts[0])
        self.turning = flow.send(other.astype(BF16), 0, TURN)
        return True

    def result(self):
        rows, cols = self.mine.shape
        out = jnp.zeros((rows, 2 * cols), F32)
        out = lax.dynamic_update_slice(out, self.mine, (0, self.turn * cols))
        received = self.turning.value.astype(F32)
        return lax.dynamic_update_slice(out, received, (0, (1 - self.turn) * cols))


def span_of(pair_ref, group, late, per_seq):
    pair = pair_ref[group]
    seq = pair // per_seq
    first = pair - seq * per_seq
    return seq, jnp.where(late == 0, first, 2 * per_seq - 1 - first)


def tile_visible(place_ref, pair_ref, seg_ref, step, part, per_seq, seq_len):
    group, cross = place_ref[0], place_ref[1]
    piece, low = step // 2, step % 2
    key, count = 0, SEQS * per_seq
    bits = count.bit_length() - 1
    for bit in range(bits):
        key = key + ((piece >> bit) & 1) * (1 << (bits - 1 - bit))
    seq_k, span_k = span_of(
        pair_ref, group ^ (key - key % 2 + low), cross ^ (key % 2), per_seq
    )
    seq_q, span_q = span_of(pair_ref, group ^ part, cross, per_seq)
    last_k = seg_ref[seq_k * seq_len + span_k * BLOCK + BLOCK - 1]
    first_q = seg_ref[seq_q * seq_len + span_q * BLOCK]
    visible = (seq_k == seq_q) & (span_k <= span_q) & (last_k >= first_q)
    spans = 2 * per_seq
    return visible, seq_k * spans + span_k, seq_q * spans + span_q


def tile_mask(seg_row_ref, seg_col_ref, place_k, place_q):
    lanes = lax.broadcasted_iota(jnp.int32, seg_col_ref.shape, 1)
    column = jnp.sum(jnp.where(lanes == place_k, seg_col_ref[...], 0), axis=1, keepdims=True)
    row = seg_row_ref[pl.ds(place_q, 1), :]
    row = jnp.concatenate([row, row], axis=1)
    return column == row


def stack_heads(ref, part):
    rows = pl.ds(part * BLOCK, BLOCK)
    return jnp.concatenate([ref[rows, :HEAD_WIDTH], ref[rows, HEAD_WIDTH:]], axis=0)


def forward_kernel(
    per_seq, place_ref, pair_ref, seg_ref, q_ref, kv_ref, row_ref, col_ref,
    low_ref, out_ref, lse_ref, max_ref, sum_ref, acc_ref,
):
    step = pl.program_id(0)
    seq_len = 2 * per_seq * BLOCK

    @pl.when(step == 0)
    def _():
        max_ref[...] = jnp.full(max_ref.shape, NEGATIVE, F32)
        sum_ref[...] = jnp.zeros(sum_ref.shape, F32)
        acc_ref[...] = jnp.zeros(acc_ref.shape, F32)

    for sub in range(2):
        rows = pl.ds(sub * BLOCK, BLOCK)
        for part in range(2):
            visible, place_k, place_q = tile_visible(
                place_ref, pair_ref, seg_ref, 2 * step + sub, part, per_seq, seq_len
            )

            @pl.when(visible)
            def _():
                keys = kv_ref[rows, :HEAD_WIDTH]
                values = kv_ref[rows, HEAD_WIDTH:]
                queries = stack_heads(q_ref, part)
                scores = lax.dot_general(keys, queries, COLS, preferred_element_type=F32)
                mask = tile_mask(row_ref, col_ref, place_k, place_q)
                scores = jnp.where(mask, scores, NEGATIVE)
                old_max = max_ref[part]
                new_max = jnp.maximum(old_max, jnp.max(scores, axis=0, keepdims=True))
                weights = jnp.where(mask, jnp.exp(scores - new_max), 0.0)
                factor = jnp.exp(old_max - new_max)
                max_ref[part] = new_max
                sum_ref[part] = sum_ref[part] * factor + jnp.sum(weights, axis=0, keepdims=True)
                acc_ref[part] = acc_ref[part] * factor + lax.dot_general(
                    values, weights.astype(BF16), ROWS, preferred_element_type=F32
                )

    @pl.when(step == pl.num_programs(0) - 1)
    def _():
        for part in range(2):
            total = sum_ref[part]
            attended = (acc_ref[part] / total).T
            rows = pl.ds(part * BLOCK, BLOCK)
            for head in range(2):
                one = attended[head * BLOCK : (head + 1) * BLOCK]
                cols = pl.ds(head * HEAD_WIDTH, HEAD_WIDTH)
                out_ref[rows, cols] = one
                low_ref[rows, cols] = one.astype(BF16)
            lse_ref[part] = max_ref[part] + jnp.log(total)


def backward_kernel(
    per_seq, place_ref, pair_ref, seg_ref, q_ref, kv_ref, row_ref, col_ref, lse_ref, out_ref, do_ref,
    dq_ref, dk_ref, dv_ref, delta_ref, dq_acc, dk_acc, dv_acc,
):
    step = pl.program_id(0)
    seq_len = 2 * per_seq * BLOCK

    @pl.when(step == 0)
    def _():
        dq_acc[...] = jnp.zeros(dq_acc.shape, F32)
        for part in range(2):
            product = stack_heads(out_ref, part) * stack_heads(do_ref, part).astype(F32)
            delta_ref[part] = jnp.sum(product.T, axis=0, keepdims=True)

    for sub in range(2):
        key_rows = pl.ds(sub * BLOCK, BLOCK)
        dk_acc[...] = jnp.zeros(dk_acc.shape, F32)
        dv_acc[...] = jnp.zeros(dv_acc.shape, F32)
        for part in range(2):
            visible, place_k, place_q = tile_visible(
                place_ref, pair_ref, seg_ref, 2 * step + sub, part, per_seq, seq_len
            )

            @pl.when(visible)
            def _():
                keys = kv_ref[key_rows, :HEAD_WIDTH]
                values = kv_ref[key_rows, HEAD_WIDTH:]
                queries = stack_heads(q_ref, part)
                grads = stack_heads(do_ref, part)
                scores = lax.dot_general(keys, queries, COLS, preferred_element_type=F32)
                mask = tile_mask(row_ref, col_ref, place_k, place_q)
                probs = jnp.where(mask, jnp.exp(scores - lse_ref[part]), 0.0)
                grad_probs = lax.dot_general(values, grads, COLS, preferred_element_type=F32)
                grad_scores = (probs * (grad_probs - delta_ref[part])).astype(BF16)
                dv_acc[...] += jnp.dot(probs.astype(BF16), grads, preferred_element_type=F32)
                dk_acc[...] += jnp.dot(grad_scores, queries, preferred_element_type=F32)
                dq_acc[part] += lax.dot_general(
                    grad_scores, keys, ROWS, preferred_element_type=F32
                )

        dk_ref[key_rows, :] = dk_acc[...].astype(BF16)
        dv_ref[key_rows, :] = dv_acc[...].astype(BF16)

    @pl.when(step == pl.num_programs(0) - 1)
    def _():
        for part in range(2):
            rows = pl.ds(part * BLOCK, BLOCK)
            for head in range(2):
                one = dq_acc[part, head * BLOCK : (head + 1) * BLOCK]
                dq_ref[rows, pl.ds(head * HEAD_WIDTH, HEAD_WIDTH)] = (
                    one * HEAD_WIDTH ** (-0.5)
                ).astype(BF16)


def whole(shape):
    return pl.BlockSpec(shape, lambda step, *refs: (0,) * len(shape))


def attend(place, pair_order, seg_flat, queries, keys_values, seg_row, seg_col, per_seq):
    steps = keys_values.shape[0] // (2 * BLOCK)
    rows, width = queries.shape
    return pl.pallas_call(
        functools.partial(forward_kernel, per_seq),
        grid_spec=pltpu.PrefetchScalarGridSpec(
            num_scalar_prefetch=3,
            grid=(steps,),
            in_specs=[
                whole(queries.shape),
                pl.BlockSpec((2 * BLOCK, 2 * HEAD_WIDTH), lambda step, *refs: (step, 0)),
                whole(seg_row.shape),
                whole(seg_col.shape),
            ],
            out_specs=[whole((rows, width)), whole((rows, width)), whole((2, 1, rows))],
            scratch_shapes=[
                pltpu.VMEM((2, 1, rows), F32),
                pltpu.VMEM((2, 1, rows), F32),
                pltpu.VMEM((2, HEAD_WIDTH, rows), F32),
            ],
        ),
        out_shape=[
            jax.ShapeDtypeStruct((rows, width), BF16),
            jax.ShapeDtypeStruct((rows, width), F32),
            jax.ShapeDtypeStruct((2, 1, rows), F32),
        ],
        compiler_params=pltpu.CompilerParams(dimension_semantics=("arbitrary",)),
        cost_estimate=pl.CostEstimate(
            flops=6_000_000_000, bytes_accessed=6_000_000, transcendentals=2_000_000
        ),
        name="attend",
    )(place, pair_order, seg_flat, queries, keys_values, seg_row, seg_col)


def attend_back(
    place, pair_order, seg_flat, queries, keys_values, seg_row, seg_col, lse, out, grads, per_seq
):
    steps = keys_values.shape[0] // (2 * BLOCK)
    rows, width = queries.shape
    return pl.pallas_call(
        functools.partial(backward_kernel, per_seq),
        grid_spec=pltpu.PrefetchScalarGridSpec(
            num_scalar_prefetch=3,
            grid=(steps,),
            in_specs=[
                whole(queries.shape),
                pl.BlockSpec((2 * BLOCK, 2 * HEAD_WIDTH), lambda step, *refs: (step, 0)),
                whole(seg_row.shape),
                whole(seg_col.shape),
                whole(lse.shape),
                whole(out.shape),
                whole(grads.shape),
            ],
            out_specs=[
                whole((rows, width)),
                pl.BlockSpec((2 * BLOCK, HEAD_WIDTH), lambda step, *refs: (step, 0)),
                pl.BlockSpec((2 * BLOCK, HEAD_WIDTH), lambda step, *refs: (step, 0)),
            ],
            scratch_shapes=[
                pltpu.VMEM((2, 1, rows), F32),
                pltpu.VMEM((2, rows, HEAD_WIDTH), F32),
                pltpu.VMEM((BLOCK, HEAD_WIDTH), F32),
                pltpu.VMEM((BLOCK, HEAD_WIDTH), F32),
            ],
        ),
        out_shape=[
            jax.ShapeDtypeStruct((rows, width), BF16),
            jax.ShapeDtypeStruct((keys_values.shape[0], HEAD_WIDTH), BF16),
            jax.ShapeDtypeStruct((keys_values.shape[0], HEAD_WIDTH), BF16),
        ],
        compiler_params=pltpu.CompilerParams(dimension_semantics=("arbitrary",)),
        cost_estimate=pl.CostEstimate(
            flops=16_000_000_000, bytes_accessed=12_000_000, transcendentals=2_000_000
        ),
        name="attend_back",
    )(place, pair_order, seg_flat, queries, keys_values, seg_row, seg_col, lse, out, grads)


def rms_back(scaled, normed, inv_rms):
    return inv_rms * (scaled - normed * jnp.mean(scaled * normed, axis=-1, keepdims=True))


def bits_of(number, count):
    return [(number >> (count - 1 - i)) & 1 for i in range(count)]


def flip(value, bits, axes):
    for bit, axis in zip(bits, axes):
        value = jnp.where(bit == 0, value, jnp.flip(value, axis))
    return value


def local(
    tokens,
    cotangent,
    segments,
    pair_order,
    norm_in,
    w_query,
    key_weight,
    value_weight,
    w_out,
    norm_mid,
    w_gate,
    w_up,
    w_down,
):
    heads = lax.axis_size("head")
    groups = lax.axis_size("blk")
    group = lax.axis_index("blk")
    head = lax.axis_index("head")
    cross, core = head // 2, head % 2
    turn = (group // TURN) % 2
    low = group % 2
    depth = groups.bit_length() - 1
    token_rows, width = tokens.shape
    group_rows = token_rows * heads
    per_seq = groups // SEQS
    shard = norm_in.shape[0]
    blk_masks = masks_of(groups)
    wide_masks = blk_masks[:-1] + [1]
    far_masks = [mask for mask in blk_masks if mask != TURN]
    key_local = HEAD_WIDTH
    query_local = w_query.shape[1] // heads
    in_cols = query_local + 2 * key_local
    ff_rows, ff_cols = w_gate.shape
    ff_own = ff_cols // 2
    group_bits = bits_of(group, depth)

    wide_axes = [-depth - 2] + [-depth + i for i in range(depth - 1)]
    wide_bits = [cross] + group_bits[:-1]

    def to_wide(value):
        lead = value.shape[:-1]
        value = value.reshape(lead + (2, 2) + (2,) * (depth - 1) + (2 * shard,))
        value = flip(value, wide_bits, wide_axes)
        base = len(lead)
        order = [base] + [base + 2 + i for i in range(depth - 2, -1, -1)]
        order += [base + 1, base + depth + 1]
        return value.transpose(*range(base), *order).reshape(lead + (width,))

    def from_wide(value):
        lead = value.shape[:-1]
        value = value.reshape(lead + (2,) + (2,) * (depth - 1) + (2, 2 * shard))
        base = len(lead)
        order = [base, base + depth] + [base + 1 + i for i in range(depth - 2, -1, -1)]
        order += [base + depth + 1]
        value = value.transpose(*range(base), *order)
        return flip(value, wide_bits, wide_axes).reshape(lead + (width,))

    far_axes = [-depth - 1 + i for i in range(depth - 2)] + [-2]
    far_bits = group_bits[: depth - 2] + [low]

    def to_far(value):
        lead = value.shape[:-1]
        value = value.reshape(lead + (2,) * depth + (ff_rows,))
        value = flip(value, far_bits, far_axes)
        base = len(lead)
        order = [base + depth - 1] + [base + i for i in range(depth - 3, -1, -1)]
        order += [base + depth - 2, base + depth]
        return value.transpose(*range(base), *order).reshape(lead + (width,))

    def from_far(value):
        lead = value.shape[:-1]
        value = value.reshape(lead + (2,) * depth + (ff_rows,))
        base = len(lead)
        order = [base + 1 + i for i in range(depth - 3, -1, -1)]
        order += [base + depth - 1, base, base + depth]
        value = value.transpose(*range(base), *order)
        return flip(value, far_bits, far_axes).reshape(lead + (width,))

    def reversed_key(place, masks):
        bits = [(place >> (len(masks) - 1 - i)) & 1 for i in range(len(masks))]
        return sum(mask for bit, mask in zip(bits, masks[::-1]) if bit)

    def in_fold_order(have, masks):
        return [have[reversed_key(place, masks)] for place in range(1 << len(masks))]

    rows = jnp.arange(group_rows, dtype=jnp.int32)
    part_rows = 2 * token_rows
    local_row = cross * part_rows + (core ^ (rows % part_rows // token_rows)) * token_rows
    local_row = local_row + rows % token_rows
    pairs = [lax.dynamic_index_in_dim(pair_order, group ^ part, keepdims=False) for part in (0, 1)]
    first_span = jnp.where(rows < part_rows, pairs[0], pairs[1]) % per_seq
    span = jnp.where(local_row < BLOCK, first_span, 2 * per_seq - 1 - first_span)
    positions = span * BLOCK + local_row % BLOCK
    angles = positions.astype(F32)[:, None] * frequencies(HEAD_WIDTH)[None, :]
    cosine, sine = jnp.cos(angles), jnp.sin(angles)
    seg_halves = segments.reshape(-1, 2, BLOCK // 2)
    seg_row = jnp.where(core == 0, seg_halves, seg_halves[:, ::-1]).reshape(-1, BLOCK)
    seg_col = seg_row.T
    seg_flat = segments.reshape(-1)
    place = jnp.stack([group, cross]).astype(jnp.int32)

    flow = Flow()

    gains = jnp.zeros((2, heads * groups, shard), BF16)
    gains = lax.dynamic_update_slice(
        gains, jnp.stack([norm_in, norm_mid])[:, None], (0, head * groups + group, 0)
    )
    hops = [blk_masks[:1], blk_masks[1:-1], blk_masks[-1:], [None]]

    def hop():
        nonlocal gains, gain_sent
        if gain_sent is not None:
            gains = gains + gain_sent.value
            gain_sent = None
        if hops:
            *direct, last = hops.pop(0)
            for mask in direct:
                gains = gains + swap(gains, 0, mask)
            gain_sent = flow.send(gains, *((CROSS, 0) if last is None else (0, last)))

    gain_sent = None

    def column_half(weights, bit):
        return jnp.concatenate(
            [
                lax.dynamic_slice_in_dim(weight, bit * (weight.shape[1] // 2), weight.shape[1] // 2, 1)
                for weight in weights
            ],
            axis=1,
        )

    def core_half(value, bit):
        parts, first = [], 0
        for count in (2 * query_local, 2 * key_local, 2 * key_local, 2 * query_local):
            parts.append(
                lax.dynamic_slice_in_dim(value, first + bit * (count // 2), count // 2, 1)
            )
            first += count
        return jnp.concatenate(parts, axis=1)

    attention_weights = (w_query, key_weight, value_weight, w_out)

    def index(value, place):
        return lax.dynamic_index_in_dim(value, place, 0, keepdims=False)

    def halves(weight, bit):
        return lax.dynamic_slice_in_dim(weight, bit * ff_own, ff_own, 1)

    ffn_weights = (w_down, w_gate, w_up)
    bulk, block_rows = Bulk(far_masks, 3), 2 * ff_rows

    def send_turn(which):
        return flow.send(halves(ffn_weights[which], 1 - turn), 0, TURN)

    def end_turn(which, sent):
        own = pair(halves(ffn_weights[which], turn), sent.value, turn, 0)
        bulk.pieces[0, which] = [own.reshape(block_rows, -1)]

    def near(rows):
        return bulk.take(flow, 1, rows, block_rows)

    def high(rows):
        return any([bulk.take(flow, mask, rows, block_rows) for mask in far_masks[:-1]])

    own_half, other_half = (column_half(attention_weights, bit) for bit in (low, 1 - low))
    cols_core = flow.send(core_half(own_half, 1 - core), CORE, 0)
    cols_low = flow.send(core_half(other_half, core), 0, 1)
    cols_both = flow.send(core_half(other_half, 1 - core), CORE, 1)
    turned = send_turn(0)
    hop()
    flow.go()
    end_turn(0, turned)
    own_cols = pair(
        pair(core_half(own_half, core), cols_low.value, low, 0),
        pair(cols_core.value, cols_both.value, low, 0),
        core, 0,
    ).reshape(4 * shard, -1)
    spread_in = Spread(own_cols[:, :in_cols], wide_masks)
    chain_out = Chain(own_cols[:, in_cols:], wide_masks)
    spread_in.wave(flow, 0)
    token_x = to_wide(tokens)
    token_low = flow.send(token_x, 0, 1)
    hop()
    flow.go()
    spread_in.wave(flow, 1)
    high(ff_rows)
    hop()
    flow.go()
    for count in range(2, depth):
        if count > 2:
            flow.go()
        spread_in.wave(flow, count)
    token_core = flow.send(token_x, CORE, 0)
    token_both = flow.send(token_low.value, CORE, 0)
    turned = send_turn(1)
    hop()
    flow.go()
    token_group = jnp.concatenate(
        [token_x, token_core.value, token_low.value, token_both.value], axis=0
    ).astype(F32)
    end_turn(1, turned)
    hop()
    spread_in.settle()
    weight_in = jnp.concatenate(in_fold_order(spread_in.have, wide_masks), axis=0)
    gains = gains + swap(gains, CORE, 0)
    gains = gains.reshape(2, width).astype(F32)
    gain_in, gain_mid = to_wide(gains[:1]), gains[1:]
    turned = send_turn(2)
    near(ff_rows)
    chain_out.advance(flow)
    cot_far = to_far(cotangent)
    cot_x = flow.send(cot_far, CROSS, 0)
    flow.go()
    end_turn(2, turned)

    inv_group = lax.rsqrt(jnp.mean(token_group * token_group, axis=-1, keepdims=True) + EPS)
    input_low = (token_group * inv_group * gain_in).astype(BF16)
    lin = flow.join(jnp.dot(input_low, weight_in, preferred_element_type=F32))
    keys_values = jnp.concatenate(
        [
            rotate(lin[:, query_local : query_local + key_local], cosine, sine).astype(BF16),
            lin[:, query_local + key_local :].astype(BF16),
        ],
        axis=-1,
    )
    queries = rotate(lin[:, :query_local], cosine, sine).astype(BF16)
    queries = queries * jnp.asarray(HEAD_WIDTH ** (-0.5), BF16)

    spread_kv = Spread(keys_values, wide_masks)
    spread_kv.wave(flow, 0)
    near(ff_rows)
    near(ff_rows)
    flow.go()
    spread_kv.wave(flow, 1)
    near(block_rows)
    high(ff_rows)
    flow.go()
    for count in range(2, depth):
        if count > 2:
            flow.go()
        spread_kv.wave(flow, count)
    chain_out.advance(flow)
    high(ff_rows)
    near(ff_rows)
    near(ff_rows)
    flow.go()
    spread_kv.settle()
    kv_all = jnp.concatenate(in_fold_order(spread_kv.have, wide_masks), axis=0)
    while chain_out.masks:
        chain_out.advance(flow)
        if not chain_out.masks:
            high(ff_rows)
            near(ff_rows)
            near(ff_rows)
            cot_t = flow.send(cot_far, 0, TURN)
        flow.go()
    attention_low, attention_f, lse = attend(
        place, pair_order, seg_flat, queries, kv_all, seg_row, seg_col, per_seq
    )
    attention_low = flow.join(attention_low)
    chain_out.settle()
    weight_out = chain_out.blocks.reshape(width, -1)
    branch = lax.dot_general(attention_low, weight_out, COLS, preferred_element_type=F32)
    branch = row_major(branch.astype(BF16)).reshape(2, 2, token_rows, width)
    branch_across = add(branch[1, 0], swap(branch[1, 1], CORE, 0), BF16)
    branch_own = add(branch[0, 0], swap(branch[0, 1], CORE, 0), F32)
    branch_sent = flow.send(branch_across, 0, 1)
    cot_xt = flow.send(cot_t.value, CROSS, 0)
    high(ff_rows // 2)
    flow.go()
    branch = branch_own + branch_sent.value.astype(F32)

    tokens_f = tokens.astype(F32)
    middle = tokens_f + from_wide(branch)
    inv_mid = lax.rsqrt(jnp.mean(middle * middle, axis=-1, keepdims=True) + EPS)
    normed_mid = middle * inv_mid
    mid_low = to_far((normed_mid * gain_mid).astype(BF16))

    half = width // 2
    left, right = mid_low[:, :half], mid_low[:, half:]
    left_x = flow.send(left, CROSS, 0)
    right_t = flow.send(right, 0, TURN)
    near(ff_rows)
    high(ff_rows // 2)
    flow.go()
    left_t = flow.send(left, 0, TURN)
    right_x = flow.send(right, CROSS, 0)
    left_xt = flow.send(left_x.value, 0, TURN)
    right_xt = flow.send(right_t.value, CROSS, 0)
    high(ff_rows // 2)
    flow.go()
    def four_rows(parts, first_col):
        return [(part, (i * token_rows, first_col)) for i, part in enumerate(parts)]

    placed = four_rows([left, left_t.value, left_x.value, left_xt.value], 0)
    placed += four_rows([right, right_t.value, right_x.value, right_xt.value], half)
    mid_four = assemble([part for part, _ in placed], [where for _, where in placed])
    def eight(four):
        return stack_rows([four, swap(four, CORE, 0)])

    def weight_of(which):
        have = bulk.parts(which)
        return jnp.concatenate(
            [part for parts in in_fold_order(have, far_masks) for part in parts], axis=0
        )

    cot_four = jnp.concatenate([cot_far, cot_t.value, cot_x.value, cot_xt.value], axis=0)
    grad_group = jnp.concatenate([cot_four, swap(cot_four, CORE, 0)], axis=0)
    while bulk.left(None, 0):
        near(block_rows), high(block_rows)
        flow.go()
    down = weight_of(0)
    near(block_rows), near(block_rows), high(block_rows)
    flow.go()
    bulk.settle()
    mid_group = eight(mid_four)
    grad_hidden = jnp.dot(grad_group, down, preferred_element_type=F32)
    while bulk.left(None, 1):
        near(block_rows), near(block_rows), high(block_rows)
        flow.go()
    gate = weight_of(1)
    while bulk.left(None, 2):
        for _ in range(4):
            near(block_rows)
        high(block_rows)
        flow.go()
    grad_hidden = flow.join(grad_hidden)
    gate_lin = flow.join(jnp.dot(mid_group, gate, preferred_element_type=F32))
    up = weight_of(2)
    up_proj = jnp.dot(mid_group, up, preferred_element_type=F32)
    gate_sig = jax.nn.sigmoid(gate_lin)
    gate_silu = gate_lin * gate_sig
    hidden_act = (gate_silu * up_proj).astype(BF16)
    grad_gate_lin = (
        grad_hidden * up_proj * gate_sig * (1.0 + gate_lin * (1.0 - gate_sig))
    ).astype(BF16)
    grad_up_proj = (grad_hidden * gate_silu).astype(BF16)

    def ffn_fold(lhs, rhs):
        total = lax.dot_general(lhs, rhs, ROWS, preferred_element_type=F32)
        total = row_major(total.astype(BF16))
        return FfnFold(total, far_masks[::-1], turn)

    ffn_folds = []

    def near(rows):
        found = [(fold.next(1), i) for i, fold in enumerate(ffn_folds)]
        found = [(-block[0], i) for block, i in found if block is not None]
        return bool(found) and ffn_folds[min(found)[1]].take(flow, 1, rows)

    def high(rows):
        found = False
        for mask in far_masks[:-1][::-1]:
            found = any(fold.take(flow, mask, rows) for fold in ffn_folds) or found
        return found

    mid_partial = lax.dot_general(
        grad_gate_lin, gate, COLS, preferred_element_type=F32
    ) + lax.dot_general(grad_up_proj, up, COLS, preferred_element_type=F32)
    mid_partial = row_major(mid_partial.astype(BF16))
    down_fold = ffn_fold(grad_group, after(hidden_act, mid_partial))
    ffn_folds.append(down_fold)
    mid_partial = mid_partial.reshape(2, 2, 2, token_rows, width)
    four = add(mid_partial[0], swap(mid_partial[1], CORE, 0), BF16)
    left, right = four[..., :half], four[..., half:]
    left_sent = flow.send(left[:, 1], 0, TURN)
    right_sent = flow.send(right[1], CROSS, 0)
    near(ff_rows)
    flow.go()
    gate_fold = ffn_fold(mid_group, after(grad_gate_lin, four))
    first_step = left_sent.value
    ffn_partial = lax.dot_general(
        after(hidden_act, four), down, COLS, preferred_element_type=F32
    )
    ffn_partial = row_major(ffn_partial.astype(BF16)).reshape(2, 2, 2, token_rows, width)
    out_four = add(ffn_partial[0], swap(ffn_partial[1], CORE, 0), BF16)
    left = add(left[:, 0], left_sent.value, BF16)
    right = add(right[0], right_sent.value, BF16)
    left_sent = flow.send(left[1], CROSS, 0)
    right_sent = flow.send(right[1], 0, TURN)
    near(ff_rows)
    high(ff_rows // 2)
    flow.go()
    ffn_folds.append(gate_fold)
    grad_mid = jnp.concatenate(
        [add(left[0], left_sent.value, F32), add(right[0], right_sent.value, F32)], axis=-1
    )
    grad_mid = from_far(grad_mid)
    norm_mid_sum = jnp.sum(grad_mid * normed_mid, axis=0)
    grad_y = cotangent.astype(F32)
    grad_middle = grad_y + rms_back(grad_mid * gain_mid, normed_mid, inv_mid)
    grad_branch = to_wide(grad_middle.astype(BF16))
    branch_low = flow.send(grad_branch, 0, 1)
    high(ff_rows // 2)
    out_parts = [flow.send(out_four[1, 0], CROSS, 0)]
    flow.go()
    up_fold = ffn_fold(mid_group, after(grad_up_proj, first_step))
    ffn_folds.append(up_fold)
    branch_group = jnp.concatenate(
        [grad_branch, swap(grad_branch, CORE, 0), branch_low.value, swap(branch_low.value, CORE, 0)],
        axis=0,
    )
    grad_attention = jnp.dot(branch_group, weight_out, preferred_element_type=F32).astype(BF16)

    def weight_fold(lhs, rhs, extra=None):
        total = lax.dot_general(lhs, rhs, ROWS, preferred_element_type=F32)
        if extra is not None:
            column = jnp.broadcast_to(to_wide(extra[None])[0][:, None], (width, 128))
            total = jnp.concatenate([total, column], axis=1)
        total = row_major(total.astype(BF16))
        return Fold(total.reshape(groups, 4 * shard, -1), wide_masks[::-1])

    out_fold = weight_fold(branch_group, attention_low, norm_mid_sum)
    out_fold.advance(flow)
    near(block_rows)
    high(ff_rows)
    flow.go()
    grad_queries, grad_keys, grad_values = attend_back(
        place, pair_order, seg_flat, queries, kv_all, seg_row, seg_col,
        lse, attention_f, grad_attention, per_seq,
    )
    grad_queries = flow.join(grad_queries)
    grad_keys = flow.join(grad_keys)
    key_fold = Fold(grad_keys.reshape(groups, group_rows, -1), wide_masks[::-1])
    value_fold = Fold(grad_values.reshape(groups, group_rows, -1), wide_masks[::-1])
    key_fold.advance(flow)
    near(block_rows)
    high(ff_rows)
    flow.go()
    key_fold.advance(flow)
    value_fold.advance(flow)
    near(block_rows)
    high(ff_rows)
    flow.go()
    query_lin = rotate(grad_queries.astype(F32), cosine, -sine).astype(BF16)
    query_fold = weight_fold(input_low, query_lin)
    turns = [down_fold, gate_fold, up_fold]

    def take_turn():
        for fold in turns:
            if fold.take_turn(flow):
                turns.remove(fold)
                return

    while True:
        running = [fold.advance(flow) for fold in (key_fold, value_fold)]
        if not any(running):
            break
        query_fold.advance(flow)
        if all(running):
            high(ff_rows // 2)
            near(block_rows)
        else:
            near(ff_rows)
            high(ff_rows // 2)
            if len(out_parts) == 1:
                out_parts.append(flow.send(out_four[1, 1], CROSS, 0))
        flow.go()
    out_two = [add(out_four[0, i], sent.value, BF16) for i, sent in enumerate(out_parts)]
    out_sent = flow.send(out_two[1], 0, TURN)
    high(ff_rows // 2)
    flow.go()
    layer_out = (middle + from_far(add(out_two[0], out_sent.value, F32))).astype(BF16)
    keys_low, values_low = key_fold.blocks[0].astype(BF16), value_fold.blocks[0].astype(BF16)
    kv_lin = jnp.concatenate(
        [rotate(keys_low.astype(F32), cosine, -sine).astype(BF16), values_low], axis=-1
    )
    grad_lin = jnp.concatenate([query_lin, kv_lin], axis=-1)
    grad_in = lax.dot_general(grad_lin, weight_in, COLS, preferred_element_type=F32)
    grad_in = row_major(grad_in.astype(BF16)).reshape(2, 2, token_rows, width)
    in_across = add(grad_in[1, 0], swap(grad_in[1, 1], CORE, 0), BF16)
    in_own = add(grad_in[0, 0], swap(grad_in[0, 1], CORE, 0), F32)
    in_sent = flow.send(in_across, 0, 1)
    kv_fold = weight_fold(input_low, kv_lin)
    kv_fold.advance(flow)
    query_fold.advance(flow)
    out_fold.advance(flow)
    flow.go()
    kv_fold.advance(flow)
    query_fold.advance(flow)
    out_fold.advance(flow)
    near(ff_rows)
    flow.go()
    kv_fold.advance(flow)
    high(ff_rows)
    near(block_rows)
    take_turn()
    flow.go()
    while True:
        running = [fold.advance(flow) for fold in (kv_fold, query_fold, out_fold)]
        if not any(running):
            break
        near(block_rows), high(block_rows)
        flow.go()

    total = jnp.concatenate(
        [fold.blocks[0] for fold in (query_fold, kv_fold, out_fold)], axis=-1
    ).reshape(2, 2, shard, -1)

    def block_of(core_bit, low_bit):
        return index(index(total, core_bit), low_bit)

    sent_core = flow.send(block_of(1 - core, low).astype(BF16), CORE, 0)
    sent_low = flow.send(block_of(core, 1 - low).astype(BF16), 0, 1)
    sent_both = flow.send(block_of(1 - core, 1 - low).astype(BF16), CORE, 1)
    for fold in list(turns):
        if fold.take_turn(flow):
            turns.remove(fold)
    flow.go()
    while True:
        near(block_rows), high(block_rows)
        for fold in list(turns):
            if fold.take_turn(flow):
                turns.remove(fold)
        if not flow.batch:
            break
        flow.go()
    total = pair(
        pair(block_of(core, low), sent_core.value.astype(F32), core, 0),
        pair(sent_low.value.astype(F32), sent_both.value.astype(F32), core, 0),
        low, 0,
    ).reshape(4, shard, -1)
    scaled = in_own + in_sent.value.astype(F32)
    inv_in = inv_group[:token_rows]
    normed_in = tokens_f * inv_in
    grad_tokens = grad_middle + rms_back(from_wide(scaled * gain_in), normed_in, inv_in)

    def columns(first, count):
        return total[..., first : first + count].transpose(1, 0, 2).reshape(shard, -1)

    in_grads = [
        columns(0, query_local),
        columns(query_local, key_local),
        columns(query_local + key_local, key_local),
    ]
    grad_norm_in = sum(
        jnp.sum(grad * weight.astype(F32), axis=1)
        for grad, weight in zip(in_grads, attention_weights)
    ) / norm_in.astype(F32)
    grad_norm_mid = jnp.sum(total[..., in_cols + query_local], axis=0)
    return (
        layer_out,
        grad_tokens,
        grad_norm_in,
        *in_grads,
        columns(in_cols, query_local),
        grad_norm_mid,
        gate_fold.result(),
        up_fold.result(),
        down_fold.result(),
    )


def solution(mesh):
    rows = P(("blk", "head"), None)
    shards = P(("head", "blk"), None)
    vector = P(("head", "blk"))
    hidden = P("blk", "head")
    return jax.shard_map(
        local,
        mesh=mesh,
        in_specs=(
            rows, rows, P(), P(), vector, shards, shards, shards, shards, vector, hidden, hidden, hidden,
        ),
        out_specs=(
            rows, rows, vector, shards, shards, shards, shards, vector, hidden, hidden, hidden,
        ),
        check_vma=False,
    )
```

```python
import functools

import jax
import jax.numpy as jnp
from jax import lax
from jax.experimental import pallas as pl
from jax.experimental.layout import Layout, with_layout_constraint
from jax.experimental.pallas import tpu as pltpu
from jax.sharding import PartitionSpec as P

QUERY_HEAD_COUNT = 8
KEY_VALUE_HEADS = 4
HEAD_WIDTH = 256
SEQS = 2
BLOCK = 256

EPS = 1e-06
THETA = 1000042.0
NEGATIVE = -1e30
ROWS = (((0,), (0,)), ((), ()))
COLS = (((1,), (1,)), ((), ()))
BF16 = jnp.bfloat16
F32 = jnp.float32

CORE, CROSS, TURN = 1, 2, 2


def frequencies(head_size):
    return 1.0 / THETA ** (jnp.arange(0, head_size, 2, dtype=F32) / head_size)


def rotate(values, cosine, sine):
    half = HEAD_WIDTH // 2
    parts = []
    for first in range(0, values.shape[-1], HEAD_WIDTH):
        a = values[:, first : first + half]
        b = values[:, first + half : first + HEAD_WIDTH]
        parts += [a * cosine - b * sine, b * cosine + a * sine]
    return jnp.concatenate(parts, axis=-1)


def row_major(value):
    return with_layout_constraint(value, Layout(tuple(range(value.ndim))))


def swap(value, head_mask, blk_mask):
    groups = lax.axis_size("blk")
    count = lax.axis_size("head") * groups
    mask = head_mask * groups + blk_mask
    pairs = [(i, i ^ mask) for i in range(count)]
    return row_major(lax.ppermute(row_major(value), ("head", "blk"), pairs))


def masks_of(size):
    out, bit = [], size >> 1
    while bit:
        out.append(bit)
        bit >>= 1
    return out


def add(a, b, dtype):
    return (a.astype(F32) + b.astype(F32)).astype(dtype)


def pair(own, received, bit, axis):
    first = jnp.where(bit == 0, own, received)
    second = jnp.where(bit == 0, received, own)
    return jnp.stack([first, second], axis=axis)


def after(value, *others):
    return lax.optimization_barrier((value, *others))[0]


def assemble_kernel(places, *refs):
    parts, out, sems = refs[:-2], refs[-2], refs[-1]
    copies = [
        pltpu.make_async_copy(
            part,
            out.at[pl.ds(row, part.shape[0]), pl.ds(col, part.shape[1])],
            sems.at[i],
        )
        for i, (part, (row, col)) in enumerate(zip(parts, places))
    ]
    for copy in copies:
        copy.start()
    for copy in copies:
        copy.wait()


def assemble(parts, places):
    rows = max(row + part.shape[0] for part, (row, _) in zip(parts, places))
    cols = max(col + part.shape[1] for part, (_, col) in zip(parts, places))
    return pl.pallas_call(
        functools.partial(assemble_kernel, places),
        in_specs=[pl.BlockSpec(memory_space=pl.ANY)] * len(parts),
        out_specs=pl.BlockSpec(memory_space=pltpu.VMEM),
        out_shape=jax.ShapeDtypeStruct((rows, cols), parts[0].dtype),
        scratch_shapes=[pltpu.SemaphoreType.DMA((len(parts),))],
        cost_estimate=pl.CostEstimate(
            flops=0, bytes_accessed=4 * rows * cols, transcendentals=0
        ),
        name="assemble",
    )(*parts)


def stack_rows(parts):
    places, row = [], 0
    for part in parts:
        places.append((row, 0))
        row += part.shape[0]
    return assemble(parts, places)


class Sent:
    value = None


class Flow:
    def __init__(self):
        self.batch, self.before = [], []

    def send(self, value, head_mask, blk_mask):
        sent = Sent()
        self.batch.append((sent, value, head_mask, blk_mask))
        return sent

    def go(self):
        if not self.batch:
            return
        values = tuple(entry[1] for entry in self.batch)
        held = lax.optimization_barrier(values + tuple(sent.value for sent in self.before))
        arrived = [
            swap(value, head_mask, blk_mask)
            for (_, _, head_mask, blk_mask), value in zip(self.batch, held)
        ]
        for (sent, *_), value in zip(self.batch, lax.optimization_barrier(tuple(arrived))):
            sent.value = value
        self.before = [entry[0] for entry in self.batch]
        self.batch = []


    def join(self, value):
        value, *arrived = lax.optimization_barrier((value, *(sent.value for sent in self.before)))
        for sent, one in zip(self.before, arrived):
            sent.value = one
        return value


class Spread:
    def __init__(self, own, masks):
        self.masks, self.have = masks, {0: own}
        self.sents = {}

    def wave(self, flow, count):
        self.settle()
        for key in sorted(self.have):
            if bin(key).count("1") == count:
                for mask in self.masks:
                    if key == 0 or mask < (key & -key):
                        self.sents[key ^ mask] = flow.send(
                            self.have[key], CROSS if mask == 1 else 0, mask & ~1
                        )

    def settle(self):
        for key, sent in list(self.sents.items()):
            self.have[key] = sent.value
            del self.sents[key]


class Chain:
    def __init__(self, own, masks):
        self.blocks, self.masks, self.sent = own[None], list(masks), None

    def advance(self, flow):
        self.settle()
        if self.masks:
            mask = self.masks.pop(0)
            self.sent = flow.send(self.blocks, CROSS if mask == 1 else 0, mask & ~1)

    def settle(self):
        if self.sent is not None:
            self.blocks = jnp.concatenate([self.blocks, self.sent.value], axis=0)
            self.sent = None


class Fold:
    def __init__(self, blocks, masks):
        self.blocks, self.masks, self.sent = blocks, list(masks), None

    def advance(self, flow):
        if self.sent is not None:
            self.blocks = add(self.keep, self.sent.value, BF16 if self.masks else F32)
            self.sent = None
        if not self.masks:
            return False
        mask = self.masks.pop(0)
        half = self.blocks.shape[0] // 2
        self.keep = self.blocks[:half]
        self.sent = flow.send(self.blocks[half:], CROSS if mask == 1 else 0, mask & ~1)
        return True


class Bulk:
    def __init__(self, masks, count):
        self.masks = masks
        self.pieces, self.sents, self.done = {}, [], {}
        keys = [0]
        self.order = {}
        for mask in masks:
            self.order[mask] = [(key, which) for key in keys for which in range(count)]
            keys = keys + [key ^ mask for key in keys]

    def settle(self):
        waiting = []
        for name, sent in self.sents:
            if sent.value is None:
                waiting.append((name, sent))
            else:
                self.pieces.setdefault(name, []).append(sent.value)
        self.sents = waiting

    def take(self, flow, mask, rows, limit):
        self.limit = limit
        self.settle()
        for name in self.order[mask]:
            piece, offset, total = self.done.get((mask, name), (0, 0, 0))
            have = self.pieces.get(name, [])
            if total == limit or piece >= len(have):
                continue
            value = have[piece][offset : offset + rows]
            offset += value.shape[0]
            total += value.shape[0]
            if offset == have[piece].shape[0]:
                piece, offset = piece + 1, 0
            self.done[mask, name] = (piece, offset, total)
            self.sents.append(((name[0] ^ mask, name[1]), flow.send(value, 0, mask)))
            return True
        return False

    def left(self, mask, which):
        return any(
            self.done.get((m, name), (0, 0, 0))[2] < self.limit
            for m in self.masks
            if mask in (None, m)
            for name in self.order[m]
            if name[1] == which
        )

    def parts(self, which):
        self.settle()
        return {key: parts for (key, place), parts in self.pieces.items() if place == which}


class FfnFold:
    def __init__(self, total, masks, turn):
        count = 1 << len(masks)
        blocks = total.reshape(count, -1, total.shape[1])
        self.rows, self.half = blocks.shape[1], blocks.shape[1] // 2
        self.raw, self.halves = [blocks[i] for i in range(count)], {}
        self.turn, self.turning = turn, None
        self.missing = [[len(masks)] * 2] + [[0, 0] for _ in range(count - 1)]
        self.tasks, self.sent_rows = {}, {}
        for stage, mask in enumerate(masks):
            half = count >> (stage + 1)
            self.tasks[mask] = [(block, half) for block in range(2 * half - 1, half - 1, -1)]
            for block in range(half, 2 * half):
                self.missing[block] = [stage, stage]
        self.got, self.sents = {}, []

    def half_of(self, block, part):
        if (block, part) not in self.halves:
            first = part * self.half
            self.halves[block, part] = self.raw[block][first : first + self.half]
        return self.halves[block, part]

    def settle(self):
        waiting = []
        for block, half, first, sent in self.sents:
            if sent.value is None:
                waiting.append((block, half, first, sent))
                continue
            value = sent.value
            while value.shape[0]:
                part = first // self.half
                rows = min(value.shape[0], (part + 1) * self.half - first)
                parts = self.got.setdefault((block, part), [])
                parts.append(value[:rows])
                value, first = value[rows:], first + rows
                if sum(one.shape[0] for one in parts) == self.half:
                    into = block - half
                    self.missing[into][part] -= 1
                    received = jnp.concatenate(parts, axis=0) if len(parts) > 1 else parts[0]
                    self.halves[into, part] = add(
                        self.half_of(into, part), received, BF16 if into else F32
                    )
        self.sents = waiting

    def ready(self, block):
        if self.missing[block][0]:
            return 0
        return self.half if self.missing[block][1] else self.rows

    def next(self, mask):
        self.settle()
        for block, half in self.tasks[mask]:
            if self.ready(block) > self.sent_rows.get(block, 0):
                return block, half
        return None

    def take(self, flow, mask, rows):
        found = self.next(mask)
        if found is None:
            return False
        block, half = found
        first = self.sent_rows.get(block, 0)
        if (block, 0) in self.halves or (block, 1) in self.halves:
            part = first // self.half
            start = first - part * self.half
            piece = self.half_of(block, part)[start : start + rows]
        else:
            piece = self.raw[block][first : min(first + rows, self.ready(block))]
        self.sent_rows[block] = first + piece.shape[0]
        if self.sent_rows[block] == self.rows:
            self.tasks[mask].remove(found)
        self.sents.append((block, half, first, flow.send(piece, 0, mask)))
        return True

    def take_turn(self, flow):
        self.settle()
        if any(self.missing[0]) or self.turning is not None:
            return False
        parts = [self.half_of(0, part) for part in (0, 1)]
        self.mine = jnp.where(self.turn == 0, parts[0], parts[1])
        other = jnp.where(self.turn == 0, parts[1], parts[0])
        self.turning = flow.send(other.astype(BF16), 0, TURN)
        return True

    def result(self):
        rows, cols = self.mine.shape
        out = jnp.zeros((rows, 2 * cols), F32)
        out = lax.dynamic_update_slice(out, self.mine, (0, self.turn * cols))
        received = self.turning.value.astype(F32)
        return lax.dynamic_update_slice(out, received, (0, (1 - self.turn) * cols))


def span_of(pair_ref, group, late, per_seq):
    pair = pair_ref[group]
    seq = pair // per_seq
    first = pair - seq * per_seq
    return seq, jnp.where(late == 0, first, 2 * per_seq - 1 - first)


def tile_visible(place_ref, pair_ref, seg_ref, step, part, per_seq, seq_len):
    group, cross = place_ref[0], place_ref[1]
    piece, low = step // 2, step % 2
    key, count = 0, SEQS * per_seq
    bits = count.bit_length() - 1
    for bit in range(bits):
        key = key + ((piece >> bit) & 1) * (1 << (bits - 1 - bit))
    seq_k, span_k = span_of(
        pair_ref, group ^ (key - key % 2 + low), cross ^ (key % 2), per_seq
    )
    seq_q, span_q = span_of(pair_ref, group ^ part, cross, per_seq)
    last_k = seg_ref[seq_k * seq_len + span_k * BLOCK + BLOCK - 1]
    first_q = seg_ref[seq_q * seq_len + span_q * BLOCK]
    visible = (seq_k == seq_q) & (span_k <= span_q) & (last_k >= first_q)
    spans = 2 * per_seq
    return visible, seq_k * spans + span_k, seq_q * spans + span_q


def tile_mask(seg_row_ref, seg_col_ref, place_k, place_q):
    lanes = lax.broadcasted_iota(jnp.int32, seg_col_ref.shape, 1)
    column = jnp.sum(jnp.where(lanes == place_k, seg_col_ref[...], 0), axis=1, keepdims=True)
    row = seg_row_ref[pl.ds(place_q, 1), :]
    row = jnp.concatenate([row, row], axis=1)
    return column == row


def stack_heads(ref, part):
    rows = pl.ds(part * BLOCK, BLOCK)
    return jnp.concatenate([ref[rows, :HEAD_WIDTH], ref[rows, HEAD_WIDTH:]], axis=0)


def forward_kernel(
    per_seq, place_ref, pair_ref, seg_ref, q_ref, kv_ref, row_ref, col_ref,
    low_ref, out_ref, lse_ref, max_ref, sum_ref, acc_ref,
):
    step = pl.program_id(0)
    seq_len = 2 * per_seq * BLOCK

    @pl.when(step == 0)
    def _():
        max_ref[...] = jnp.full(max_ref.shape, NEGATIVE, F32)
        sum_ref[...] = jnp.zeros(sum_ref.shape, F32)
        acc_ref[...] = jnp.zeros(acc_ref.shape, F32)

    for sub in range(2):
        rows = pl.ds(sub * BLOCK, BLOCK)
        for part in range(2):
            visible, place_k, place_q = tile_visible(
                place_ref, pair_ref, seg_ref, 2 * step + sub, part, per_seq, seq_len
            )

            @pl.when(visible)
            def _():
                keys = kv_ref[rows, :HEAD_WIDTH]
                values = kv_ref[rows, HEAD_WIDTH:]
                queries = stack_heads(q_ref, part)
                scores = lax.dot_general(keys, queries, COLS, preferred_element_type=F32)
                mask = tile_mask(row_ref, col_ref, place_k, place_q)
                scores = jnp.where(mask, scores, NEGATIVE)
                old_max = max_ref[part]
                new_max = jnp.maximum(old_max, jnp.max(scores, axis=0, keepdims=True))
                weights = jnp.where(mask, jnp.exp(scores - new_max), 0.0)
                factor = jnp.exp(old_max - new_max)
                max_ref[part] = new_max
                sum_ref[part] = sum_ref[part] * factor + jnp.sum(weights, axis=0, keepdims=True)
                acc_ref[part] = acc_ref[part] * factor + lax.dot_general(
                    values, weights.astype(BF16), ROWS, preferred_element_type=F32
                )

    @pl.when(step == pl.num_programs(0) - 1)
    def _():
        for part in range(2):
            total = sum_ref[part]
            attended = (acc_ref[part] / total).T
            rows = pl.ds(part * BLOCK, BLOCK)
            for head in range(2):
                one = attended[head * BLOCK : (head + 1) * BLOCK]
                cols = pl.ds(head * HEAD_WIDTH, HEAD_WIDTH)
                out_ref[rows, cols] = one
                low_ref[rows, cols] = one.astype(BF16)
            lse_ref[part] = max_ref[part] + jnp.log(total)


def backward_kernel(
    per_seq, place_ref, pair_ref, seg_ref, q_ref, kv_ref, row_ref, col_ref, lse_ref, out_ref, do_ref,
    dq_ref, dk_ref, dv_ref, delta_ref, dq_acc, dk_acc, dv_acc,
):
    step = pl.program_id(0)
    seq_len = 2 * per_seq * BLOCK

    @pl.when(step == 0)
    def _():
        dq_acc[...] = jnp.zeros(dq_acc.shape, F32)
        for part in range(2):
            product = stack_heads(out_ref, part) * stack_heads(do_ref, part).astype(F32)
            delta_ref[part] = jnp.sum(product.T, axis=0, keepdims=True)

    for sub in range(2):
        key_rows = pl.ds(sub * BLOCK, BLOCK)
        dk_acc[...] = jnp.zeros(dk_acc.shape, F32)
        dv_acc[...] = jnp.zeros(dv_acc.shape, F32)
        for part in range(2):
            visible, place_k, place_q = tile_visible(
                place_ref, pair_ref, seg_ref, 2 * step + sub, part, per_seq, seq_len
            )

            @pl.when(visible)
            def _():
                keys = kv_ref[key_rows, :HEAD_WIDTH]
                values = kv_ref[key_rows, HEAD_WIDTH:]
                queries = stack_heads(q_ref, part)
                grads = stack_heads(do_ref, part)
                scores = lax.dot_general(keys, queries, COLS, preferred_element_type=F32)
                mask = tile_mask(row_ref, col_ref, place_k, place_q)
                probs = jnp.where(mask, jnp.exp(scores - lse_ref[part]), 0.0)
                grad_probs = lax.dot_general(values, grads, COLS, preferred_element_type=F32)
                grad_scores = (probs * (grad_probs - delta_ref[part])).astype(BF16)
                dv_acc[...] += jnp.dot(probs.astype(BF16), grads, preferred_element_type=F32)
                dk_acc[...] += jnp.dot(grad_scores, queries, preferred_element_type=F32)
                dq_acc[part] += lax.dot_general(
                    grad_scores, keys, ROWS, preferred_element_type=F32
                )

        dk_ref[key_rows, :] = dk_acc[...].astype(BF16)
        dv_ref[key_rows, :] = dv_acc[...].astype(BF16)

    @pl.when(step == pl.num_programs(0) - 1)
    def _():
        for part in range(2):
            rows = pl.ds(part * BLOCK, BLOCK)
            for head in range(2):
                one = dq_acc[part, head * BLOCK : (head + 1) * BLOCK]
                dq_ref[rows, pl.ds(head * HEAD_WIDTH, HEAD_WIDTH)] = (
                    one * HEAD_WIDTH ** (-0.5)
                ).astype(BF16)


def whole(shape):
    return pl.BlockSpec(shape, lambda step, *refs: (0,) * len(shape))


def attend(place, pair_order, seg_flat, queries, keys_values, seg_row, seg_col, per_seq):
    steps = keys_values.shape[0] // (2 * BLOCK)
    rows, width = queries.shape
    return pl.pallas_call(
        functools.partial(forward_kernel, per_seq),
        grid_spec=pltpu.PrefetchScalarGridSpec(
            num_scalar_prefetch=3,
            grid=(steps,),
            in_specs=[
                whole(queries.shape),
                pl.BlockSpec((2 * BLOCK, 2 * HEAD_WIDTH), lambda step, *refs: (step, 0)),
                whole(seg_row.shape),
                whole(seg_col.shape),
            ],
            out_specs=[whole((rows, width)), whole((rows, width)), whole((2, 1, rows))],
            scratch_shapes=[
                pltpu.VMEM((2, 1, rows), F32),
                pltpu.VMEM((2, 1, rows), F32),
                pltpu.VMEM((2, HEAD_WIDTH, rows), F32),
            ],
        ),
        out_shape=[
            jax.ShapeDtypeStruct((rows, width), BF16),
            jax.ShapeDtypeStruct((rows, width), F32),
            jax.ShapeDtypeStruct((2, 1, rows), F32),
        ],
        compiler_params=pltpu.CompilerParams(dimension_semantics=("arbitrary",)),
        cost_estimate=pl.CostEstimate(
            flops=6_000_000_000, bytes_accessed=6_000_000, transcendentals=2_000_000
        ),
        name="attend",
    )(place, pair_order, seg_flat, queries, keys_values, seg_row, seg_col)


def attend_back(
    place, pair_order, seg_flat, queries, keys_values, seg_row, seg_col, lse, out, grads, per_seq
):
    steps = keys_values.shape[0] // (2 * BLOCK)
    rows, width = queries.shape
    return pl.pallas_call(
        functools.partial(backward_kernel, per_seq),
        grid_spec=pltpu.PrefetchScalarGridSpec(
            num_scalar_prefetch=3,
            grid=(steps,),
            in_specs=[
                whole(queries.shape),
                pl.BlockSpec((2 * BLOCK, 2 * HEAD_WIDTH), lambda step, *refs: (step, 0)),
                whole(seg_row.shape),
                whole(seg_col.shape),
                whole(lse.shape),
                whole(out.shape),
                whole(grads.shape),
            ],
            out_specs=[
                whole((rows, width)),
                pl.BlockSpec((2 * BLOCK, HEAD_WIDTH), lambda step, *refs: (step, 0)),
                pl.BlockSpec((2 * BLOCK, HEAD_WIDTH), lambda step, *refs: (step, 0)),
            ],
            scratch_shapes=[
                pltpu.VMEM((2, 1, rows), F32),
                pltpu.VMEM((2, rows, HEAD_WIDTH), F32),
                pltpu.VMEM((BLOCK, HEAD_WIDTH), F32),
                pltpu.VMEM((BLOCK, HEAD_WIDTH), F32),
            ],
        ),
        out_shape=[
            jax.ShapeDtypeStruct((rows, width), BF16),
            jax.ShapeDtypeStruct((keys_values.shape[0], HEAD_WIDTH), BF16),
            jax.ShapeDtypeStruct((keys_values.shape[0], HEAD_WIDTH), BF16),
        ],
        compiler_params=pltpu.CompilerParams(dimension_semantics=("arbitrary",)),
        cost_estimate=pl.CostEstimate(
            flops=16_000_000_000, bytes_accessed=12_000_000, transcendentals=2_000_000
        ),
        name="attend_back",
    )(place, pair_order, seg_flat, queries, keys_values, seg_row, seg_col, lse, out, grads)


def rms_back(scaled, normed, inv_rms):
    return inv_rms * (scaled - normed * jnp.mean(scaled * normed, axis=-1, keepdims=True))


def bits_of(number, count):
    return [(number >> (count - 1 - i)) & 1 for i in range(count)]


def flip(value, bits, axes):
    for bit, axis in zip(bits, axes):
        value = jnp.where(bit == 0, value, jnp.flip(value, axis))
    return value


def local(
    tokens,
    cotangent,
    segments,
    pair_order,
    norm_in,
    w_query,
    key_weight,
    value_weight,
    w_out,
    norm_mid,
    w_gate,
    w_up,
    w_down,
):
    heads = lax.axis_size("head")
    groups = lax.axis_size("blk")
    group = lax.axis_index("blk")
    head = lax.axis_index("head")
    cross, core = head // 2, head % 2
    turn = (group // TURN) % 2
    low = group % 2
    depth = groups.bit_length() - 1
    token_rows, width = tokens.shape
    group_rows = token_rows * heads
    per_seq = groups // SEQS
    shard = norm_in.shape[0]
    blk_masks = masks_of(groups)
    wide_masks = blk_masks[:-1] + [1]
    far_masks = [mask for mask in blk_masks if mask != TURN]
    key_local = HEAD_WIDTH
    query_local = w_query.shape[1] // heads
    in_cols = query_local + 2 * key_local
    ff_rows, ff_cols = w_gate.shape
    ff_own = ff_cols // 2
    group_bits = bits_of(group, depth)

    wide_axes = [-depth - 2] + [-depth + i for i in range(depth - 1)]
    wide_bits = [cross] + group_bits[:-1]

    def to_wide(value):
        lead = value.shape[:-1]
        value = value.reshape(lead + (2, 2) + (2,) * (depth - 1) + (2 * shard,))
        value = flip(value, wide_bits, wide_axes)
        base = len(lead)
        order = [base] + [base + 2 + i for i in range(depth - 2, -1, -1)]
        order += [base + 1, base + depth + 1]
        return value.transpose(*range(base), *order).reshape(lead + (width,))

    def from_wide(value):
        lead = value.shape[:-1]
        value = value.reshape(lead + (2,) + (2,) * (depth - 1) + (2, 2 * shard))
        base = len(lead)
        order = [base, base + depth] + [base + 1 + i for i in range(depth - 2, -1, -1)]
        order += [base + depth + 1]
        value = value.transpose(*range(base), *order)
        return flip(value, wide_bits, wide_axes).reshape(lead + (width,))

    far_axes = [-depth - 1 + i for i in range(depth - 2)] + [-2]
    far_bits = group_bits[: depth - 2] + [low]

    def to_far(value):
        lead = value.shape[:-1]
        value = value.reshape(lead + (2,) * depth + (ff_rows,))
        value = flip(value, far_bits, far_axes)
        base = len(lead)
        order = [base + depth - 1] + [base + i for i in range(depth - 3, -1, -1)]
        order += [base + depth - 2, base + depth]
        return value.transpose(*range(base), *order).reshape(lead + (width,))

    def from_far(value):
        lead = value.shape[:-1]
        value = value.reshape(lead + (2,) * depth + (ff_rows,))
        base = len(lead)
        order = [base + 1 + i for i in range(depth - 3, -1, -1)]
        order += [base + depth - 1, base, base + depth]
        value = value.transpose(*range(base), *order)
        return flip(value, far_bits, far_axes).reshape(lead + (width,))

    def reversed_key(place, masks):
        bits = [(place >> (len(masks) - 1 - i)) & 1 for i in range(len(masks))]
        return sum(mask for bit, mask in zip(bits, masks[::-1]) if bit)

    def in_fold_order(have, masks):
        return [have[reversed_key(place, masks)] for place in range(1 << len(masks))]

    rows = jnp.arange(group_rows, dtype=jnp.int32)
    part_rows = 2 * token_rows
    local_row = cross * part_rows + (core ^ (rows % part_rows // token_rows)) * token_rows
    local_row = local_row + rows % token_rows
    pairs = [lax.dynamic_index_in_dim(pair_order, group ^ part, keepdims=False) for part in (0, 1)]
    first_span = jnp.where(rows < part_rows, pairs[0], pairs[1]) % per_seq
    span = jnp.where(local_row < BLOCK, first_span, 2 * per_seq - 1 - first_span)
    positions = span * BLOCK + local_row % BLOCK
    angles = positions.astype(F32)[:, None] * frequencies(HEAD_WIDTH)[None, :]
    cosine, sine = jnp.cos(angles), jnp.sin(angles)
    seg_halves = segments.reshape(-1, 2, BLOCK // 2)
    seg_row = jnp.where(core == 0, seg_halves, seg_halves[:, ::-1]).reshape(-1, BLOCK)
    seg_col = seg_row.T
    seg_flat = segments.reshape(-1)
    place = jnp.stack([group, cross]).astype(jnp.int32)

    flow = Flow()

    gains = jnp.zeros((2, heads * groups, shard), BF16)
    gains = lax.dynamic_update_slice(
        gains, jnp.stack([norm_in, norm_mid])[:, None], (0, head * groups + group, 0)
    )
    hops = [blk_masks[:1], blk_masks[1:-1], blk_masks[-1:], [None]]

    def hop():
        nonlocal gains, gain_sent
        if gain_sent is not None:
            gains = gains + gain_sent.value
            gain_sent = None
        if hops:
            *direct, last = hops.pop(0)
            for mask in direct:
                gains = gains + swap(gains, 0, mask)
            gain_sent = flow.send(gains, *((CROSS, 0) if last is None else (0, last)))

    gain_sent = None

    def column_half(weights, bit):
        return jnp.concatenate(
            [
                lax.dynamic_slice_in_dim(weight, bit * (weight.shape[1] // 2), weight.shape[1] // 2, 1)
                for weight in weights
            ],
            axis=1,
        )

    def core_half(value, bit):
        parts, first = [], 0
        for count in (2 * query_local, 2 * key_local, 2 * key_local, 2 * query_local):
            parts.append(
                lax.dynamic_slice_in_dim(value, first + bit * (count // 2), count // 2, 1)
            )
            first += count
        return jnp.concatenate(parts, axis=1)

    attention_weights = (w_query, key_weight, value_weight, w_out)

    def index(value, place):
        return lax.dynamic_index_in_dim(value, place, 0, keepdims=False)

    def halves(weight, bit):
        return lax.dynamic_slice_in_dim(weight, bit * ff_own, ff_own, 1)

    ffn_weights = (w_down, w_gate, w_up)
    bulk, block_rows = Bulk(far_masks, 3), 2 * ff_rows

    def send_turn(which):
        return flow.send(halves(ffn_weights[which], 1 - turn), 0, TURN)

    def end_turn(which, sent):
        own = pair(halves(ffn_weights[which], turn), sent.value, turn, 0)
        bulk.pieces[0, which] = [own.reshape(block_rows, -1)]

    def near(rows):
        return bulk.take(flow, 1, rows, block_rows)

    def high(rows):
        return any([bulk.take(flow, mask, rows, block_rows) for mask in far_masks[:-1]])

    own_half, other_half = (column_half(attention_weights, bit) for bit in (low, 1 - low))
    cols_core = flow.send(core_half(own_half, 1 - core), CORE, 0)
    cols_low = flow.send(core_half(other_half, core), 0, 1)
    cols_both = flow.send(core_half(other_half, 1 - core), CORE, 1)
    turned = send_turn(0)
    hop()
    flow.go()
    end_turn(0, turned)
    own_cols = pair(
        pair(core_half(own_half, core), cols_low.value, low, 0),
        pair(cols_core.value, cols_both.value, low, 0),
        core, 0,
    ).reshape(4 * shard, -1)
    spread_in = Spread(own_cols[:, :in_cols], wide_masks)
    chain_out = Chain(own_cols[:, in_cols:], wide_masks)
    spread_in.wave(flow, 0)
    token_x = to_wide(tokens)
    token_low = flow.send(token_x, 0, 1)
    hop()
    flow.go()
    spread_in.wave(flow, 1)
    high(ff_rows)
    hop()
    flow.go()
    for count in range(2, depth):
        if count > 2:
            flow.go()
        spread_in.wave(flow, count)
    token_core = flow.send(token_x, CORE, 0)
    token_both = flow.send(token_low.value, CORE, 0)
    turned = send_turn(1)
    hop()
    flow.go()
    token_group = jnp.concatenate(
        [token_x, token_core.value, token_low.value, token_both.value], axis=0
    ).astype(F32)
    end_turn(1, turned)
    hop()
    spread_in.settle()
    weight_in = jnp.concatenate(in_fold_order(spread_in.have, wide_masks), axis=0)
    gains = gains + swap(gains, CORE, 0)
    gains = gains.reshape(2, width).astype(F32)
    gain_in, gain_mid = to_wide(gains[:1]), gains[1:]
    turned = send_turn(2)
    near(ff_rows)
    chain_out.advance(flow)
    cot_far = to_far(cotangent)
    cot_x = flow.send(cot_far, CROSS, 0)
    flow.go()
    end_turn(2, turned)

    inv_group = lax.rsqrt(jnp.mean(token_group * token_group, axis=-1, keepdims=True) + EPS)
    input_low = (token_group * inv_group * gain_in).astype(BF16)
    lin = flow.join(jnp.dot(input_low, weight_in, preferred_element_type=F32))
    keys_values = jnp.concatenate(
        [
            rotate(lin[:, query_local : query_local + key_local], cosine, sine).astype(BF16),
            lin[:, query_local + key_local :].astype(BF16),
        ],
        axis=-1,
    )
    queries = rotate(lin[:, :query_local], cosine, sine).astype(BF16)
    queries = queries * jnp.asarray(HEAD_WIDTH ** (-0.5), BF16)

    spread_kv = Spread(keys_values, wide_masks)
    spread_kv.wave(flow, 0)
    near(ff_rows)
    near(ff_rows)
    flow.go()
    spread_kv.wave(flow, 1)
    near(block_rows)
    high(ff_rows)
    flow.go()
    for count in range(2, depth):
        if count > 2:
            flow.go()
        spread_kv.wave(flow, count)
    chain_out.advance(flow)
    high(ff_rows)
    near(ff_rows)
    near(ff_rows)
    flow.go()
    spread_kv.settle()
    kv_all = jnp.concatenate(in_fold_order(spread_kv.have, wide_masks), axis=0)
    while chain_out.masks:
        chain_out.advance(flow)
        if not chain_out.masks:
            high(ff_rows)
            near(ff_rows)
            near(ff_rows)
            cot_t = flow.send(cot_far, 0, TURN)
        flow.go()
    attention_low, attention_f, lse = attend(
        place, pair_order, seg_flat, queries, kv_all, seg_row, seg_col, per_seq
    )
    attention_low = flow.join(attention_low)
    chain_out.settle()
    weight_out = chain_out.blocks.reshape(width, -1)
    branch = lax.dot_general(attention_low, weight_out, COLS, preferred_element_type=F32)
    branch = row_major(branch.astype(BF16)).reshape(2, 2, token_rows, width)
    branch_across = add(branch[1, 0], swap(branch[1, 1], CORE, 0), BF16)
    branch_own = add(branch[0, 0], swap(branch[0, 1], CORE, 0), F32)
    branch_sent = flow.send(branch_across, 0, 1)
    cot_xt = flow.send(cot_t.value, CROSS, 0)
    high(ff_rows // 2)
    flow.go()
    branch = branch_own + branch_sent.value.astype(F32)

    tokens_f = tokens.astype(F32)
    middle = tokens_f + from_wide(branch)
    inv_mid = lax.rsqrt(jnp.mean(middle * middle, axis=-1, keepdims=True) + EPS)
    normed_mid = middle * inv_mid
    mid_low = to_far((normed_mid * gain_mid).astype(BF16))

    half = width // 2
    left, right = mid_low[:, :half], mid_low[:, half:]
    left_x = flow.send(left, CROSS, 0)
    right_t = flow.send(right, 0, TURN)
    near(ff_rows)
    high(ff_rows // 2)
    flow.go()
    left_t = flow.send(left, 0, TURN)
    right_x = flow.send(right, CROSS, 0)
    left_xt = flow.send(left_x.value, 0, TURN)
    right_xt = flow.send(right_t.value, CROSS, 0)
    high(ff_rows // 2)
    flow.go()
    def four_rows(parts, first_col):
        return [(part, (i * token_rows, first_col)) for i, part in enumerate(parts)]

    placed = four_rows([left, left_t.value, left_x.value, left_xt.value], 0)
    placed += four_rows([right, right_t.value, right_x.value, right_xt.value], half)
    mid_four = assemble([part for part, _ in placed], [where for _, where in placed])
    def eight(four):
        return stack_rows([four, swap(four, CORE, 0)])

    def weight_of(which):
        have = bulk.parts(which)
        return jnp.concatenate(
            [part for parts in in_fold_order(have, far_masks) for part in parts], axis=0
        )

    cot_four = jnp.concatenate([cot_far, cot_t.value, cot_x.value, cot_xt.value], axis=0)
    grad_group = jnp.concatenate([cot_four, swap(cot_four, CORE, 0)], axis=0)
    while bulk.left(None, 0):
        near(block_rows), high(block_rows)
        flow.go()
    down = weight_of(0)
    near(block_rows), near(block_rows), high(block_rows)
    flow.go()
    bulk.settle()
    mid_group = eight(mid_four)
    grad_hidden = jnp.dot(grad_group, down, preferred_element_type=F32)
    while bulk.left(None, 1):
        near(block_rows), near(block_rows), high(block_rows)
        flow.go()
    gate = weight_of(1)
    while bulk.left(None, 2):
        for _ in range(4):
            near(block_rows)
        high(block_rows)
        flow.go()
    grad_hidden = flow.join(grad_hidden)
    gate_lin = flow.join(jnp.dot(mid_group, gate, preferred_element_type=F32))
    up = weight_of(2)
    up_proj = jnp.dot(mid_group, up, preferred_element_type=F32)
    gate_sig = jax.nn.sigmoid(gate_lin)
    gate_silu = gate_lin * gate_sig
    hidden_act = (gate_silu * up_proj).astype(BF16)
    grad_gate_lin = (
        grad_hidden * up_proj * gate_sig * (1.0 + gate_lin * (1.0 - gate_sig))
    ).astype(BF16)
    grad_up_proj = (grad_hidden * gate_silu).astype(BF16)

    def ffn_fold(lhs, rhs):
        total = lax.dot_general(lhs, rhs, ROWS, preferred_element_type=F32)
        total = row_major(total.astype(BF16))
        return FfnFold(total, far_masks[::-1], turn)

    ffn_folds = []

    def near(rows):
        found = [(fold.next(1), i) for i, fold in enumerate(ffn_folds)]
        found = [(-block[0], i) for block, i in found if block is not None]
        return bool(found) and ffn_folds[min(found)[1]].take(flow, 1, rows)

    def high(rows):
        found = False
        for mask in far_masks[:-1][::-1]:
            found = any(fold.take(flow, mask, rows) for fold in ffn_folds) or found
        return found

    mid_partial = lax.dot_general(
        grad_gate_lin, gate, COLS, preferred_element_type=F32
    ) + lax.dot_general(grad_up_proj, up, COLS, preferred_element_type=F32)
    mid_partial = row_major(mid_partial.astype(BF16))
    down_fold = ffn_fold(grad_group, after(hidden_act, mid_partial))
    ffn_folds.append(down_fold)
    mid_partial = mid_partial.reshape(2, 2, 2, token_rows, width)
    four = add(mid_partial[0], swap(mid_partial[1], CORE, 0), BF16)
    left, right = four[..., :half], four[..., half:]
    left_sent = flow.send(left[:, 1], 0, TURN)
    right_sent = flow.send(right[1], CROSS, 0)
    near(ff_rows)
    flow.go()
    gate_fold = ffn_fold(mid_group, after(grad_gate_lin, four))
    first_step = left_sent.value
    ffn_partial = lax.dot_general(
        after(hidden_act, four), down, COLS, preferred_element_type=F32
    )
    ffn_partial = row_major(ffn_partial.astype(BF16)).reshape(2, 2, 2, token_rows, width)
    out_four = add(ffn_partial[0], swap(ffn_partial[1], CORE, 0), BF16)
    left = add(left[:, 0], left_sent.value, BF16)
    right = add(right[0], right_sent.value, BF16)
    left_sent = flow.send(left[1], CROSS, 0)
    right_sent = flow.send(right[1], 0, TURN)
    near(ff_rows)
    high(ff_rows // 2)
    flow.go()
    ffn_folds.append(gate_fold)
    grad_mid = jnp.concatenate(
        [add(left[0], left_sent.value, F32), add(right[0], right_sent.value, F32)], axis=-1
    )
    grad_mid = from_far(grad_mid)
    norm_mid_sum = jnp.sum(grad_mid * normed_mid, axis=0)
    grad_y = cotangent.astype(F32)
    grad_middle = grad_y + rms_back(grad_mid * gain_mid, normed_mid, inv_mid)
    grad_branch = to_wide(grad_middle.astype(BF16))
    branch_low = flow.send(grad_branch, 0, 1)
    high(ff_rows // 2)
    out_parts = [flow.send(out_four[1, 0], CROSS, 0)]
    flow.go()
    up_fold = ffn_fold(mid_group, after(grad_up_proj, first_step))
    ffn_folds.append(up_fold)
    branch_group = jnp.concatenate(
        [grad_branch, swap(grad_branch, CORE, 0), branch_low.value, swap(branch_low.value, CORE, 0)],
        axis=0,
    )
    grad_attention = jnp.dot(branch_group, weight_out, preferred_element_type=F32).astype(BF16)

    def weight_fold(lhs, rhs, extra=None):
        total = lax.dot_general(lhs, rhs, ROWS, preferred_element_type=F32)
        if extra is not None:
            column = jnp.broadcast_to(to_wide(extra[None])[0][:, None], (width, 128))
            total = jnp.concatenate([total, column], axis=1)
        total = row_major(total.astype(BF16))
        return Fold(total.reshape(groups, 4 * shard, -1), wide_masks[::-1])

    out_blocks = weight_fold(branch_group, attention_low, norm_mid_sum).blocks
    out_fold = Fold(out_blocks[..., : query_local - 128], wide_masks[::-1])
    out_rest = Fold(out_blocks[..., query_local - 128 :], wide_masks[::-1])
    out_fold.advance(flow)
    near(block_rows)
    high(ff_rows)
    flow.go()
    grad_queries, grad_keys, grad_values = attend_back(
        place, pair_order, seg_flat, queries, kv_all, seg_row, seg_col,
        lse, attention_f, grad_attention, per_seq,
    )
    grad_queries = flow.join(grad_queries)
    grad_keys = flow.join(grad_keys)
    key_fold = Fold(grad_keys.reshape(groups, group_rows, -1), wide_masks[::-1])
    value_fold = Fold(grad_values.reshape(groups, group_rows, -1), wide_masks[::-1])
    key_fold.advance(flow)
    near(block_rows)
    high(ff_rows)
    flow.go()
    key_fold.advance(flow)
    value_fold.advance(flow)
    near(block_rows)
    high(ff_rows)
    flow.go()
    query_lin = rotate(grad_queries.astype(F32), cosine, -sine).astype(BF16)
    query_fold = weight_fold(input_low, query_lin)
    turns = [down_fold, gate_fold, up_fold]

    def take_turn():
        for fold in turns:
            if fold.take_turn(flow):
                turns.remove(fold)
                return

    while True:
        running = [fold.advance(flow) for fold in (key_fold, value_fold)]
        if not any(running):
            break
        query_fold.advance(flow)
        if all(running):
            high(ff_rows // 2)
            near(block_rows)
        else:
            near(ff_rows)
            high(ff_rows // 2)
            if len(out_parts) == 1:
                out_parts.append(flow.send(out_four[1, 1], CROSS, 0))
        flow.go()
    out_two = [add(out_four[0, i], sent.value, BF16) for i, sent in enumerate(out_parts)]
    out_sent = flow.send(out_two[1], 0, TURN)
    out_rest.advance(flow)
    high(ff_rows // 2)
    flow.go()
    layer_out = (middle + from_far(add(out_two[0], out_sent.value, F32))).astype(BF16)
    keys_low, values_low = key_fold.blocks[0].astype(BF16), value_fold.blocks[0].astype(BF16)
    kv_lin = jnp.concatenate(
        [rotate(keys_low.astype(F32), cosine, -sine).astype(BF16), values_low], axis=-1
    )
    grad_lin = jnp.concatenate([query_lin, kv_lin], axis=-1)
    grad_in = lax.dot_general(grad_lin, weight_in, COLS, preferred_element_type=F32)
    grad_in = row_major(grad_in.astype(BF16)).reshape(2, 2, token_rows, width)
    in_across = add(grad_in[1, 0], swap(grad_in[1, 1], CORE, 0), BF16)
    in_own = add(grad_in[0, 0], swap(grad_in[0, 1], CORE, 0), F32)
    in_sent = flow.send(in_across, 0, 1)
    kv_fold = weight_fold(input_low, kv_lin)
    kv_fold.advance(flow)
    query_fold.advance(flow)
    out_fold.advance(flow)
    out_rest.advance(flow)
    flow.go()
    kv_fold.advance(flow)
    query_fold.advance(flow)
    out_fold.advance(flow)
    out_rest.advance(flow)
    near(ff_rows)
    flow.go()
    kv_fold.advance(flow)
    high(ff_rows)
    near(block_rows)
    take_turn()
    flow.go()
    while True:
        running = [fold.advance(flow) for fold in (kv_fold, query_fold, out_fold, out_rest)]
        if not any(running):
            break
        near(block_rows), high(block_rows)
        flow.go()

    total = jnp.concatenate(
        [fold.blocks[0] for fold in (query_fold, kv_fold, out_fold, out_rest)], axis=-1
    ).reshape(2, 2, shard, -1)

    def block_of(core_bit, low_bit):
        return index(index(total, core_bit), low_bit)

    sent_core = flow.send(block_of(1 - core, low).astype(BF16), CORE, 0)
    sent_low = flow.send(block_of(core, 1 - low).astype(BF16), 0, 1)
    sent_both = flow.send(block_of(1 - core, 1 - low).astype(BF16), CORE, 1)
    for fold in list(turns):
        if fold.take_turn(flow):
            turns.remove(fold)
    flow.go()
    while True:
        near(block_rows), high(block_rows)
        for fold in list(turns):
            if fold.take_turn(flow):
                turns.remove(fold)
        if not flow.batch:
            break
        flow.go()
    total = pair(
        pair(block_of(core, low), sent_core.value.astype(F32), core, 0),
        pair(sent_low.value.astype(F32), sent_both.value.astype(F32), core, 0),
        low, 0,
    ).reshape(4, shard, -1)
    scaled = in_own + in_sent.value.astype(F32)
    inv_in = inv_group[:token_rows]
    normed_in = tokens_f * inv_in
    grad_tokens = grad_middle + rms_back(from_wide(scaled * gain_in), normed_in, inv_in)

    def columns(first, count):
        return total[..., first : first + count].transpose(1, 0, 2).reshape(shard, -1)

    in_grads = [
        columns(0, query_local),
        columns(query_local, key_local),
        columns(query_local + key_local, key_local),
    ]
    grad_norm_in = sum(
        jnp.sum(grad * weight.astype(F32), axis=1)
        for grad, weight in zip(in_grads, attention_weights)
    ) / norm_in.astype(F32)
    grad_norm_mid = jnp.sum(total[..., in_cols + query_local], axis=0)
    return (
        layer_out,
        grad_tokens,
        grad_norm_in,
        *in_grads,
        columns(in_cols, query_local),
        grad_norm_mid,
        gate_fold.result(),
        up_fold.result(),
        down_fold.result(),
    )


def solution(mesh):
    rows = P(("blk", "head"), None)
    shards = P(("head", "blk"), None)
    vector = P(("head", "blk"))
    hidden = P("blk", "head")
    return jax.shard_map(
        local,
        mesh=mesh,
        in_specs=(
            rows, rows, P(), P(), vector, shards, shards, shards, shards, vector, hidden, hidden, hidden,
        ),
        out_specs=(
            rows, rows, vector, shards, shards, shards, shards, vector, hidden, hidden, hidden,
        ),
        check_vma=False,
    )
```
